32 devices in a mesh: section: 2 (over x), seq: 16 (over z, y, core).
Axes of the slice: x: 2, y: 2, z: 4, core: 2. Of those that a mesh axis runs over, the one named last changes fastest.
Arguments:
- latents: bfloat16 [4, 1024, 1024], P(None, 'seq'), may hold values from -6 to 6
- norm_gain: float32 [2, 1024], P('section'), may hold values from 0.1 to 1.9
- qkv_weight: bfloat16 [2, 1024, 3072], P('section', 'seq'), may hold values from -1 to 1
- proj_weight: bfloat16 [2, 1024, 1024], P('section', 'seq'), may hold values from -0.1875 to 0.1875
- merge_weight: bfloat16 [2, 1024, 1024], P('section', 'seq'), may hold values from -0.125 to 0.125
Outputs:
- denoised: bfloat16 [4, 1024, 1024], P(None, 'seq', 'section')
The draws below stay inside these ranges and needn't reach their ends.
All inputs are finite; a program needn't handle non-finite values.
Results may differ from the reference program's by a relative error of at most 0.017.
Values may be sent and summed in bfloat16 or wider, within the bound.
No kernel may reach another device: no remote copies, remote signals or barrier semaphores. Data moves between devices by JAX's collectives and lax.ppermute only.
A program may use at most 64 MiB of HBM per device.

```python
import jax
import jax.numpy as jnp
from jax import lax

D = 1024
HEADS = 16
HEAD_DIM = 64
WINDOWS = 4
WINDOW = 1024
N_SECTION = 2


def draw_qkv_weight(key, part):
    drawn = jax.random.normal(key, (N_SECTION, D, 3 * D), jnp.float32) * D ** (-0.5)
    return jnp.clip(drawn, -1.0, 1.0).astype(jnp.bfloat16)


def block_levels(key, dims, shards, least, high):
    loudness = 1.0
    for position, shards_of in shards:
        heights = jax.random.uniform(jax.random.fold_in(jax.random.fold_in(key, 6), position), (shards_of,), jnp.float32, least / len(shards), high / len(shards))
        loudness = loudness * jnp.repeat(jnp.exp(heights), dims[position] // shards_of).reshape((-1,) + (1,) * (len(dims) - 1 - position))
    return loudness


def scatter_about(own_key, shape, scale, bound, cuts=(), held_as=jnp.bfloat16):
    values = scale * jax.random.normal(own_key, shape, jnp.float32)
    if cuts:
        values = values * block_levels(own_key, shape, cuts, -0.22, 0.18)
    return jnp.clip(values, -bound, bound).astype(held_as)


def setup_inputs(seed: int = 0) -> dict:
    key_list = jax.random.split(jax.random.key(seed), 6)
    latents = scatter_about(key_list[0], (WINDOWS, WINDOW, D), 1.0, 6.0, ((1, 16),))
    norm_gain = jnp.clip(1.0 + 0.18 * jax.random.normal(key_list[1], (N_SECTION, D), jnp.float32), 0.1, 1.9)
    qkv_weight = draw_qkv_weight(jax.random.fold_in(key_list[5], 71), 0)
    proj_weight = scatter_about(key_list[3], (N_SECTION, D, D), D ** -0.5, 0.1875, ((0, 2), (1, 16)))
    merge_weight = scatter_about(key_list[4], (N_SECTION, D, D), (2 * D) ** -0.5, 0.125, ((0, 2), (1, 16)))
    return dict(latents=latents, norm_gain=norm_gain, qkv_weight=qkv_weight, proj_weight=proj_weight, merge_weight=merge_weight)


EPSILON = 1e-05

def layer_norm(hidden, gain_row):
    values = hidden.astype(jnp.float32)
    center = values - lax.optimization_barrier(jnp.mean(values, axis=-1, keepdims=True))
    spread = lax.optimization_barrier(jnp.mean(center * center, axis=-1, keepdims=True))
    return (center * lax.rsqrt(spread + EPSILON) * gain_row).astype(jnp.bfloat16)

def attend_head(operands):
    query_head, key_head, value_head = operands
    scores = jnp.dot(query_head, key_head.T, preferred_element_type=jnp.float32) * HEAD_DIM ** (-0.5)
    row_max = lax.optimization_barrier(jnp.max(scores, axis=-1, keepdims=True))
    weights = jnp.exp(scores - row_max)
    totals = lax.optimization_barrier(jnp.sum(weights, axis=-1, keepdims=True))
    probs = weights.astype(jnp.bfloat16)
    mixed = jnp.dot(probs, value_head, preferred_element_type=jnp.float32)
    return (mixed / totals).astype(jnp.bfloat16)

def block(hidden, gain_row, w_qkv, w_proj):
    normed = layer_norm(hidden, gain_row)
    packed = jnp.dot(normed, w_qkv, preferred_element_type=jnp.float32).astype(jnp.bfloat16)
    rows = hidden.shape[0]

    def split_heads(columns):
        return columns.reshape(rows, HEADS, HEAD_DIM).transpose(1, 0, 2)
    queries = split_heads(packed[:, :D])
    keys_all = split_heads(packed[:, D:2 * D])
    values_all = split_heads(packed[:, 2 * D:])
    mixed = lax.map(attend_head, (queries, keys_all, values_all))
    mixed = mixed.transpose(1, 0, 2).reshape(rows, D)
    update = jnp.dot(mixed, w_proj, preferred_element_type=jnp.float32)
    return (hidden.astype(jnp.float32) + update).astype(jnp.bfloat16)

def one_window(hidden, norm_gain, qkv_weight, proj_weight, merge_weight):
    skip_terms = []
    midpoint = N_SECTION // 2
    for section_no in range(N_SECTION):
        if section_no >= midpoint:
            joined = jnp.dot(hidden, merge_weight[section_no], preferred_element_type=jnp.float32)
            hidden = (joined + skip_terms[N_SECTION - 1 - section_no].astype(jnp.float32)).astype(jnp.bfloat16)
        hidden = block(hidden, norm_gain[section_no], qkv_weight[section_no], proj_weight[section_no])
        if section_no < midpoint:
            skip_terms.append(jnp.dot(hidden, merge_weight[section_no], preferred_element_type=jnp.float32).astype(jnp.bfloat16))
    return hidden

def reference(latents, norm_gain, qkv_weight, proj_weight, merge_weight):
    outputs = [one_window(latents[window_no], norm_gain, qkv_weight, proj_weight, merge_weight) for window_no in range(WINDOWS)]
    return jnp.stack(outputs, axis=0)
```

```python
import jax
import jax.numpy as jnp
from jax import lax
from jax.experimental import pallas as pl
from jax.experimental.pallas import tpu as pltpu
from jax.sharding import PartitionSpec as P

HEADS = 16
HEAD_DIM = 64


EPSILON = 1e-05


def partner(value, axis, bit):
    mask = 2**bit
    pairs = [(source, source ^ mask) for source in range(lax.axis_size(axis))]
    return lax.ppermute(value, axis, pairs)


def shifted(value, axis, steps):
    count = lax.axis_size(axis)
    initial, last = (max(0, -steps), min(count, count - steps))
    return lax.ppermute(value, axis, [(source, source + steps) for source in range(initial, last)])


def layer_norm(hidden, gain_row):
    values = hidden.astype(jnp.float32)
    center = values - jnp.mean(values, axis=-1, keepdims=True)
    spread = jnp.mean(center * center, axis=-1, keepdims=True)
    return (center * lax.rsqrt(spread + EPSILON) * gain_row).astype(jnp.bfloat16)


def body(latents, norm_gain, qkv_weight, proj_weight, merge_weight):
    seq_count = lax.axis_size("seq")
    section_count = lax.axis_size("section")
    my_section = lax.axis_index("section")
    midpoint = section_count // 2
    windows = latents.shape[0]
    tok_rows = latents.shape[1]
    features = latents.shape[2]
    repeat = max(seq_count // HEADS, 1)
    groups = seq_count // repeat
    head_cols = features * repeat // seq_count
    per_device = head_cols // HEAD_DIM
    part_rows = tok_rows // repeat
    scale_factor = HEAD_DIM ** (-0.5)
    w_qkv, w_proj, w_merge = (
        lax.all_gather(qkv_weight, "seq", axis=1, tiled=True),
        lax.all_gather(proj_weight, "seq", axis=1, tiled=True),
        lax.all_gather(merge_weight, "seq", axis=1, tiled=True),
    )
    w_qkv = w_qkv[0]
    w_proj = w_proj[0]
    w_merge = w_merge[0]
    gain_row = norm_gain[0]
    decoder = my_section >= midpoint
    encoder = my_section < midpoint
    query_shape = (seq_count, part_rows * head_cols)
    key_shape = (seq_count, tok_rows * head_cols)

    def to_heads(array_in, spread_copies):
        if spread_copies:
            grouped = array_in.reshape(tok_rows, groups, head_cols).transpose(1, 0, 2)
            grouped = grouped.reshape(groups, 1, tok_rows * head_cols)
            grouped = jnp.broadcast_to(grouped, (groups, repeat, tok_rows * head_cols))
            return grouped.reshape(seq_count, tok_rows * head_cols)
        grouped = array_in.reshape(part_rows, repeat, groups, head_cols).transpose(2, 1, 0, 3)
        return grouped.reshape(seq_count, part_rows * head_cols)

    def from_heads(array_in):
        grouped = array_in.reshape(groups, repeat, part_rows, head_cols).transpose(2, 1, 0, 3)
        return grouped.reshape(tok_rows, features)

    def project(carried):
        normed = layer_norm(carried, gain_row)
        packed = jnp.dot(normed, w_qkv, preferred_element_type=jnp.float32).astype(jnp.bfloat16)
        return (
            to_heads(packed[:, :features], False),
            to_heads(packed[:, features : 2 * features], True),
            to_heads(packed[:, 2 * features :], True),
        )

    def spare_heads():
        return (
            jnp.zeros(query_shape, jnp.bfloat16),
            jnp.zeros(key_shape, jnp.bfloat16),
            jnp.zeros(key_shape, jnp.bfloat16),
        )

    def attend(queries, keys_in, values_in):
        query_rows = queries.reshape(-1, per_device, HEAD_DIM)
        key_rows = keys_in.reshape(-1, per_device, HEAD_DIM)
        value_rows = values_in.reshape(-1, per_device, HEAD_DIM)
        block_rows = min(512, query_rows.shape[0])
        blocked = query_rows.reshape(-1, block_rows, per_device, HEAD_DIM)

        def one_block(query_block):
            scores = (
                jnp.einsum(
                    "qhd,khd->hqk", query_block, key_rows, preferred_element_type=jnp.float32
                )
                * scale_factor
            )
            row_max = jnp.max(scores, axis=-1, keepdims=True)
            weights = jnp.exp(scores - row_max)
            totals = jnp.sum(weights, axis=-1)
            probs = weights.astype(jnp.bfloat16)
            mixed = jnp.einsum(
                "hqk,khd->qhd", probs, value_rows, preferred_element_type=jnp.float32
            )
            return (mixed / totals.T[:, :, None]).astype(jnp.bfloat16)

        return lax.map(one_block, blocked).reshape(query_shape)

    def mirror_each(skip_term):
        for bit_no in range(section_count.bit_length() - 1):
            skip_term = partner(skip_term, "section", bit_no)
        return skip_term

    def tick(tick_no, loop_state):
        incoming, skip_store, result = loop_state
        window_no = tick_no - my_section
        active = (window_no >= 0) & (window_no < windows)
        chosen = jnp.clip(window_no, 0, windows - 1)
        fresh = lax.dynamic_index_in_dim(latents, chosen, 0, keepdims=False)
        entering = jnp.where(my_section == 0, fresh, incoming)
        skip_slot = lax.dynamic_index_in_dim(skip_store, chosen, 0, keepdims=False)
        carried = lax.cond(
            active & decoder,
            lambda: (
                jnp.dot(entering, w_merge, preferred_element_type=jnp.float32)
                + skip_slot.astype(jnp.float32)
            ).astype(jnp.bfloat16),
            lambda: entering,
        )
        queries, keys_in, values_in = lax.cond(active, lambda: project(carried), spare_heads)
        queries, keys_in, values_in = (
            lax.all_to_all(queries, "seq", split_axis=0, concat_axis=0, tiled=True),
            lax.all_to_all(keys_in, "seq", split_axis=0, concat_axis=0, tiled=True),
            lax.all_to_all(values_in, "seq", split_axis=0, concat_axis=0, tiled=True),
        )
        attended = lax.cond(
            active,
            lambda: attend(queries, keys_in, values_in),
            lambda: jnp.zeros(query_shape, jnp.bfloat16),
        )
        attended = lax.all_to_all(attended, "seq", split_axis=0, concat_axis=0, tiled=True)
        leaving = lax.cond(
            active,
            lambda: (
                carried.astype(jnp.float32)
                + jnp.dot(from_heads(attended), w_proj, preferred_element_type=jnp.float32)
            ).astype(jnp.bfloat16),
            lambda: carried,
        )
        skip_term = lax.cond(
            active & encoder,
            lambda: jnp.dot(leaving, w_merge, preferred_element_type=jnp.float32).astype(
                jnp.bfloat16
            ),
            lambda: jnp.zeros_like(leaving),
        )
        arrived = mirror_each(skip_term)
        source_no = tick_no - (section_count - 1 - my_section)
        landing = decoder & (source_no >= 0) & (source_no < windows)
        target = jnp.clip(source_no, 0, windows - 1)
        updated = lax.dynamic_update_index_in_dim(skip_store, arrived, target, 0)
        skip_store = jnp.where(landing, updated, skip_store)
        incoming = shifted(leaving, "section", 1)
        finished = lax.dynamic_update_index_in_dim(result, leaving.astype(jnp.float32), chosen, 0)
        result = jnp.where(active & (my_section == section_count - 1), finished, result)
        return (incoming, skip_store, result)

    loop_state = (
        jnp.zeros(latents.shape[1:], jnp.bfloat16),
        jnp.zeros_like(latents),
        jnp.zeros(latents.shape, jnp.float32),
    )
    loop_state = lax.fori_loop(0, windows + section_count - 1, tick, loop_state)
    result = loop_state[2]
    return lax.psum_scatter(result.astype(jnp.bfloat16), "section", scatter_dimension=2, tiled=True)


class Plan:
    def __init__(self, sections, seq_count, windows, tok_rows, features):
        self.sections = sections
        self.seq_count = seq_count
        self.windows = windows
        self.tok_rows = tok_rows
        self.features = features
        self.inner = seq_count // windows
        self.slots = sections * self.inner
        self.half = tok_rows // sections
        self.shard = windows * self.half
        self.tokens = self.slots * self.shard
        self.cols = features // self.slots
        self.half_cols = features // sections
        self.w_rows = features // seq_count
        self.group = self.inner * self.w_rows
        self.chips = [(mx, mi) for mx in range(sections) for mi in range(0, self.inner, 2)]

    @staticmethod
    def fits(sections, seq_count, windows, tok_rows, features):
        if sections != 2 or windows & (windows - 1) or seq_count % (2 * windows):
            return False
        inner = seq_count // windows
        if inner & (inner - 1) or features % (sections * inner * 2 * HEAD_DIM):
            return False
        return features == HEADS * HEAD_DIM and tok_rows % 32 == 0

    def mask(self, mx=0, mz=0, mi=0):
        return mx * self.seq_count + mz * self.inner + mi


def attention(qkv, out, cols, rows_q):
    tokens = qkv.shape[0]
    lane_head = lax.broadcasted_iota(jnp.int32, (1, cols), 1) // HEAD_DIM

    def one_block(block_no, carry):
        rows = pl.ds(pl.multiple_of(block_no * rows_q, rows_q), rows_q)
        query = qkv[rows, 0:cols]
        keys_in = qkv[:, cols : 2 * cols]
        values_in = qkv[:, 2 * cols : 3 * cols]
        mixed = jnp.zeros((rows_q, cols), jnp.float32)
        for head in range(cols // HEAD_DIM):
            mine = lane_head == head
            picked = jnp.where(mine, query, jnp.zeros_like(query))
            scores = lax.dot_general(
                picked, keys_in, (((1,), (1,)), ((), ())), preferred_element_type=jnp.float32
            )
            row_max = jnp.max(scores, axis=-1, keepdims=True)
            weights = jnp.exp(scores - row_max)
            totals = jnp.sum(weights, axis=-1, keepdims=True)
            part = jnp.dot(
                weights.astype(jnp.bfloat16), values_in, preferred_element_type=jnp.float32
            )
            mixed = jnp.where(mine, part / totals, mixed)
        out[rows, :] = mixed.astype(jnp.bfloat16)
        return carry

    lax.fori_loop(0, tokens // rows_q, one_block, 0)


def project_rows(normed, w_qkv, cols):
    packed = jnp.dot(normed, w_qkv, preferred_element_type=jnp.float32)
    lane = lax.broadcasted_iota(jnp.int32, (1, packed.shape[1]), 1)
    packed = packed.astype(jnp.bfloat16)
    return jnp.where(lane < cols, packed * jnp.bfloat16(HEAD_DIM ** (-0.5)), packed)


def slot_of(plan, where, mx, mi):
    return (where[0] ^ mx) * plan.inner + (where[2] ^ mi)


def plane_copies(plan, where, own, swap, target, sems, base):
    copies = []
    rows = plan.shard
    for chip_no, (mx, mi) in enumerate(plan.chips):
        for core, source in ((0, own), (1, swap)):
            slot = slot_of(plan, where, mx, mi ^ core)
            start = pl.multiple_of(slot * rows, rows)
            copies.append(
                pltpu.make_async_copy(
                    source.at[pl.ds(chip_no * rows, rows)],
                    target.at[pl.ds(start, rows)],
                    sems.at[base + len(copies)],
                )
            )
    return copies


def lane_copies(plan, where, own, swap, target, sems, base):
    copies = []
    for chip_no, (mx, mi) in enumerate(plan.chips):
        for core, source in ((0, own), (1, swap)):
            slot = slot_of(plan, where, mx, mi ^ core)
            start = pl.multiple_of(slot * plan.cols, plan.cols)
            copies.append(
                pltpu.make_async_copy(
                    source.at[chip_no],
                    target.at[:, pl.ds(start, plan.cols)],
                    sems.at[base + len(copies)],
                )
            )
    return copies


def qkv_copies(plan, where, pieces, target, sems, base):
    copies = []
    rows = plan.w_rows
    for mz, piece in enumerate(pieces):
        for mi in range(plan.inner):
            shard = (where[1] ^ mz) * plan.inner + (where[2] ^ mi)
            start = pl.multiple_of(shard * rows, rows)
            copies.append(
                pltpu.make_async_copy(
                    piece.at[pl.ds(mi * rows, rows)],
                    target.at[pl.ds(start, rows)],
                    sems.at[base + len(copies)],
                )
            )
    return copies


def first_kernel(plan, where, hid_own, hid_swap, gain, *rest):
    pieces = rest[: plan.windows]
    out, hid, w_qkv, qkv, sems = rest[plan.windows :]
    hid_copies = plane_copies(plan, where, hid_own, hid_swap, hid, sems, 0)
    w_copies = qkv_copies(plan, where, pieces, w_qkv, sems, len(hid_copies))
    for copy in hid_copies + w_copies:
        copy.start()
    for copy in hid_copies + w_copies:
        copy.wait()
    rows = min(256, plan.tokens)

    def one_block(block_no, carry):
        part = pl.ds(pl.multiple_of(block_no * rows, rows), rows)
        normed = layer_norm(hid[part, :], gain[...])
        qkv[part, :] = project_rows(normed, w_qkv[...], plan.cols)
        return carry

    lax.fori_loop(0, plan.tokens // rows, one_block, 0)
    attention(qkv, out, plan.cols, rows)


def second_kernel(plan, where, hid_own, hid_swap, att_own, att_swap, mat_own, mat_swap, gain, *rest):
    pieces = rest[: plan.windows]
    out, kept, hid, att, mats, w_qkv, joined, qkv, mixed, sems = rest[plan.windows :]
    copies = plane_copies(plan, where, hid_own, hid_swap, hid, sems, 0)
    copies += lane_copies(plan, where, att_own, att_swap, att, sems, len(copies))
    copies += qkv_copies(plan, where, pieces, w_qkv, sems, len(copies))
    rows = plan.w_rows
    for chip_no, (mx, mi) in enumerate(plan.chips):
        for core, source in ((0, mat_own), (1, mat_swap)):
            for mz in range(plan.windows):
                shard = (where[1] ^ mz) * plan.inner + (where[2] ^ mi ^ core)
                start = pl.multiple_of(shard * rows, rows)
                copies.append(
                    pltpu.make_async_copy(
                        source.at[pl.ds((chip_no * plan.windows + mz) * rows, rows)],
                        mats.at[where[0] ^ mx, pl.ds(start, rows)],
                        sems.at[len(copies)],
                    )
                )
    for copy in copies:
        copy.start()
    for copy in copies:
        copy.wait()
    block = min(256, plan.tokens)
    width = plan.half_cols

    def one_block(block_no, carry):
        part = pl.ds(pl.multiple_of(block_no * block, block), block)
        attended = att[part, :]
        hidden = jnp.concatenate(
            [
                jnp.dot(attended, mats[side, :, 0:width], preferred_element_type=jnp.float32)
                for side in range(plan.sections)
            ],
            axis=1,
        )
        hidden = (hid[part, :].astype(jnp.float32) + hidden).astype(jnp.bfloat16)
        merged = jnp.concatenate(
            [
                jnp.dot(hidden, mats[side, :, width:], preferred_element_type=jnp.float32)
                for side in range(plan.sections)
            ],
            axis=1,
        ).astype(jnp.bfloat16)
        joined[part, :] = merged
        normed = layer_norm(merged, gain[...])
        qkv[part, :] = project_rows(normed, w_qkv[...], plan.cols)
        return carry

    lax.fori_loop(0, plan.tokens // block, one_block, 0)
    attention(qkv, mixed, plan.cols, block)
    lanes = pl.ds(pl.multiple_of(where[0] * width, width), width)
    for side in range(plan.sections):
        for mi in range(plan.inner):
            slot = side * plan.inner + (where[2] ^ mi)
            part = pl.ds(pl.multiple_of(slot * plan.shard, plan.shard), plan.shard)
            out[mi, pl.ds(side * plan.shard, plan.shard), :] = mixed[part, :]
            if mi == 0:
                kept[pl.ds(side * plan.shard, plan.shard), :] = joined[part, lanes]


def third_kernel(plan, where, att_own, att_swap, mat_own, mat_swap, kept, out, att, mat, sems):
    copies = lane_copies(plan, where, att_own, att_swap, att, sems, 0)
    rows = plan.w_rows
    for pair, mi in enumerate(range(0, plan.inner, 2)):
        for core, source in ((0, mat_own), (1, mat_swap)):
            for mz in range(plan.windows):
                shard = (where[1] ^ mz) * plan.inner + (where[2] ^ mi ^ core)
                start = pl.multiple_of(shard * rows, rows)
                copies.append(
                    pltpu.make_async_copy(
                        source.at[pl.ds((pair * plan.windows + mz) * rows, rows)],
                        mat.at[pl.ds(start, rows)],
                        sems.at[len(copies)],
                    )
                )
    for copy in copies:
        copy.start()
    for copy in copies:
        copy.wait()
    result = jnp.dot(att[...], mat[...], preferred_element_type=jnp.float32)
    result = (kept[...].astype(jnp.float32) + result).astype(jnp.bfloat16)
    for side in range(plan.sections):
        for mz in range(plan.windows):
            start = side * plan.shard + mz * plan.half
            out[mz, side * plan.half : (side + 1) * plan.half, :] = result[
                start : start + plan.half, :
            ]


def plane_body(latents, norm_gain, qkv_weight, proj_weight, merge_weight):
    plan = Plan(
        lax.axis_size("section"), lax.axis_size("seq"), latents.shape[0], *latents.shape[1:]
    )
    windows, inner, shard, cols = (plan.windows, plan.inner, plan.shard, plan.cols)
    section = lax.axis_index("section")
    position = lax.axis_index("seq")
    window, place = (position // inner, position % inner)
    where = jnp.stack([section, window, place]).astype(jnp.int32)
    devices = plan.sections * plan.seq_count

    def swap(value, mask):
        pairs = [(source, source ^ mask) for source in range(devices)]
        return lax.ppermute(value, ("section", "seq"), pairs)

    def across(value, masks):
        return [value] + [swap(value, mask) for mask in masks]

    z_masks = [plan.mask(mz=mz) for mz in range(1, windows)]
    chip_masks = [plan.mask(mx=mx, mi=mi) for mx, mi in plan.chips[1:]]
    core_mask = plan.mask(mi=1)
    smem = pl.BlockSpec(memory_space=pltpu.SMEM)
    anywhere = pl.BlockSpec(memory_space=pl.ANY)
    vmem = pl.BlockSpec(memory_space=pltpu.VMEM)

    def plane_gather(value):
        own = jnp.concatenate(across(value, chip_masks), axis=0)
        return own, swap(own, core_mask)

    def share(mz):
        return lax.dynamic_slice(
            latents,
            (window ^ mz, section * plan.half, 0),
            (1, plan.half, plan.features),
        )[0]

    shares = [share(0)] + [swap(share(mz), plan.mask(mz=mz)) for mz in range(1, windows)]
    hid_own, hid_swap = plane_gather(jnp.concatenate(shares, axis=0))

    width = plan.half_cols

    def columns(side):
        parts = [
            lax.dynamic_slice(
                qkv_weight[0], (0, part * plan.features + side * width), (plan.w_rows, width)
            )
            for part in range(3)
        ]
        parts.append(lax.dynamic_slice(proj_weight[0], (0, side * width), (plan.w_rows, width)))
        parts.append(lax.dynamic_slice(merge_weight[0], (0, side * width), (plan.w_rows, width)))
        return jnp.concatenate(parts, axis=1)

    kept_half = columns(section)
    other_half = swap(columns(1 - section), plan.mask(mx=1))
    first = section == 0
    half_a = jnp.where(first, kept_half, other_half)
    half_b = jnp.where(first, other_half, kept_half)
    merge_half = (
        half_a[:, 4 * width :].astype(jnp.float32) + half_b[:, 4 * width :].astype(jnp.float32)
    ).astype(jnp.bfloat16)

    def head_columns(mi):
        return jnp.concatenate(
            [
                lax.dynamic_slice(
                    half, (0, part * width + (place ^ mi) * cols), (plan.w_rows, cols)
                )
                for half in (half_a, half_b)
                for part in range(3)
            ],
            axis=1,
        )

    rows_in = [head_columns(0)] + [
        swap(head_columns(mi), plan.mask(mi=mi)) for mi in range(1, inner)
    ]
    rows_in = jnp.concatenate(rows_in, axis=0)
    pieces_a = across(rows_in[:, : 3 * cols], z_masks)
    mats = jnp.concatenate([half_a[:, 3 * width : 4 * width], merge_half], axis=1)
    mats = jnp.concatenate(across(mats, z_masks), axis=0)
    mat_own, mat_swap = plane_gather(mats)
    pieces_b = across(rows_in[:, 3 * cols :], z_masks)
    last = jnp.concatenate(across(half_b[:, 3 * width : 4 * width], z_masks), axis=0)
    last_own = jnp.concatenate(
        across(last, [plan.mask(mi=mi) for mi in range(2, inner, 2)]), axis=0
    )
    last_swap = swap(last_own, core_mask)

    gains = jnp.where(
        first,
        jnp.concatenate([norm_gain, swap(norm_gain, plan.mask(mx=1))], axis=0),
        jnp.concatenate([swap(norm_gain, plan.mask(mx=1)), norm_gain], axis=0),
    )
    tokens, features = (plan.tokens, plan.features)
    n_shard = plan.windows * plan.inner
    bf16 = jnp.bfloat16

    attended = pl.pallas_call(
        lambda *refs: first_kernel(plan, *refs),
        out_shape=jax.ShapeDtypeStruct((tokens, cols), bf16),
        in_specs=[smem, anywhere, anywhere, vmem] + [anywhere] * windows,
        out_specs=vmem,
        scratch_shapes=[
            pltpu.VMEM((tokens, features), bf16),
            pltpu.VMEM((features, 3 * cols), bf16),
            pltpu.VMEM((tokens, 3 * cols), bf16),
            pltpu.SemaphoreType.DMA((plan.slots + n_shard,)),
        ],
        name="first",
    )(where, hid_own, hid_swap, gains[0:1], *pieces_a)

    att_own = jnp.stack(across(attended, chip_masks), axis=0)
    att_swap = swap(att_own, core_mask)
    attended, kept = pl.pallas_call(
        lambda *refs: second_kernel(plan, *refs),
        out_shape=(
            jax.ShapeDtypeStruct((inner, plan.sections * shard, cols), bf16),
            jax.ShapeDtypeStruct((plan.sections * shard, width), bf16),
        ),
        in_specs=[smem] + [anywhere] * 6 + [vmem] + [anywhere] * windows,
        out_specs=(vmem, vmem),
        scratch_shapes=[
            pltpu.VMEM((tokens, features), bf16),
            pltpu.VMEM((tokens, features), bf16),
            pltpu.VMEM((plan.sections, features, 2 * width), bf16),
            pltpu.VMEM((features, 3 * cols), bf16),
            pltpu.VMEM((tokens, features), bf16),
            pltpu.VMEM((tokens, 3 * cols), bf16),
            pltpu.VMEM((tokens, cols), bf16),
            pltpu.SemaphoreType.DMA((2 * plan.slots + n_shard + plan.slots * windows,)),
        ],
        name="second",
    )(where, hid_own, hid_swap, att_own, att_swap, mat_own, mat_swap, gains[1:2], *pieces_b)

    back = jnp.stack(
        [attended[0:2]]
        + [
            swap(attended[mi : mi + 2], plan.mask(mx=mx, mi=mi)) for mx, mi in plan.chips[1:]
        ],
        axis=0,
    )
    back_own = back[:, 0]
    back_swap = swap(back[:, 1], core_mask)
    outcome = pl.pallas_call(
        lambda *refs: third_kernel(plan, *refs),
        out_shape=jax.ShapeDtypeStruct((windows, plan.tok_rows, width), bf16),
        in_specs=[smem] + [anywhere] * 4 + [vmem],
        out_specs=vmem,
        scratch_shapes=[
            pltpu.VMEM((plan.sections * shard, features), bf16),
            pltpu.VMEM((features, width), bf16),
            pltpu.SemaphoreType.DMA((plan.slots + n_shard,)),
        ],
        name="third",
    )(where, back_own, back_swap, last_own, last_swap, kept)

    result = jnp.zeros_like(outcome)
    for mz in range(windows):
        piece = outcome[mz] if mz == 0 else swap(outcome[mz], plan.mask(mz=mz))
        result = lax.dynamic_update_index_in_dim(result, piece, window ^ mz, 0)
    return result


def solution(mesh):
    placed = (
        P(None, "seq", None),
        P("section", None),
        P("section", "seq", None),
        P("section", "seq", None),
        P("section", "seq", None),
    )

    def step(latents, *weights):
        fits = Plan.fits(
            mesh.shape["section"],
            mesh.shape["seq"],
            latents.shape[0],
            latents.shape[1] // mesh.shape["seq"],
            latents.shape[2],
        )
        mapped = jax.shard_map(
            plane_body if fits else body,
            mesh=mesh,
            in_specs=placed,
            out_specs=P(None, "seq", "section"),
            check_vma=False,
        )
        return mapped(latents, *weights)

    return step
```

```python
import jax
import jax.numpy as jnp
from jax import lax
from jax.experimental import pallas as pl
from jax.experimental.pallas import tpu as pltpu
from jax.sharding import PartitionSpec as P

HEADS = 16
HEAD_DIM = 64


EPSILON = 1e-05


def partner(value, axis, bit):
    mask = 2**bit
    pairs = [(source, source ^ mask) for source in range(lax.axis_size(axis))]
    return lax.ppermute(value, axis, pairs)


def shifted(value, axis, steps):
    count = lax.axis_size(axis)
    initial, last = (max(0, -steps), min(count, count - steps))
    return lax.ppermute(value, axis, [(source, source + steps) for source in range(initial, last)])


def layer_norm(hidden, gain_row):
    values = hidden.astype(jnp.float32)
    center = values - jnp.mean(values, axis=-1, keepdims=True)
    spread = jnp.mean(center * center, axis=-1, keepdims=True)
    return (center * lax.rsqrt(spread + EPSILON) * gain_row).astype(jnp.bfloat16)


def body(latents, norm_gain, qkv_weight, proj_weight, merge_weight):
    seq_count = lax.axis_size("seq")
    section_count = lax.axis_size("section")
    my_section = lax.axis_index("section")
    midpoint = section_count // 2
    windows = latents.shape[0]
    tok_rows = latents.shape[1]
    features = latents.shape[2]
    repeat = max(seq_count // HEADS, 1)
    groups = seq_count // repeat
    head_cols = features * repeat // seq_count
    per_device = head_cols // HEAD_DIM
    part_rows = tok_rows // repeat
    scale_factor = HEAD_DIM ** (-0.5)
    w_qkv, w_proj, w_merge = (
        lax.all_gather(qkv_weight, "seq", axis=1, tiled=True),
        lax.all_gather(proj_weight, "seq", axis=1, tiled=True),
        lax.all_gather(merge_weight, "seq", axis=1, tiled=True),
    )
    w_qkv = w_qkv[0]
    w_proj = w_proj[0]
    w_merge = w_merge[0]
    gain_row = norm_gain[0]
    decoder = my_section >= midpoint
    encoder = my_section < midpoint
    query_shape = (seq_count, part_rows * head_cols)
    key_shape = (seq_count, tok_rows * head_cols)

    def to_heads(array_in, spread_copies):
        if spread_copies:
            grouped = array_in.reshape(tok_rows, groups, head_cols).transpose(1, 0, 2)
            grouped = grouped.reshape(groups, 1, tok_rows * head_cols)
            grouped = jnp.broadcast_to(grouped, (groups, repeat, tok_rows * head_cols))
            return grouped.reshape(seq_count, tok_rows * head_cols)
        grouped = array_in.reshape(part_rows, repeat, groups, head_cols).transpose(2, 1, 0, 3)
        return grouped.reshape(seq_count, part_rows * head_cols)

    def from_heads(array_in):
        grouped = array_in.reshape(groups, repeat, part_rows, head_cols).transpose(2, 1, 0, 3)
        return grouped.reshape(tok_rows, features)

    def project(carried):
        normed = layer_norm(carried, gain_row)
        packed = jnp.dot(normed, w_qkv, preferred_element_type=jnp.float32).astype(jnp.bfloat16)
        return (
            to_heads(packed[:, :features], False),
            to_heads(packed[:, features : 2 * features], True),
            to_heads(packed[:, 2 * features :], True),
        )

    def spare_heads():
        return (
            jnp.zeros(query_shape, jnp.bfloat16),
            jnp.zeros(key_shape, jnp.bfloat16),
            jnp.zeros(key_shape, jnp.bfloat16),
        )

    def attend(queries, keys_in, values_in):
        query_rows = queries.reshape(-1, per_device, HEAD_DIM)
        key_rows = keys_in.reshape(-1, per_device, HEAD_DIM)
        value_rows = values_in.reshape(-1, per_device, HEAD_DIM)
        block_rows = min(512, query_rows.shape[0])
        blocked = query_rows.reshape(-1, block_rows, per_device, HEAD_DIM)

        def one_block(query_block):
            scores = (
                jnp.einsum(
                    "qhd,khd->hqk", query_block, key_rows, preferred_element_type=jnp.float32
                )
                * scale_factor
            )
            row_max = jnp.max(scores, axis=-1, keepdims=True)
            weights = jnp.exp(scores - row_max)
            totals = jnp.sum(weights, axis=-1)
            probs = weights.astype(jnp.bfloat16)
            mixed = jnp.einsum(
                "hqk,khd->qhd", probs, value_rows, preferred_element_type=jnp.float32
            )
            return (mixed / totals.T[:, :, None]).astype(jnp.bfloat16)

        return lax.map(one_block, blocked).reshape(query_shape)

    def mirror_each(skip_term):
        for bit_no in range(section_count.bit_length() - 1):
            skip_term = partner(skip_term, "section", bit_no)
        return skip_term

    def tick(tick_no, loop_state):
        incoming, skip_store, result = loop_state
        window_no = tick_no - my_section
        active = (window_no >= 0) & (window_no < windows)
        chosen = jnp.clip(window_no, 0, windows - 1)
        fresh = lax.dynamic_index_in_dim(latents, chosen, 0, keepdims=False)
        entering = jnp.where(my_section == 0, fresh, incoming)
        skip_slot = lax.dynamic_index_in_dim(skip_store, chosen, 0, keepdims=False)
        carried = lax.cond(
            active & decoder,
            lambda: (
                jnp.dot(entering, w_merge, preferred_element_type=jnp.float32)
                + skip_slot.astype(jnp.float32)
            ).astype(jnp.bfloat16),
            lambda: entering,
        )
        queries, keys_in, values_in = lax.cond(active, lambda: project(carried), spare_heads)
        queries, keys_in, values_in = (
            lax.all_to_all(queries, "seq", split_axis=0, concat_axis=0, tiled=True),
            lax.all_to_all(keys_in, "seq", split_axis=0, concat_axis=0, tiled=True),
            lax.all_to_all(values_in, "seq", split_axis=0, concat_axis=0, tiled=True),
        )
        attended = lax.cond(
            active,
            lambda: attend(queries, keys_in, values_in),
            lambda: jnp.zeros(query_shape, jnp.bfloat16),
        )
        attended = lax.all_to_all(attended, "seq", split_axis=0, concat_axis=0, tiled=True)
        leaving = lax.cond(
            active,
            lambda: (
                carried.astype(jnp.float32)
                + jnp.dot(from_heads(attended), w_proj, preferred_element_type=jnp.float32)
            ).astype(jnp.bfloat16),
            lambda: carried,
        )
        skip_term = lax.cond(
            active & encoder,
            lambda: jnp.dot(leaving, w_merge, preferred_element_type=jnp.float32).astype(
                jnp.bfloat16
            ),
            lambda: jnp.zeros_like(leaving),
        )
        arrived = mirror_each(skip_term)
        source_no = tick_no - (section_count - 1 - my_section)
        landing = decoder & (source_no >= 0) & (source_no < windows)
        target = jnp.clip(source_no, 0, windows - 1)
        updated = lax.dynamic_update_index_in_dim(skip_store, arrived, target, 0)
        skip_store = jnp.where(landing, updated, skip_store)
        incoming = shifted(leaving, "section", 1)
        finished = lax.dynamic_update_index_in_dim(result, leaving.astype(jnp.float32), chosen, 0)
        result = jnp.where(active & (my_section == section_count - 1), finished, result)
        return (incoming, skip_store, result)

    loop_state = (
        jnp.zeros(latents.shape[1:], jnp.bfloat16),
        jnp.zeros_like(latents),
        jnp.zeros(latents.shape, jnp.float32),
    )
    loop_state = lax.fori_loop(0, windows + section_count - 1, tick, loop_state)
    result = loop_state[2]
    return lax.psum_scatter(result.astype(jnp.bfloat16), "section", scatter_dimension=2, tiled=True)


class Plan:
    def __init__(self, sections, seq_count, windows, tok_rows, features):
        self.sections = sections
        self.seq_count = seq_count
        self.windows = windows
        self.tok_rows = tok_rows
        self.features = features
        self.inner = seq_count // windows
        self.slots = sections * self.inner
        self.half = tok_rows // sections
        self.shard = windows * self.half
        self.tokens = self.slots * self.shard
        self.cols = features // self.slots
        self.half_cols = features // sections
        self.w_rows = features // seq_count
        self.group = self.inner * self.w_rows
        self.chips = [(mx, mi) for mx in range(sections) for mi in range(0, self.inner, 2)]

    @staticmethod
    def fits(sections, seq_count, windows, tok_rows, features):
        if sections != 2 or windows & (windows - 1) or seq_count % (2 * windows):
            return False
        inner = seq_count // windows
        if inner & (inner - 1) or features % (sections * inner * 2 * HEAD_DIM):
            return False
        return features == HEADS * HEAD_DIM and tok_rows % 32 == 0

    def mask(self, mx=0, mz=0, mi=0):
        return mx * self.seq_count + mz * self.inner + mi


def attention(qkv, out, cols, rows_q):
    tokens = qkv.shape[0]
    lane_head = lax.broadcasted_iota(jnp.int32, (1, cols), 1) // HEAD_DIM

    def one_block(block_no, carry):
        rows = pl.ds(pl.multiple_of(block_no * rows_q, rows_q), rows_q)
        query = qkv[rows, 0:cols]
        keys_in = qkv[:, cols : 2 * cols]
        values_in = qkv[:, 2 * cols : 3 * cols]
        mixed = jnp.zeros((rows_q, cols), jnp.float32)
        for head in range(cols // HEAD_DIM):
            mine = lane_head == head
            picked = jnp.where(mine, query, jnp.zeros_like(query))
            scores = lax.dot_general(
                picked, keys_in, (((1,), (1,)), ((), ())), preferred_element_type=jnp.float32
            )
            row_max = jnp.max(scores, axis=-1, keepdims=True)
            weights = jnp.exp(scores - row_max)
            totals = jnp.sum(weights, axis=-1, keepdims=True)
            part = jnp.dot(
                weights.astype(jnp.bfloat16), values_in, preferred_element_type=jnp.float32
            )
            mixed = jnp.where(mine, part / totals, mixed)
        out[rows, :] = mixed.astype(jnp.bfloat16)
        return carry

    lax.fori_loop(0, tokens // rows_q, one_block, 0)


def project_rows(normed, w_qkv, cols):
    packed = jnp.dot(normed, w_qkv, preferred_element_type=jnp.float32)
    lane = lax.broadcasted_iota(jnp.int32, (1, packed.shape[1]), 1)
    packed = packed.astype(jnp.bfloat16)
    return jnp.where(lane < cols, packed * jnp.bfloat16(HEAD_DIM ** (-0.5)), packed)


def slot_of(plan, where, mx, mi):
    return (where[0] ^ mx) * plan.inner + (where[2] ^ mi)


def aligned(index, size):
    return pl.ds(pl.multiple_of(index * size, size), size)


def start_all(copies):
    for copy in copies:
        copy.start()
    for copy in copies:
        copy.wait()


def prepare_kernel(plan, where, latents, qkv_weight, proj_weight, merge_weight, *rest):
    shares = rest[: plan.windows]
    keep, give, cross, sems = rest[plan.windows :]
    copies = []

    def add(source, target):
        copies.append(pltpu.make_async_copy(source, target, sems.at[len(copies)]))

    for core, target in ((1, give), (0, keep)):
        for chip_no, (mx, mi) in enumerate(plan.chips):
            slot = slot_of(plan, where, mx, mi ^ core)
            for part in range(3):
                add(
                    qkv_weight.at[0, :, aligned(part * plan.slots + slot, plan.cols)],
                    target.at[chip_no, :, part * plan.cols : (part + 1) * plan.cols],
                )
    width = plan.half_cols
    for part, matrix in enumerate((proj_weight, merge_weight)):
        add(
            matrix.at[0, :, aligned(where[0] ^ 1, width)],
            cross.at[:, part * width : (part + 1) * width],
        )
    for mz in range(plan.windows):
        add(latents.at[where[1] ^ mz, aligned(where[0], plan.half), :], shares[mz])
    start_all(copies)


def pair_kernel(plan, keep, given, *outs):
    rows = plan.w_rows
    for chip_no, out in enumerate(outs):
        out[0:rows, :] = keep[chip_no]
        out[rows:, :] = given[chip_no]


def sort_kernel(plan, where, *refs):
    count = len(plan.chips)
    pieces, outs = (refs[:count], refs[count:])
    rows = 2 * plan.w_rows
    for section in range(plan.sections):

        @pl.when(where[0] == section)
        def _():
            for piece, (mx, mi) in zip(pieces, plan.chips):
                start = mi * plan.w_rows
                outs[section ^ mx][start : start + rows, :] = piece[...]


def merge_kernel(plan, where, proj_weight, merge_weight, crossed, mats, last):
    width = plan.half_cols
    for section in range(plan.sections):

        @pl.when(where[0] == section)
        def _():
            lanes = slice(section * width, (section + 1) * width)
            mine = proj_weight[0, :, lanes]
            others = crossed[:, 0:width]
            mats[:, 0:width] = mine if section == 0 else others
            last[...] = others if section == 0 else mine
            total = merge_weight[0, :, lanes].astype(jnp.float32)
            total = total + crossed[:, width:].astype(jnp.float32)
            mats[:, width:] = total.astype(jnp.bfloat16)


def stack_kernel(*refs):
    start = 0
    for piece in refs[:-1]:
        rows = piece.shape[0]
        refs[-1][start : start + rows, :] = piece[...]
        start += rows


def gather_weights(plan, where, pieces, target):
    rows = plan.w_rows
    for mz, piece in enumerate(pieces):
        for mi in range(plan.inner):
            shard = (where[1] ^ mz) * plan.inner + (where[2] ^ mi)
            target[aligned(shard, rows), :] = piece[mi * rows : (mi + 1) * rows, :]


def plane_order(plan):
    return [(mx, mi ^ core) for core in range(2) for mx, mi in plan.chips]


def first_kernel(plan, where, gain, *rest):
    hidden_in = rest[: plan.slots]
    pieces = rest[plan.slots : plan.slots + plan.windows]
    out, w_qkv, qkv = rest[plan.slots + plan.windows :]
    gather_weights(plan, where, pieces, w_qkv)
    for piece, (mx, mi) in zip(hidden_in, plane_order(plan)):
        normed = layer_norm(piece[...], gain[...])
        rows = aligned(slot_of(plan, where, mx, mi), plan.shard)
        qkv[rows, :] = project_rows(normed, w_qkv[...], plan.cols)
    attention(qkv, out, plan.cols, min(256, plan.tokens))


def second_kernel(plan, where, gain, *rest):
    slots, windows = (plan.slots, plan.windows)
    hidden_in, rest = (rest[:slots], rest[slots:])
    attended_in, rest = (rest[:slots], rest[slots:])
    mats_in, rest = (rest[:slots], rest[slots:])
    pieces, rest = (rest[:windows], rest[windows:])
    outs, rest = (rest[: plan.inner // 2], rest[plan.inner // 2 :])
    kept, att, mats, w_qkv, joined, qkv, mixed = rest
    order = plane_order(plan)
    for piece, (mx, mi) in zip(attended_in, order):
        att[:, aligned(slot_of(plan, where, mx, mi), plan.cols)] = piece[...]
    rows = plan.w_rows
    for piece, (mx, mi) in zip(mats_in, order):
        for mz in range(windows):
            shard = (where[1] ^ mz) * plan.inner + (where[2] ^ mi)
            mats[where[0] ^ mx, aligned(shard, rows), :] = piece[mz * rows : (mz + 1) * rows, :]
    gather_weights(plan, where, pieces, w_qkv)
    width = plan.half_cols
    for piece, (mx, mi) in zip(hidden_in, order):
        part = aligned(slot_of(plan, where, mx, mi), plan.shard)
        attended = att[part, :]
        hidden = jnp.concatenate(
            [
                jnp.dot(attended, mats[side, :, 0:width], preferred_element_type=jnp.float32)
                for side in range(plan.sections)
            ],
            axis=1,
        )
        hidden = (piece[...].astype(jnp.float32) + hidden).astype(jnp.bfloat16)
        merged = jnp.concatenate(
            [
                jnp.dot(hidden, mats[side, :, width:], preferred_element_type=jnp.float32)
                for side in range(plan.sections)
            ],
            axis=1,
        ).astype(jnp.bfloat16)
        joined[part, :] = merged
        normed = layer_norm(merged, gain[...])
        qkv[part, :] = project_rows(normed, w_qkv[...], plan.cols)
    attention(qkv, mixed, plan.cols, min(256, plan.tokens))
    lanes = aligned(where[0], width)
    for side in range(plan.sections):
        for mi in range(plan.inner):
            part = aligned(side * plan.inner + (where[2] ^ mi), plan.shard)
            start = ((mi % 2) * plan.sections + side) * plan.shard
            outs[mi // 2][start : start + plan.shard, :] = mixed[part, :]
            if mi == 0:
                kept[side * plan.shard : (side + 1) * plan.shard, :] = joined[part, lanes]


def third_kernel(plan, where, kept, *rest):
    chips, rest = (rest[: len(plan.chips)], rest[len(plan.chips) :])
    swapped, mats_in = (rest[0], rest[1 : 1 + plan.inner])
    outs, (att, mat) = (rest[1 + plan.inner : -2], rest[-2:])
    rows = plan.sections * plan.shard
    for chip_no, (mx, mi) in enumerate(plan.chips):
        for core in range(2):
            lanes = aligned(slot_of(plan, where, mx, mi ^ core), plan.cols)
            if core == 0:
                att[:, lanes] = chips[chip_no][0:rows, :]
            else:
                att[:, lanes] = swapped[chip_no * rows : (chip_no + 1) * rows, :]
    rows = plan.w_rows
    order = [mi ^ core for core in range(2) for mi in range(0, plan.inner, 2)]
    for piece, mi in zip(mats_in, order):
        for mz in range(plan.windows):
            shard = (where[1] ^ mz) * plan.inner + (where[2] ^ mi)
            mat[aligned(shard, rows), :] = piece[mz * rows : (mz + 1) * rows, :]
    result = jnp.dot(att[...], mat[...], preferred_element_type=jnp.float32)
    result = (kept[...].astype(jnp.float32) + result).astype(jnp.bfloat16)
    for side in range(plan.sections):
        for mz in range(plan.windows):
            start = side * plan.shard + mz * plan.half
            outs[mz][side * plan.half : (side + 1) * plan.half, :] = result[
                start : start + plan.half, :
            ]


def place_kernel(plan, where, *refs):
    for mz in range(plan.windows):
        refs[-1][where[1] ^ mz] = refs[mz][...]


def halves_kernel(plan, *refs):
    rows = plan.sections * plan.shard
    for chip_no, piece in enumerate(refs[:-1]):
        refs[-1][chip_no * rows : (chip_no + 1) * rows, :] = piece[rows:, :]


def plane_body(latents, norm_gain, qkv_weight, proj_weight, merge_weight):
    plan = Plan(
        lax.axis_size("section"), lax.axis_size("seq"), latents.shape[0], *latents.shape[1:]
    )
    windows, inner, shard, cols = (plan.windows, plan.inner, plan.shard, plan.cols)
    section = lax.axis_index("section")
    position = lax.axis_index("seq")
    window, place = (position // inner, position % inner)
    lane = lax.iota(jnp.int32, 3)
    where = jnp.where(lane == 0, section, jnp.where(lane == 1, window, place)).astype(jnp.int32)
    devices = plan.sections * plan.seq_count
    bf16 = jnp.bfloat16
    smem = pl.BlockSpec(memory_space=pltpu.SMEM)
    anywhere = pl.BlockSpec(memory_space=pl.ANY)
    vmem = pl.BlockSpec(memory_space=pltpu.VMEM)
    tokens, features, width = (plan.tokens, plan.features, plan.half_cols)

    def swap(value, mask):
        pairs = [(source, source ^ mask) for source in range(devices)]
        return lax.ppermute(value, ("section", "seq"), pairs)

    def call(kernel, outs, ins, scratch=(), specs=None, flops=0, limit=40):
        shapes = tuple(jax.ShapeDtypeStruct(shape, bf16) for shape in outs)
        moved = sum(2 * value.size for value in ins)
        return pl.pallas_call(
            kernel,
            out_shape=shapes,
            in_specs=specs or [vmem] * len(ins),
            out_specs=tuple(vmem for _ in shapes),
            scratch_shapes=list(scratch),
            cost_estimate=pl.CostEstimate(
                flops=flops, bytes_accessed=moved, transcendentals=0
            ),
            compiler_params=pltpu.CompilerParams(vmem_limit_bytes=limit << 20),
        )(*ins)

    def stack(pieces):
        rows = sum(piece.shape[0] for piece in pieces)
        return call(stack_kernel, [(rows, pieces[0].shape[1])], pieces, limit=8)[0]

    def z_gather(value):
        far = swap(value, plan.mask(mz=2))
        near = swap(value, plan.mask(mz=1))
        return [value, near, far, swap(far, plan.mask(mz=1))]

    def chip_gather(value):
        return [value] + [
            swap(value, plan.mask(mx=mx, mi=mi))
            for chip_no, (mx, mi) in enumerate(plan.chips)
            if chip_no
        ]

    def core_gather(pieces):
        return pieces + [swap(piece, plan.mask(mi=1)) for piece in pieces]

    n_parts = 6 * len(plan.chips)
    prepared = call(
        lambda *refs: prepare_kernel(plan, *refs),
        [(plan.half, features)] * windows
        + [(len(plan.chips), plan.w_rows, 3 * cols)] * 2
        + [(plan.w_rows, 2 * width)],
        [where, latents, qkv_weight, proj_weight, merge_weight],
        [pltpu.SemaphoreType.DMA((n_parts + 2 + windows,))],
        [smem] + [anywhere] * 4,
        limit=8,
    )
    shares, (keep, give, cross) = (prepared[:windows], prepared[windows:])
    given = swap(give, plan.mask(mi=1))
    crossed = swap(cross, plan.mask(mx=1))
    other_gain = swap(norm_gain, plan.mask(mx=1))
    gain_a = jnp.where(section == 0, norm_gain, other_gain)
    gain_b = jnp.where(section == 0, other_gain, norm_gain)
    shares = [shares[0]] + [swap(shares[mz], plan.mask(mz=mz)) for mz in range(1, windows)]
    outgoing = call(
        lambda *refs: pair_kernel(plan, *refs),
        [(2 * plan.w_rows, 3 * cols)] * len(plan.chips),
        [keep, given],
        limit=8,
    )
    incoming = [outgoing[0]] + [
        swap(outgoing[chip_no], plan.mask(mx=mx, mi=mi))
        for chip_no, (mx, mi) in enumerate(plan.chips)
        if chip_no
    ]
    mats, last = call(
        lambda *refs: merge_kernel(plan, *refs),
        [(plan.w_rows, 2 * width), (plan.w_rows, width)],
        [where, proj_weight, merge_weight, crossed],
        (),
        [smem] + [vmem] * 3,
        limit=8,
    )
    mats = z_gather(mats)
    hidden = chip_gather(stack(shares))
    hidden = core_gather(hidden)
    rows_a, rows_b = call(
        lambda *refs: sort_kernel(plan, *refs),
        [(plan.group, 3 * cols)] * 2,
        [where] + incoming,
        (),
        [smem] + [vmem] * len(incoming),
        limit=8,
    )
    pieces_a = z_gather(rows_a)
    mats = chip_gather(stack(mats))
    pieces_b = [rows_b] + [swap(rows_b, plan.mask(mz=mz)) for mz in range(1, windows)]
    last = [last] + [swap(last, plan.mask(mz=mz)) for mz in range(1, windows)]

    (attended,) = call(
        lambda *refs: first_kernel(plan, *refs),
        [(tokens, cols)],
        [where, gain_a] + hidden + pieces_a,
        [pltpu.VMEM((features, 3 * cols), bf16), pltpu.VMEM((tokens, 3 * cols), bf16)],
        [smem] + [vmem] * (1 + len(hidden) + windows),
        flops=10_000_000_000,
    )
    attended = core_gather(chip_gather(attended))
    mats = core_gather(mats)
    last = stack(last)
    last = [last] + [swap(last, plan.mask(mi=mi)) for mi in range(2, inner, 2)]
    last = core_gather(last)
    *attended, kept = call(
        lambda *refs: second_kernel(plan, *refs),
        [(2 * plan.sections * shard, cols)] * (inner // 2) + [(plan.sections * shard, width)],
        [where, gain_b] + hidden + attended + mats + pieces_b,
        [
            pltpu.VMEM((tokens, features), bf16),
            pltpu.VMEM((plan.sections, features, 2 * width), bf16),
            pltpu.VMEM((features, 3 * cols), bf16),
            pltpu.VMEM((tokens, features), bf16),
            pltpu.VMEM((tokens, 3 * cols), bf16),
            pltpu.VMEM((tokens, cols), bf16),
        ],
        [smem] + [vmem] * (1 + 3 * plan.slots + windows),
        flops=18_000_000_000,
    )
    back = [attended[0]] + [
        swap(attended[mi // 2], plan.mask(mx=mx, mi=mi))
        for chip_no, (mx, mi) in enumerate(plan.chips)
        if chip_no
    ]
    (halves,) = call(
        lambda *refs: halves_kernel(plan, *refs),
        [(len(plan.chips) * plan.sections * shard, cols)],
        back,
        limit=8,
    )
    swapped = swap(halves, plan.mask(mi=1))
    outcome = call(
        lambda *refs: third_kernel(plan, *refs),
        [(plan.tok_rows, width)] * windows,
        [where, kept] + back + [swapped] + last,
        [
            pltpu.VMEM((plan.sections * shard, features), bf16),
            pltpu.VMEM((features, width), bf16),
        ],
        [smem] + [vmem] * (2 + len(back) + inner),
        flops=1_000_000_000,
        limit=16,
    )
    outcome = [outcome[0]] + [swap(outcome[mz], plan.mask(mz=mz)) for mz in range(1, windows)]
    return call(
        lambda *refs: place_kernel(plan, *refs),
        [(windows, plan.tok_rows, width)],
        [where] + outcome,
        (),
        [smem] + [vmem] * windows,
        limit=8,
    )[0]


def solution(mesh):
    placed = (
        P(None, "seq", None),
        P("section", None),
        P("section", "seq", None),
        P("section", "seq", None),
        P("section", "seq", None),
    )

    def plane_step(*arguments):
        return plane_body(*arguments)

    def step(latents, *weights):
        fits = Plan.fits(
            mesh.shape["section"],
            mesh.shape["seq"],
            latents.shape[0],
            latents.shape[1] // mesh.shape["seq"],
            latents.shape[2],
        )
        mapped = jax.shard_map(
            plane_step if fits else body,
            mesh=mesh,
            in_specs=placed,
            out_specs=P(None, "seq", "section"),
            check_vma=False,
        )
        return mapped(latents, *weights)

    return step
```

```python
import jax
import jax.numpy as jnp
from jax import lax
from jax.experimental import pallas as pl
from jax.experimental.pallas import tpu as pltpu
from jax.sharding import PartitionSpec as P

HEADS = 16
HEAD_DIM = 64


EPSILON = 1e-05


def partner(value, axis, bit):
    mask = 2**bit
    pairs = [(source, source ^ mask) for source in range(lax.axis_size(axis))]
    return lax.ppermute(value, axis, pairs)


def shifted(value, axis, steps):
    count = lax.axis_size(axis)
    initial, last = (max(0, -steps), min(count, count - steps))
    return lax.ppermute(value, axis, [(source, source + steps) for source in range(initial, last)])


def layer_norm(hidden, gain_row):
    values = hidden.astype(jnp.float32)
    center = values - jnp.mean(values, axis=-1, keepdims=True)
    spread = jnp.mean(center * center, axis=-1, keepdims=True)
    return (center * lax.rsqrt(spread + EPSILON) * gain_row).astype(jnp.bfloat16)


def body(latents, norm_gain, qkv_weight, proj_weight, merge_weight):
    seq_count = lax.axis_size("seq")
    section_count = lax.axis_size("section")
    my_section = lax.axis_index("section")
    midpoint = section_count // 2
    windows = latents.shape[0]
    tok_rows = latents.shape[1]
    features = latents.shape[2]
    repeat = max(seq_count // HEADS, 1)
    groups = seq_count // repeat
    head_cols = features * repeat // seq_count
    per_device = head_cols // HEAD_DIM
    part_rows = tok_rows // repeat
    scale_factor = HEAD_DIM ** (-0.5)
    w_qkv, w_proj, w_merge = (
        lax.all_gather(qkv_weight, "seq", axis=1, tiled=True),
        lax.all_gather(proj_weight, "seq", axis=1, tiled=True),
        lax.all_gather(merge_weight, "seq", axis=1, tiled=True),
    )
    w_qkv = w_qkv[0]
    w_proj = w_proj[0]
    w_merge = w_merge[0]
    gain_row = norm_gain[0]
    decoder = my_section >= midpoint
    encoder = my_section < midpoint
    query_shape = (seq_count, part_rows * head_cols)
    key_shape = (seq_count, tok_rows * head_cols)

    def to_heads(array_in, spread_copies):
        if spread_copies:
            grouped = array_in.reshape(tok_rows, groups, head_cols).transpose(1, 0, 2)
            grouped = grouped.reshape(groups, 1, tok_rows * head_cols)
            grouped = jnp.broadcast_to(grouped, (groups, repeat, tok_rows * head_cols))
            return grouped.reshape(seq_count, tok_rows * head_cols)
        grouped = array_in.reshape(part_rows, repeat, groups, head_cols).transpose(2, 1, 0, 3)
        return grouped.reshape(seq_count, part_rows * head_cols)

    def from_heads(array_in):
        grouped = array_in.reshape(groups, repeat, part_rows, head_cols).transpose(2, 1, 0, 3)
        return grouped.reshape(tok_rows, features)

    def project(carried):
        normed = layer_norm(carried, gain_row)
        packed = jnp.dot(normed, w_qkv, preferred_element_type=jnp.float32).astype(jnp.bfloat16)
        return (
            to_heads(packed[:, :features], False),
            to_heads(packed[:, features : 2 * features], True),
            to_heads(packed[:, 2 * features :], True),
        )

    def spare_heads():
        return (
            jnp.zeros(query_shape, jnp.bfloat16),
            jnp.zeros(key_shape, jnp.bfloat16),
            jnp.zeros(key_shape, jnp.bfloat16),
        )

    def attend(queries, keys_in, values_in):
        query_rows = queries.reshape(-1, per_device, HEAD_DIM)
        key_rows = keys_in.reshape(-1, per_device, HEAD_DIM)
        value_rows = values_in.reshape(-1, per_device, HEAD_DIM)
        block_rows = min(512, query_rows.shape[0])
        blocked = query_rows.reshape(-1, block_rows, per_device, HEAD_DIM)

        def one_block(query_block):
            scores = (
                jnp.einsum(
                    "qhd,khd->hqk", query_block, key_rows, preferred_element_type=jnp.float32
                )
                * scale_factor
            )
            row_max = jnp.max(scores, axis=-1, keepdims=True)
            weights = jnp.exp(scores - row_max)
            totals = jnp.sum(weights, axis=-1)
            probs = weights.astype(jnp.bfloat16)
            mixed = jnp.einsum(
                "hqk,khd->qhd", probs, value_rows, preferred_element_type=jnp.float32
            )
            return (mixed / totals.T[:, :, None]).astype(jnp.bfloat16)

        return lax.map(one_block, blocked).reshape(query_shape)

    def mirror_each(skip_term):
        for bit_no in range(section_count.bit_length() - 1):
            skip_term = partner(skip_term, "section", bit_no)
        return skip_term

    def tick(tick_no, loop_state):
        incoming, skip_store, result = loop_state
        window_no = tick_no - my_section
        active = (window_no >= 0) & (window_no < windows)
        chosen = jnp.clip(window_no, 0, windows - 1)
        fresh = lax.dynamic_index_in_dim(latents, chosen, 0, keepdims=False)
        entering = jnp.where(my_section == 0, fresh, incoming)
        skip_slot = lax.dynamic_index_in_dim(skip_store, chosen, 0, keepdims=False)
        carried = lax.cond(
            active & decoder,
            lambda: (
                jnp.dot(entering, w_merge, preferred_element_type=jnp.float32)
                + skip_slot.astype(jnp.float32)
            ).astype(jnp.bfloat16),
            lambda: entering,
        )
        queries, keys_in, values_in = lax.cond(active, lambda: project(carried), spare_heads)
        queries, keys_in, values_in = (
            lax.all_to_all(queries, "seq", split_axis=0, concat_axis=0, tiled=True),
            lax.all_to_all(keys_in, "seq", split_axis=0, concat_axis=0, tiled=True),
            lax.all_to_all(values_in, "seq", split_axis=0, concat_axis=0, tiled=True),
        )
        attended = lax.cond(
            active,
            lambda: attend(queries, keys_in, values_in),
            lambda: jnp.zeros(query_shape, jnp.bfloat16),
        )
        attended = lax.all_to_all(attended, "seq", split_axis=0, concat_axis=0, tiled=True)
        leaving = lax.cond(
            active,
            lambda: (
                carried.astype(jnp.float32)
                + jnp.dot(from_heads(attended), w_proj, preferred_element_type=jnp.float32)
            ).astype(jnp.bfloat16),
            lambda: carried,
        )
        skip_term = lax.cond(
            active & encoder,
            lambda: jnp.dot(leaving, w_merge, preferred_element_type=jnp.float32).astype(
                jnp.bfloat16
            ),
            lambda: jnp.zeros_like(leaving),
        )
        arrived = mirror_each(skip_term)
        source_no = tick_no - (section_count - 1 - my_section)
        landing = decoder & (source_no >= 0) & (source_no < windows)
        target = jnp.clip(source_no, 0, windows - 1)
        updated = lax.dynamic_update_index_in_dim(skip_store, arrived, target, 0)
        skip_store = jnp.where(landing, updated, skip_store)
        incoming = shifted(leaving, "section", 1)
        finished = lax.dynamic_update_index_in_dim(result, leaving.astype(jnp.float32), chosen, 0)
        result = jnp.where(active & (my_section == section_count - 1), finished, result)
        return (incoming, skip_store, result)

    loop_state = (
        jnp.zeros(latents.shape[1:], jnp.bfloat16),
        jnp.zeros_like(latents),
        jnp.zeros(latents.shape, jnp.float32),
    )
    loop_state = lax.fori_loop(0, windows + section_count - 1, tick, loop_state)
    result = loop_state[2]
    return lax.psum_scatter(result.astype(jnp.bfloat16), "section", scatter_dimension=2, tiled=True)


class Plan:
    def __init__(self, sections, seq_count, windows, tok_rows, features):
        self.sections = sections
        self.seq_count = seq_count
        self.windows = windows
        self.tok_rows = tok_rows
        self.features = features
        self.inner = seq_count // windows
        self.slots = sections * self.inner
        self.half = tok_rows // sections
        self.shard = windows * self.half
        self.tokens = self.slots * self.shard
        self.cols = features // self.slots
        self.half_cols = features // sections
        self.w_rows = features // seq_count
        self.group = self.inner * self.w_rows
        self.chips = [(mx, mi) for mx in range(sections) for mi in range(0, self.inner, 2)]

    @staticmethod
    def fits(sections, seq_count, windows, tok_rows, features):
        if sections != 2 or windows & (windows - 1) or seq_count % (2 * windows):
            return False
        inner = seq_count // windows
        if inner & (inner - 1) or features % (sections * inner * 2 * HEAD_DIM):
            return False
        return features == HEADS * HEAD_DIM and tok_rows % 32 == 0

    def mask(self, mx=0, mz=0, mi=0):
        return mx * self.seq_count + mz * self.inner + mi


def attention(qkv, out, cols, rows_q):
    tokens = qkv.shape[0]
    lane_head = lax.broadcasted_iota(jnp.int32, (1, cols), 1) // HEAD_DIM

    def one_block(block_no, carry):
        rows = pl.ds(pl.multiple_of(block_no * rows_q, rows_q), rows_q)
        query = qkv[rows, 0:cols]
        keys_in = qkv[:, cols : 2 * cols]
        values_in = qkv[:, 2 * cols : 3 * cols]
        mixed = jnp.zeros((rows_q, cols), jnp.float32)
        for head in range(cols // HEAD_DIM):
            mine = lane_head == head
            picked = jnp.where(mine, query, jnp.zeros_like(query))
            scores = lax.dot_general(
                picked, keys_in, (((1,), (1,)), ((), ())), preferred_element_type=jnp.float32
            )
            row_max = jnp.max(scores, axis=-1, keepdims=True)
            weights = jnp.exp(scores - row_max)
            totals = jnp.sum(weights, axis=-1, keepdims=True)
            part = jnp.dot(
                weights.astype(jnp.bfloat16), values_in, preferred_element_type=jnp.float32
            )
            mixed = jnp.where(mine, part / totals, mixed)
        out[rows, :] = mixed.astype(jnp.bfloat16)
        return carry

    lax.fori_loop(0, tokens // rows_q, one_block, 0)


def project_rows(normed, w_qkv, cols):
    packed = jnp.dot(normed, w_qkv, preferred_element_type=jnp.float32)
    lane = lax.broadcasted_iota(jnp.int32, (1, packed.shape[1]), 1)
    packed = packed.astype(jnp.bfloat16)
    return jnp.where(lane < cols, packed * jnp.bfloat16(HEAD_DIM ** (-0.5)), packed)


def slot_of(plan, where, mx, mi):
    return (where[0] ^ mx) * plan.inner + (where[2] ^ mi)


def aligned(index, size):
    return pl.ds(pl.multiple_of(index * size, size), size)


def prepare_kernel(plan, where, latents, gain, qkv_weight, proj_weight, merge_weight, *rest):
    shares = rest[: plan.windows]
    keep, give, cross, held, sems = rest[plan.windows :]
    copies = []

    def add(source, target):
        copies.append(pltpu.make_async_copy(source, target, sems.at[len(copies)]))

    for part in range(3):
        add(
            qkv_weight.at[0, :, part * plan.features : (part + 1) * plan.features],
            held.at[part],
        )
    width, rows = (plan.half_cols, plan.w_rows)
    for part, matrix in enumerate((proj_weight, merge_weight)):
        add(
            matrix.at[0, :, aligned(where[0] ^ 1, width)],
            cross.at[part * rows : (part + 1) * rows, :],
        )
    for mz in range(plan.windows):
        add(latents.at[where[1] ^ mz, aligned(where[0], plan.half), :], shares[mz])
    for copy in copies:
        copy.start()
    first_row = (where[1] * plan.inner + where[2]) * rows
    row = first_row + lax.broadcasted_iota(jnp.int32, (rows, plan.features), 0)
    lane = lax.broadcasted_iota(jnp.int32, (rows, plan.features), 1)
    factors = jnp.where(row == lane, gain[...], jnp.zeros((1, plan.features), jnp.float32))
    factors = jnp.sum(factors, axis=1, keepdims=True)
    for copy in copies[:3]:
        copy.wait()
    for core, target in ((1, give), (0, keep)):
        for chip_no, (mx, mi) in enumerate(plan.chips):
            lanes = aligned(slot_of(plan, where, mx, mi ^ core), plan.cols)
            for part in range(3):
                scaled = held[part, :, lanes].astype(jnp.float32) * factors
                target[chip_no, :, part * plan.cols : (part + 1) * plan.cols] = scaled.astype(
                    jnp.bfloat16
                )
    for copy in copies[3:]:
        copy.wait()


def pair_kernel(plan, keep, given, cross, *outs):
    rows = plan.w_rows
    for chip_no, (out, chip) in enumerate(zip(outs, plan.chips)):
        out[0:rows, 0 : 3 * plan.cols] = keep[chip_no]
        out[rows:, 0 : 3 * plan.cols] = given[chip_no]
        if chip == (1, 0):
            out[:, 3 * plan.cols :] = cross[...]


def sort_kernel(plan, where, proj_weight, merge_weight, *refs):
    count = len(plan.chips)
    pieces, (rows_a, rows_b, mats) = (refs[:count], refs[count:])
    rows, width, cols = (plan.w_rows, plan.half_cols, 3 * plan.cols)
    lone = width // plan.inner
    crossed = pieces[plan.chips.index((1, 0))]
    for section in range(plan.sections):

        @pl.when(where[0] == section)
        def _():
            outs = (rows_a, rows_b)
            for piece, (mx, mi) in zip(pieces, plan.chips):
                part = slice(mi * rows, (mi + 2) * rows)
                outs[section ^ mx][part, 0:cols] = piece[:, 0:cols]
            lanes = slice(section * width, (section + 1) * width)
            mine = proj_weight[0, :, lanes]
            others = crossed[0:rows, cols:]
            mats[:, 0:width] = mine if section == 0 else others
            last = others if section == 0 else mine
            for mi in range(plan.inner):
                rows_b[mi * rows : (mi + 1) * rows, cols:] = last[:, mi * lone : (mi + 1) * lone]
            total = merge_weight[0, :, lanes].astype(jnp.float32)
            total = total + crossed[rows:, cols:].astype(jnp.float32)
            mats[:, width:] = total.astype(jnp.bfloat16)


def last_kernel(plan, *refs):
    rows, lone = (plan.w_rows, plan.half_cols // plan.inner)
    for mz, piece in enumerate(refs[:-1]):
        for mi in range(plan.inner):
            refs[-1][mz * rows : (mz + 1) * rows, mi * lone : (mi + 1) * lone] = piece[
                mi * rows : (mi + 1) * rows, 3 * plan.cols :
            ]


def stack_kernel(*refs):
    start = 0
    for piece in refs[:-1]:
        rows = piece.shape[0]
        refs[-1][start : start + rows, :] = piece[...]
        start += rows


def gather_weights(plan, where, pieces, target):
    rows = plan.w_rows
    for mz, piece in enumerate(pieces):
        for mi in range(plan.inner):
            shard = (where[1] ^ mz) * plan.inner + (where[2] ^ mi)
            target[aligned(shard, rows), :] = piece[
                mi * rows : (mi + 1) * rows, 0 : 3 * plan.cols
            ]


def plane_order(plan):
    return [(mx, mi ^ core) for core in range(2) for mx, mi in plan.chips]


def normalize(values):
    center = values - jnp.mean(values, axis=-1, keepdims=True)
    spread = jnp.mean(center * center, axis=-1, keepdims=True)
    return (center * lax.rsqrt(spread + EPSILON)).astype(jnp.bfloat16)


def row_blocks(plan, one_block):
    size = min(512, plan.tokens)

    def step(block_no, carry):
        one_block(aligned(block_no, size))
        return carry

    lax.fori_loop(0, plan.tokens // size, step, 0)


def first_kernel(plan, where, *rest):
    hidden_in = rest[: plan.slots]
    pieces = rest[plan.slots : plan.slots + plan.windows]
    out, w_qkv, normed, qkv = rest[plan.slots + plan.windows :]
    gather_weights(plan, where, pieces, w_qkv)
    for piece, (mx, mi) in zip(hidden_in, plane_order(plan)):
        rows = aligned(slot_of(plan, where, mx, mi), plan.shard)
        normed[rows, :] = normalize(piece[...].astype(jnp.float32))

    def one_block(rows):
        qkv[rows, :] = project_rows(normed[rows, :], w_qkv[...], plan.cols)

    row_blocks(plan, one_block)
    attention(qkv, out, plan.cols, min(256, plan.tokens))


def second_kernel(plan, where, *rest):
    slots, windows = (plan.slots, plan.windows)
    hidden_in, rest = (rest[:slots], rest[slots:])
    attended_in, rest = (rest[:slots], rest[slots:])
    mats_in, rest = (rest[:slots], rest[slots:])
    pieces, rest = (rest[:windows], rest[windows:])
    outs, rest = (rest[: plan.inner // 2], rest[plan.inner // 2 :])
    kept, hid, att, mats, w_qkv, joined, qkv, mixed = rest
    order = plane_order(plan)
    for piece, (mx, mi) in zip(hidden_in, order):
        hid[aligned(slot_of(plan, where, mx, mi), plan.shard), :] = piece[...]
    for piece, (mx, mi) in zip(attended_in, order):
        att[:, aligned(slot_of(plan, where, mx, mi), plan.cols)] = piece[...]
    rows = plan.w_rows
    for piece, (mx, mi) in zip(mats_in, order):
        for mz in range(windows):
            shard = (where[1] ^ mz) * plan.inner + (where[2] ^ mi)
            mats[where[0] ^ mx, aligned(shard, rows), :] = piece[mz * rows : (mz + 1) * rows, :]
    gather_weights(plan, where, pieces, w_qkv)
    width = plan.half_cols

    def one_block(part):
        attended = att[part, :]
        hidden = jnp.concatenate(
            [
                jnp.dot(attended, mats[side, :, 0:width], preferred_element_type=jnp.float32)
                for side in range(plan.sections)
            ],
            axis=1,
        )
        hidden = (hid[part, :].astype(jnp.float32) + hidden).astype(jnp.bfloat16)
        merged = jnp.concatenate(
            [
                jnp.dot(hidden, mats[side, :, width:], preferred_element_type=jnp.float32)
                for side in range(plan.sections)
            ],
            axis=1,
        )
        merged = merged.astype(jnp.bfloat16)
        joined[part, :] = merged
        qkv[part, :] = project_rows(
            normalize(merged.astype(jnp.float32)), w_qkv[...], plan.cols
        )

    row_blocks(plan, one_block)
    attention(qkv, mixed, plan.cols, min(256, plan.tokens))
    lanes = aligned(where[0], width)
    for side in range(plan.sections):
        for mi in range(plan.inner):
            part = aligned(side * plan.inner + (where[2] ^ mi), plan.shard)
            start = ((mi % 2) * plan.sections + side) * plan.shard
            outs[mi // 2][start : start + plan.shard, :] = mixed[part, :]
            if mi == 0:
                kept[side * plan.shard : (side + 1) * plan.shard, :] = joined[part, lanes]


def third_kernel(plan, where, kept, *rest):
    chips, rest = (rest[: len(plan.chips)], rest[len(plan.chips) :])
    swapped, mats_in = (rest[0], rest[1 : 1 + plan.inner])
    outs, (att, mat) = (rest[1 + plan.inner : -2], rest[-2:])
    rows = plan.sections * plan.shard
    for chip_no, (mx, mi) in enumerate(plan.chips):
        for core in range(2):
            lanes = aligned(slot_of(plan, where, mx, mi ^ core), plan.cols)
            if core == 0:
                att[:, lanes] = chips[chip_no][0:rows, :]
            else:
                att[:, lanes] = swapped[chip_no * rows : (chip_no + 1) * rows, :]
    rows = plan.w_rows
    order = [mi ^ core for core in range(2) for mi in range(0, plan.inner, 2)]
    for piece, mi in zip(mats_in, order):
        for mz in range(plan.windows):
            shard = (where[1] ^ mz) * plan.inner + (where[2] ^ mi)
            mat[aligned(shard, rows), :] = piece[mz * rows : (mz + 1) * rows, :]
    result = jnp.dot(att[...], mat[...], preferred_element_type=jnp.float32)
    result = (kept[...].astype(jnp.float32) + result).astype(jnp.bfloat16)
    for side in range(plan.sections):
        for mz in range(plan.windows):
            start = side * plan.shard + mz * plan.half
            outs[mz][side * plan.half : (side + 1) * plan.half, :] = result[
                start : start + plan.half, :
            ]


def place_kernel(plan, where, *refs):
    for mz in range(plan.windows):
        refs[-1][where[1] ^ mz] = refs[mz][...]


def halves_kernel(plan, *refs):
    rows = plan.sections * plan.shard
    for chip_no, piece in enumerate(refs[:-1]):
        refs[-1][chip_no * rows : (chip_no + 1) * rows, :] = piece[rows:, :]


def plane_body(latents, norm_gain, qkv_weight, proj_weight, merge_weight):
    plan = Plan(
        lax.axis_size("section"), lax.axis_size("seq"), latents.shape[0], *latents.shape[1:]
    )
    windows, inner, shard, cols = (plan.windows, plan.inner, plan.shard, plan.cols)
    section = lax.axis_index("section")
    position = lax.axis_index("seq")
    window, place = (position // inner, position % inner)
    lane = lax.iota(jnp.int32, 3)
    where = jnp.where(lane == 0, section, jnp.where(lane == 1, window, place)).astype(jnp.int32)
    devices = plan.sections * plan.seq_count
    bf16 = jnp.bfloat16
    smem = pl.BlockSpec(memory_space=pltpu.SMEM)
    hbm = pl.BlockSpec(memory_space=pltpu.HBM)
    vmem = pl.BlockSpec(memory_space=pltpu.VMEM)
    tokens, features, width = (plan.tokens, plan.features, plan.half_cols)

    def swap(value, mask):
        pairs = [(source, source ^ mask) for source in range(devices)]
        return lax.ppermute(value, ("section", "seq"), pairs)

    def call(kernel, outs, ins, scratch=(), specs=None, flops=0, limit=40):
        shapes = tuple(jax.ShapeDtypeStruct(shape, bf16) for shape in outs)
        moved = sum(2 * value.size for value in ins)
        return pl.pallas_call(
            kernel,
            out_shape=shapes,
            in_specs=specs or [vmem] * len(ins),
            out_specs=tuple(vmem for _ in shapes),
            scratch_shapes=list(scratch),
            cost_estimate=pl.CostEstimate(
                flops=flops, bytes_accessed=moved, transcendentals=0
            ),
            compiler_params=pltpu.CompilerParams(vmem_limit_bytes=limit << 20),
        )(*ins)

    def stack(pieces):
        rows = sum(piece.shape[0] for piece in pieces)
        return call(stack_kernel, [(rows, pieces[0].shape[1])], pieces, limit=8)[0]

    def z_gather(value):
        pieces = [value]
        for mz in range(1, windows):
            low = mz & -mz
            pieces.append(swap(pieces[mz - low], plan.mask(mz=low)))
        return pieces

    def chip_gather(value):
        return [value] + [
            swap(value, plan.mask(mx=mx, mi=mi))
            for chip_no, (mx, mi) in enumerate(plan.chips)
            if chip_no
        ]

    def core_gather(pieces):
        return pieces + [swap(piece, plan.mask(mi=1)) for piece in pieces]

    prepared = call(
        lambda *refs: prepare_kernel(plan, *refs),
        [(plan.half, features)] * windows
        + [(len(plan.chips), plan.w_rows, 3 * cols)] * 2
        + [(2 * plan.w_rows, width)],
        [where, latents, norm_gain, qkv_weight, proj_weight, merge_weight],
        [
            pltpu.VMEM((3, plan.w_rows, features), bf16),
            pltpu.SemaphoreType.DMA((5 + windows,)),
        ],
        [smem, hbm, vmem, hbm, hbm, hbm],
        limit=8,
    )
    shares, (keep, give, cross) = (prepared[:windows], prepared[windows:])
    given = swap(give, plan.mask(mi=1))
    shares = [shares[0]] + [swap(shares[mz], plan.mask(mz=mz)) for mz in range(1, windows)]
    outgoing = call(
        lambda *refs: pair_kernel(plan, *refs),
        [
            (2 * plan.w_rows, 3 * cols + (width if chip == (1, 0) else 0))
            for chip in plan.chips
        ],
        [keep, given, cross],
        limit=8,
    )
    incoming = [outgoing[0]] + [
        swap(outgoing[chip_no], plan.mask(mx=mx, mi=mi))
        for chip_no, (mx, mi) in enumerate(plan.chips)
        if chip_no
    ]
    hidden = chip_gather(stack(shares))
    hidden = core_gather(hidden)
    rows_a, rows_b, mats = call(
        lambda *refs: sort_kernel(plan, *refs),
        [
            (plan.group, 3 * cols),
            (plan.group, 3 * cols + width // inner),
            (plan.w_rows, 2 * width),
        ],
        [where, proj_weight, merge_weight] + incoming,
        (),
        [smem] + [vmem] * (2 + len(incoming)),
        limit=8,
    )
    mats = z_gather(mats)
    pieces_a = z_gather(rows_a)
    pieces_b = z_gather(rows_b)
    mats = chip_gather(stack(mats))

    (attended,) = call(
        lambda *refs: first_kernel(plan, *refs),
        [(tokens, cols)],
        [where] + hidden + pieces_a,
        [
            pltpu.VMEM((features, 3 * cols), bf16),
            pltpu.VMEM((tokens, features), bf16),
            pltpu.VMEM((tokens, 3 * cols), bf16),
        ],
        [smem] + [vmem] * (len(hidden) + windows),
        flops=10_000_000_000,
    )
    attended = core_gather(chip_gather(attended))
    mats = core_gather(mats)
    (last,) = call(lambda *refs: last_kernel(plan, *refs), [(plan.group, width)], pieces_b, limit=8)
    last = [last] + [swap(last, plan.mask(mi=mi)) for mi in range(2, inner, 2)]
    last = core_gather(last)
    *attended, kept = call(
        lambda *refs: second_kernel(plan, *refs),
        [(2 * plan.sections * shard, cols)] * (inner // 2) + [(plan.sections * shard, width)],
        [where] + hidden + attended + mats + pieces_b,
        [
            pltpu.VMEM((tokens, features), bf16),
            pltpu.VMEM((tokens, features), bf16),
            pltpu.VMEM((plan.sections, features, 2 * width), bf16),
            pltpu.VMEM((features, 3 * cols), bf16),
            pltpu.VMEM((tokens, features), bf16),
            pltpu.VMEM((tokens, 3 * cols), bf16),
            pltpu.VMEM((tokens, cols), bf16),
        ],
        [smem] + [vmem] * (3 * plan.slots + windows),
        flops=18_000_000_000,
    )
    back = [attended[0]] + [
        swap(attended[mi // 2], plan.mask(mx=mx, mi=mi))
        for chip_no, (mx, mi) in enumerate(plan.chips)
        if chip_no
    ]
    (halves,) = call(
        lambda *refs: halves_kernel(plan, *refs),
        [(len(plan.chips) * plan.sections * shard, cols)],
        back,
        limit=8,
    )
    swapped = swap(halves, plan.mask(mi=1))
    outcome = call(
        lambda *refs: third_kernel(plan, *refs),
        [(plan.tok_rows, width)] * windows,
        [where, kept] + back + [swapped] + last,
        [
            pltpu.VMEM((plan.sections * shard, features), bf16),
            pltpu.VMEM((features, width), bf16),
        ],
        [smem] + [vmem] * (2 + len(back) + inner),
        flops=1_000_000_000,
        limit=16,
    )
    outcome = [outcome[0]] + [swap(outcome[mz], plan.mask(mz=mz)) for mz in range(1, windows)]
    return call(
        lambda *refs: place_kernel(plan, *refs),
        [(windows, plan.tok_rows, width)],
        [where] + outcome,
        (),
        [smem] + [vmem] * windows,
        limit=8,
    )[0]


def solution(mesh):
    placed = (
        P(None, "seq", None),
        P("section", None),
        P("section", "seq", None),
        P("section", "seq", None),
        P("section", "seq", None),
    )

    def plane_step(*arguments):
        return plane_body(*arguments)

    def step(latents, *weights):
        sizes = (
            mesh.shape["section"],
            mesh.shape["seq"],
            latents.shape[0],
            latents.shape[1] // mesh.shape["seq"],
            latents.shape[2],
        )
        fits = Plan.fits(*sizes)
        mapped = jax.shard_map(
            plane_step if fits else body,
            mesh=mesh,
            in_specs=placed,
            out_specs=P(None, "seq", "section"),
            check_vma=False,
        )
        return mapped(latents, *weights)

    return step
```

```python
import jax
import jax.numpy as jnp
from jax import lax
from jax.experimental import pallas as pl
from jax.experimental.pallas import tpu as pltpu
from jax.sharding import PartitionSpec as P

HEADS = 16
HEAD_DIM = 64


EPSILON = 1e-05


def partner(value, axis, bit):
    mask = 2**bit
    pairs = [(source, source ^ mask) for source in range(lax.axis_size(axis))]
    return lax.ppermute(value, axis, pairs)


def shifted(value, axis, steps):
    count = lax.axis_size(axis)
    initial, last = (max(0, -steps), min(count, count - steps))
    return lax.ppermute(value, axis, [(source, source + steps) for source in range(initial, last)])


def layer_norm(hidden, gain_row):
    values = hidden.astype(jnp.float32)
    center = values - jnp.mean(values, axis=-1, keepdims=True)
    spread = jnp.mean(center * center, axis=-1, keepdims=True)
    return (center * lax.rsqrt(spread + EPSILON) * gain_row).astype(jnp.bfloat16)


def body(latents, norm_gain, qkv_weight, proj_weight, merge_weight):
    seq_count = lax.axis_size("seq")
    section_count = lax.axis_size("section")
    my_section = lax.axis_index("section")
    midpoint = section_count // 2
    windows = latents.shape[0]
    tok_rows = latents.shape[1]
    features = latents.shape[2]
    repeat = max(seq_count // HEADS, 1)
    groups = seq_count // repeat
    head_cols = features * repeat // seq_count
    per_device = head_cols // HEAD_DIM
    part_rows = tok_rows // repeat
    scale_factor = HEAD_DIM ** (-0.5)
    w_qkv, w_proj, w_merge = (
        lax.all_gather(qkv_weight, "seq", axis=1, tiled=True),
        lax.all_gather(proj_weight, "seq", axis=1, tiled=True),
        lax.all_gather(merge_weight, "seq", axis=1, tiled=True),
    )
    w_qkv = w_qkv[0]
    w_proj = w_proj[0]
    w_merge = w_merge[0]
    gain_row = norm_gain[0]
    decoder = my_section >= midpoint
    encoder = my_section < midpoint
    query_shape = (seq_count, part_rows * head_cols)
    key_shape = (seq_count, tok_rows * head_cols)

    def to_heads(array_in, spread_copies):
        if spread_copies:
            grouped = array_in.reshape(tok_rows, groups, head_cols).transpose(1, 0, 2)
            grouped = grouped.reshape(groups, 1, tok_rows * head_cols)
            grouped = jnp.broadcast_to(grouped, (groups, repeat, tok_rows * head_cols))
            return grouped.reshape(seq_count, tok_rows * head_cols)
        grouped = array_in.reshape(part_rows, repeat, groups, head_cols).transpose(2, 1, 0, 3)
        return grouped.reshape(seq_count, part_rows * head_cols)

    def from_heads(array_in):
        grouped = array_in.reshape(groups, repeat, part_rows, head_cols).transpose(2, 1, 0, 3)
        return grouped.reshape(tok_rows, features)

    def project(carried):
        normed = layer_norm(carried, gain_row)
        packed = jnp.dot(normed, w_qkv, preferred_element_type=jnp.float32).astype(jnp.bfloat16)
        return (
            to_heads(packed[:, :features], False),
            to_heads(packed[:, features : 2 * features], True),
            to_heads(packed[:, 2 * features :], True),
        )

    def spare_heads():
        return (
            jnp.zeros(query_shape, jnp.bfloat16),
            jnp.zeros(key_shape, jnp.bfloat16),
            jnp.zeros(key_shape, jnp.bfloat16),
        )

    def attend(queries, keys_in, values_in):
        query_rows = queries.reshape(-1, per_device, HEAD_DIM)
        key_rows = keys_in.reshape(-1, per_device, HEAD_DIM)
        value_rows = values_in.reshape(-1, per_device, HEAD_DIM)
        block_rows = min(512, query_rows.shape[0])
        blocked = query_rows.reshape(-1, block_rows, per_device, HEAD_DIM)

        def one_block(query_block):
            scores = (
                jnp.einsum(
                    "qhd,khd->hqk", query_block, key_rows, preferred_element_type=jnp.float32
                )
                * scale_factor
            )
            row_max = jnp.max(scores, axis=-1, keepdims=True)
            weights = jnp.exp(scores - row_max)
            totals = jnp.sum(weights, axis=-1)
            probs = weights.astype(jnp.bfloat16)
            mixed = jnp.einsum(
                "hqk,khd->qhd", probs, value_rows, preferred_element_type=jnp.float32
            )
            return (mixed / totals.T[:, :, None]).astype(jnp.bfloat16)

        return lax.map(one_block, blocked).reshape(query_shape)

    def mirror_each(skip_term):
        for bit_no in range(section_count.bit_length() - 1):
            skip_term = partner(skip_term, "section", bit_no)
        return skip_term

    def tick(tick_no, loop_state):
        incoming, skip_store, result = loop_state
        window_no = tick_no - my_section
        active = (window_no >= 0) & (window_no < windows)
        chosen = jnp.clip(window_no, 0, windows - 1)
        fresh = lax.dynamic_index_in_dim(latents, chosen, 0, keepdims=False)
        entering = jnp.where(my_section == 0, fresh, incoming)
        skip_slot = lax.dynamic_index_in_dim(skip_store, chosen, 0, keepdims=False)
        carried = lax.cond(
            active & decoder,
            lambda: (
                jnp.dot(entering, w_merge, preferred_element_type=jnp.float32)
                + skip_slot.astype(jnp.float32)
            ).astype(jnp.bfloat16),
            lambda: entering,
        )
        queries, keys_in, values_in = lax.cond(active, lambda: project(carried), spare_heads)
        queries, keys_in, values_in = (
            lax.all_to_all(queries, "seq", split_axis=0, concat_axis=0, tiled=True),
            lax.all_to_all(keys_in, "seq", split_axis=0, concat_axis=0, tiled=True),
            lax.all_to_all(values_in, "seq", split_axis=0, concat_axis=0, tiled=True),
        )
        attended = lax.cond(
            active,
            lambda: attend(queries, keys_in, values_in),
            lambda: jnp.zeros(query_shape, jnp.bfloat16),
        )
        attended = lax.all_to_all(attended, "seq", split_axis=0, concat_axis=0, tiled=True)
        leaving = lax.cond(
            active,
            lambda: (
                carried.astype(jnp.float32)
                + jnp.dot(from_heads(attended), w_proj, preferred_element_type=jnp.float32)
            ).astype(jnp.bfloat16),
            lambda: carried,
        )
        skip_term = lax.cond(
            active & encoder,
            lambda: jnp.dot(leaving, w_merge, preferred_element_type=jnp.float32).astype(
                jnp.bfloat16
            ),
            lambda: jnp.zeros_like(leaving),
        )
        arrived = mirror_each(skip_term)
        source_no = tick_no - (section_count - 1 - my_section)
        landing = decoder & (source_no >= 0) & (source_no < windows)
        target = jnp.clip(source_no, 0, windows - 1)
        updated = lax.dynamic_update_index_in_dim(skip_store, arrived, target, 0)
        skip_store = jnp.where(landing, updated, skip_store)
        incoming = shifted(leaving, "section", 1)
        finished = lax.dynamic_update_index_in_dim(result, leaving.astype(jnp.float32), chosen, 0)
        result = jnp.where(active & (my_section == section_count - 1), finished, result)
        return (incoming, skip_store, result)

    loop_state = (
        jnp.zeros(latents.shape[1:], jnp.bfloat16),
        jnp.zeros_like(latents),
        jnp.zeros(latents.shape, jnp.float32),
    )
    loop_state = lax.fori_loop(0, windows + section_count - 1, tick, loop_state)
    result = loop_state[2]
    return lax.psum_scatter(result.astype(jnp.bfloat16), "section", scatter_dimension=2, tiled=True)


class Plan:
    def __init__(self, sections, seq_count, windows, tok_rows, features):
        self.sections = sections
        self.seq_count = seq_count
        self.windows = windows
        self.tok_rows = tok_rows
        self.features = features
        self.inner = seq_count // windows
        self.slots = sections * self.inner
        self.half = tok_rows // sections
        self.shard = windows * self.half
        self.tokens = self.slots * self.shard
        self.cols = features // self.slots
        self.half_cols = features // sections
        self.w_rows = features // seq_count
        self.group = self.inner * self.w_rows
        self.chips = [(mx, mi) for mx in range(sections) for mi in range(0, self.inner, 2)]

    @staticmethod
    def fits(sections, seq_count, windows, tok_rows, features):
        if sections != 2 or windows & (windows - 1) or seq_count % (2 * windows):
            return False
        inner = seq_count // windows
        if inner & (inner - 1) or features % (sections * inner * 2 * HEAD_DIM):
            return False
        return features == HEADS * HEAD_DIM and tok_rows % 32 == 0

    def mask(self, mx=0, mz=0, mi=0):
        return mx * self.seq_count + mz * self.inner + mi


def attention(qkv, out, cols, rows_q):
    tokens = qkv.shape[0]
    lane_head = lax.broadcasted_iota(jnp.int32, (1, cols), 1) // HEAD_DIM

    def one_block(block_no, carry):
        rows = pl.ds(pl.multiple_of(block_no * rows_q, rows_q), rows_q)
        query = qkv[rows, 0:cols]
        keys_in = qkv[:, cols : 2 * cols]
        values_in = qkv[:, 2 * cols : 3 * cols]
        mixed = jnp.zeros((rows_q, cols), jnp.float32)
        for head in range(cols // HEAD_DIM):
            mine = lane_head == head
            picked = jnp.where(mine, query, jnp.zeros_like(query))
            scores = lax.dot_general(
                picked, keys_in, (((1,), (1,)), ((), ())), preferred_element_type=jnp.float32
            )
            row_max = jnp.max(scores, axis=-1, keepdims=True)
            weights = jnp.exp(scores - row_max)
            totals = jnp.sum(weights, axis=-1, keepdims=True)
            part = jnp.dot(
                weights.astype(jnp.bfloat16), values_in, preferred_element_type=jnp.float32
            )
            mixed = jnp.where(mine, part / totals, mixed)
        out[rows, :] = mixed.astype(jnp.bfloat16)
        return carry

    lax.fori_loop(0, tokens // rows_q, one_block, 0)


def project_rows(normed, w_qkv, cols):
    packed = jnp.dot(normed, w_qkv, preferred_element_type=jnp.float32)
    lane = lax.broadcasted_iota(jnp.int32, (1, packed.shape[1]), 1)
    packed = packed.astype(jnp.bfloat16)
    return jnp.where(lane < cols, packed * jnp.bfloat16(HEAD_DIM ** (-0.5)), packed)


def slot_of(plan, where, mx, mi):
    return (where[0] ^ mx) * plan.inner + (where[2] ^ mi)


def aligned(index, size):
    return pl.ds(pl.multiple_of(index * size, size), size)


def prepare_kernel(plan, where, latents, gain, qkv_weight, proj_weight, merge_weight, *rest):
    shares = rest[: plan.windows]
    keep, give, cross, held, sems = rest[plan.windows :]
    copies = []

    def add(source, target):
        copies.append(pltpu.make_async_copy(source, target, sems.at[len(copies)]))

    for part in range(3):
        add(
            qkv_weight.at[0, :, part * plan.features : (part + 1) * plan.features],
            held.at[part],
        )
    width, rows = (plan.half_cols, plan.w_rows)
    for part, matrix in enumerate((proj_weight, merge_weight)):
        add(
            matrix.at[0, :, aligned(where[0] ^ 1, width)],
            cross.at[part * rows : (part + 1) * rows, :],
        )
    for mz in range(plan.windows):
        add(latents.at[where[1] ^ mz, aligned(where[0], plan.half), :], shares[mz])
    for copy in copies:
        copy.start()
    first_row = (where[1] * plan.inner + where[2]) * rows
    row = first_row + lax.broadcasted_iota(jnp.int32, (rows, plan.features), 0)
    lane = lax.broadcasted_iota(jnp.int32, (rows, plan.features), 1)
    factors = jnp.where(row == lane, gain[...], jnp.zeros((1, plan.features), jnp.float32))
    factors = jnp.sum(factors, axis=1, keepdims=True)
    for copy in copies[:3]:
        copy.wait()
    for core, target in ((1, give), (0, keep)):
        for chip_no, (mx, mi) in enumerate(plan.chips):
            lanes = aligned(slot_of(plan, where, mx, mi ^ core), plan.cols)
            for part in range(3):
                scaled = held[part, :, lanes].astype(jnp.float32) * factors
                target[chip_no, :, part * plan.cols : (part + 1) * plan.cols] = scaled.astype(
                    jnp.bfloat16
                )
    for copy in copies[3:]:
        copy.wait()


def pair_kernel(plan, keep, given, *outs):
    rows = plan.w_rows
    for chip_no, out in enumerate(outs):
        out[0:rows, :] = keep[chip_no]
        out[rows:, :] = given[chip_no]


def merge_kernel(plan, where, proj_weight, merge_weight, crossed, mats, last):
    rows, width = (plan.w_rows, plan.half_cols)
    for section in range(plan.sections):

        @pl.when(where[0] == section)
        def _():
            lanes = slice(section * width, (section + 1) * width)
            mine = proj_weight[0, :, lanes]
            others = crossed[0:rows, :]
            mats[:, 0:width] = mine if section == 0 else others
            last[...] = others if section == 0 else mine
            total = merge_weight[0, :, lanes].astype(jnp.float32)
            total = total + crossed[rows:, :].astype(jnp.float32)
            mats[:, width:] = total.astype(jnp.bfloat16)


def sort_kernel(plan, where, last, *refs):
    count = len(plan.chips)
    pieces, (rows_a, rows_b) = (refs[:count], refs[count:])
    rows, cols = (plan.w_rows, 3 * plan.cols)
    lone = plan.half_cols // plan.inner
    for section in range(plan.sections):

        @pl.when(where[0] == section)
        def _():
            outs = (rows_a, rows_b)
            for piece, (mx, mi) in zip(pieces, plan.chips):
                part = slice(mi * rows, (mi + 2) * rows)
                outs[section ^ mx][part, 0:cols] = piece[...]

    for mi in range(plan.inner):
        rows_b[mi * rows : (mi + 1) * rows, cols:] = last[:, mi * lone : (mi + 1) * lone]


def last_kernel(plan, *refs):
    rows, lone = (plan.w_rows, plan.half_cols // plan.inner)
    for mz, piece in enumerate(refs[:-1]):
        for mi in range(plan.inner):
            refs[-1][mz * rows : (mz + 1) * rows, mi * lone : (mi + 1) * lone] = piece[
                mi * rows : (mi + 1) * rows, 3 * plan.cols :
            ]


def stack_kernel(*refs):
    start = 0
    for piece in refs[:-1]:
        rows = piece.shape[0]
        refs[-1][start : start + rows, :] = piece[...]
        start += rows


def gather_weights(plan, where, pieces, target):
    rows = plan.w_rows
    for mz, piece in enumerate(pieces):
        for mi in range(plan.inner):
            shard = (where[1] ^ mz) * plan.inner + (where[2] ^ mi)
            target[aligned(shard, rows), :] = piece[
                mi * rows : (mi + 1) * rows, 0 : 3 * plan.cols
            ]


def plane_order(plan):
    return [(mx, mi ^ core) for core in range(2) for mx, mi in plan.chips]


def normalize(values):
    center = values - jnp.mean(values, axis=-1, keepdims=True)
    spread = jnp.mean(center * center, axis=-1, keepdims=True)
    return (center * lax.rsqrt(spread + EPSILON)).astype(jnp.bfloat16)


def row_blocks(plan, one_block):
    size = min(512, plan.tokens)

    def step(block_no, carry):
        one_block(aligned(block_no, size))
        return carry

    lax.fori_loop(0, plan.tokens // size, step, 0)


def first_kernel(plan, where, *rest):
    hidden_in = rest[: plan.slots]
    pieces = rest[plan.slots : plan.slots + plan.windows]
    out, w_qkv, normed, qkv = rest[plan.slots + plan.windows :]
    gather_weights(plan, where, pieces, w_qkv)
    for piece, (mx, mi) in zip(hidden_in, plane_order(plan)):
        rows = aligned(slot_of(plan, where, mx, mi), plan.shard)
        normed[rows, :] = normalize(piece[...].astype(jnp.float32))

    def one_block(rows):
        qkv[rows, :] = project_rows(normed[rows, :], w_qkv[...], plan.cols)

    row_blocks(plan, one_block)
    attention(qkv, out, plan.cols, min(256, plan.tokens))


def second_kernel(plan, where, *rest):
    slots, windows = (plan.slots, plan.windows)
    hidden_in, rest = (rest[:slots], rest[slots:])
    attended_in, rest = (rest[:slots], rest[slots:])
    mats_in, rest = (rest[:slots], rest[slots:])
    pieces, rest = (rest[:windows], rest[windows:])
    outs, rest = (rest[: plan.inner // 2], rest[plan.inner // 2 :])
    kept, hid, att, mats, w_qkv, joined, qkv, mixed = rest
    order = plane_order(plan)
    for piece, (mx, mi) in zip(hidden_in, order):
        hid[aligned(slot_of(plan, where, mx, mi), plan.shard), :] = piece[...]
    for piece, (mx, mi) in zip(attended_in, order):
        att[:, aligned(slot_of(plan, where, mx, mi), plan.cols)] = piece[...]
    rows = plan.w_rows
    for piece, (mx, mi) in zip(mats_in, order):
        for mz in range(windows):
            shard = (where[1] ^ mz) * plan.inner + (where[2] ^ mi)
            mats[where[0] ^ mx, aligned(shard, rows), :] = piece[mz * rows : (mz + 1) * rows, :]
    gather_weights(plan, where, pieces, w_qkv)
    width = plan.half_cols

    def one_block(part):
        attended = att[part, :]
        hidden = jnp.concatenate(
            [
                jnp.dot(attended, mats[side, :, 0:width], preferred_element_type=jnp.float32)
                for side in range(plan.sections)
            ],
            axis=1,
        )
        hidden = (hid[part, :].astype(jnp.float32) + hidden).astype(jnp.bfloat16)
        merged = jnp.concatenate(
            [
                jnp.dot(hidden, mats[side, :, width:], preferred_element_type=jnp.float32)
                for side in range(plan.sections)
            ],
            axis=1,
        )
        merged = merged.astype(jnp.bfloat16)
        joined[part, :] = merged
        qkv[part, :] = project_rows(
            normalize(merged.astype(jnp.float32)), w_qkv[...], plan.cols
        )

    row_blocks(plan, one_block)
    attention(qkv, mixed, plan.cols, min(256, plan.tokens))
    lanes = aligned(where[0], width)
    for side in range(plan.sections):
        for mi in range(plan.inner):
            part = aligned(side * plan.inner + (where[2] ^ mi), plan.shard)
            start = ((mi % 2) * plan.sections + side) * plan.shard
            outs[mi // 2][start : start + plan.shard, :] = mixed[part, :]
            if mi == 0:
                kept[side * plan.shard : (side + 1) * plan.shard, :] = joined[part, lanes]


def third_kernel(plan, where, kept, *rest):
    chips, rest = (rest[: len(plan.chips)], rest[len(plan.chips) :])
    swapped, mats_in = (rest[0], rest[1 : 1 + plan.inner])
    outs, (att, mat) = (rest[1 + plan.inner : -2], rest[-2:])
    rows = plan.sections * plan.shard
    for chip_no, (mx, mi) in enumerate(plan.chips):
        for core in range(2):
            lanes = aligned(slot_of(plan, where, mx, mi ^ core), plan.cols)
            if core == 0:
                att[:, lanes] = chips[chip_no][0:rows, :]
            else:
                att[:, lanes] = swapped[chip_no * rows : (chip_no + 1) * rows, :]
    rows = plan.w_rows
    order = [mi ^ core for core in range(2) for mi in range(0, plan.inner, 2)]
    for piece, mi in zip(mats_in, order):
        for mz in range(plan.windows):
            shard = (where[1] ^ mz) * plan.inner + (where[2] ^ mi)
            mat[aligned(shard, rows), :] = piece[mz * rows : (mz + 1) * rows, :]
    result = jnp.dot(att[...], mat[...], preferred_element_type=jnp.float32)
    result = (kept[...].astype(jnp.float32) + result).astype(jnp.bfloat16)
    for side in range(plan.sections):
        for mz in range(plan.windows):
            start = side * plan.shard + mz * plan.half
            outs[mz][side * plan.half : (side + 1) * plan.half, :] = result[
                start : start + plan.half, :
            ]


def place_kernel(plan, where, *refs):
    for mz in range(plan.windows):
        refs[-1][where[1] ^ mz] = refs[mz][...]


def halves_kernel(plan, *refs):
    rows = plan.sections * plan.shard
    for chip_no, piece in enumerate(refs[:-1]):
        refs[-1][chip_no * rows : (chip_no + 1) * rows, :] = piece[rows:, :]


def plane_body(latents, norm_gain, qkv_weight, proj_weight, merge_weight):
    plan = Plan(
        lax.axis_size("section"), lax.axis_size("seq"), latents.shape[0], *latents.shape[1:]
    )
    windows, inner, shard, cols = (plan.windows, plan.inner, plan.shard, plan.cols)
    section = lax.axis_index("section")
    position = lax.axis_index("seq")
    window, place = (position // inner, position % inner)
    lane = lax.iota(jnp.int32, 3)
    where = jnp.where(lane == 0, section, jnp.where(lane == 1, window, place)).astype(jnp.int32)
    devices = plan.sections * plan.seq_count
    bf16 = jnp.bfloat16
    smem = pl.BlockSpec(memory_space=pltpu.SMEM)
    hbm = pl.BlockSpec(memory_space=pltpu.HBM)
    vmem = pl.BlockSpec(memory_space=pltpu.VMEM)
    tokens, features, width = (plan.tokens, plan.features, plan.half_cols)

    def swap(value, mask):
        pairs = [(source, source ^ mask) for source in range(devices)]
        return lax.ppermute(value, ("section", "seq"), pairs)

    def call(kernel, outs, ins, scratch=(), specs=None, flops=0, limit=40):
        shapes = tuple(jax.ShapeDtypeStruct(shape, bf16) for shape in outs)
        moved = sum(2 * value.size for value in ins)
        return pl.pallas_call(
            kernel,
            out_shape=shapes,
            in_specs=specs or [vmem] * len(ins),
            out_specs=tuple(vmem for _ in shapes),
            scratch_shapes=list(scratch),
            cost_estimate=pl.CostEstimate(
                flops=flops, bytes_accessed=moved, transcendentals=0
            ),
            compiler_params=pltpu.CompilerParams(vmem_limit_bytes=limit << 20),
        )(*ins)

    def stack(pieces):
        rows = sum(piece.shape[0] for piece in pieces)
        return call(stack_kernel, [(rows, pieces[0].shape[1])], pieces, limit=8)[0]

    def z_gather(value):
        pieces = [value]
        for mz in range(1, windows):
            low = mz & -mz
            pieces.append(swap(pieces[mz - low], plan.mask(mz=low)))
        return pieces

    def chip_gather(value):
        return [value] + [
            swap(value, plan.mask(mx=mx, mi=mi))
            for chip_no, (mx, mi) in enumerate(plan.chips)
            if chip_no
        ]

    def core_gather(pieces):
        return pieces + [swap(piece, plan.mask(mi=1)) for piece in pieces]

    latents, qkv_weight, proj_weight, merge_weight = (
        pltpu.with_memory_space_constraint(value, pltpu.HBM)
        for value in (latents, qkv_weight, proj_weight, merge_weight)
    )
    prepared = call(
        lambda *refs: prepare_kernel(plan, *refs),
        [(plan.half, features)] * windows
        + [(len(plan.chips), plan.w_rows, 3 * cols)] * 2
        + [(2 * plan.w_rows, width)],
        [where, latents, norm_gain, qkv_weight, proj_weight, merge_weight],
        [
            pltpu.VMEM((3, plan.w_rows, features), bf16),
            pltpu.SemaphoreType.DMA((5 + windows,)),
        ],
        [smem, hbm, vmem, hbm, hbm, hbm],
        limit=8,
    )
    shares, (keep, give, cross) = (prepared[:windows], prepared[windows:])
    given = swap(give, plan.mask(mi=1))
    crossed = swap(cross, plan.mask(mx=1))
    shares = [shares[0]] + [swap(shares[mz], plan.mask(mz=mz)) for mz in range(1, windows)]
    outgoing = call(
        lambda *refs: pair_kernel(plan, *refs),
        [(2 * plan.w_rows, 3 * cols)] * len(plan.chips),
        [keep, given],
        limit=8,
    )
    incoming = [outgoing[0]] + [
        swap(outgoing[chip_no], plan.mask(mx=mx, mi=mi))
        for chip_no, (mx, mi) in enumerate(plan.chips)
        if chip_no
    ]
    hidden = chip_gather(stack(shares))
    hidden = core_gather(hidden)
    mats, last = call(
        lambda *refs: merge_kernel(plan, *refs),
        [(plan.w_rows, 2 * width), (plan.w_rows, width)],
        [where, proj_weight, merge_weight, crossed],
        (),
        [smem] + [vmem] * 3,
        limit=8,
    )
    rows_a, rows_b = call(
        lambda *refs: sort_kernel(plan, *refs),
        [
            (plan.group, 3 * cols),
            (plan.group, 3 * cols + width // inner),
        ],
        [where, last] + incoming,
        (),
        [smem] + [vmem] * (1 + len(incoming)),
        limit=8,
    )
    mats = z_gather(mats)
    pieces_a = z_gather(rows_a)
    pieces_b = z_gather(rows_b)
    mats = chip_gather(stack(mats))

    (attended,) = call(
        lambda *refs: first_kernel(plan, *refs),
        [(tokens, cols)],
        [where] + hidden + pieces_a,
        [
            pltpu.VMEM((features, 3 * cols), bf16),
            pltpu.VMEM((tokens, features), bf16),
            pltpu.VMEM((tokens, 3 * cols), bf16),
        ],
        [smem] + [vmem] * (len(hidden) + windows),
        flops=10_000_000_000,
    )
    attended = core_gather(chip_gather(attended))
    mats = core_gather(mats)
    (last,) = call(lambda *refs: last_kernel(plan, *refs), [(plan.group, width)], pieces_b, limit=8)
    last = [last] + [swap(last, plan.mask(mi=mi)) for mi in range(2, inner, 2)]
    last = core_gather(last)
    *attended, kept = call(
        lambda *refs: second_kernel(plan, *refs),
        [(2 * plan.sections * shard, cols)] * (inner // 2) + [(plan.sections * shard, width)],
        [where] + hidden + attended + mats + pieces_b,
        [
            pltpu.VMEM((tokens, features), bf16),
            pltpu.VMEM((tokens, features), bf16),
            pltpu.VMEM((plan.sections, features, 2 * width), bf16),
            pltpu.VMEM((features, 3 * cols), bf16),
            pltpu.VMEM((tokens, features), bf16),
            pltpu.VMEM((tokens, 3 * cols), bf16),
            pltpu.VMEM((tokens, cols), bf16),
        ],
        [smem] + [vmem] * (3 * plan.slots + windows),
        flops=18_000_000_000,
    )
    back = [attended[0]] + [
        swap(attended[mi // 2], plan.mask(mx=mx, mi=mi))
        for chip_no, (mx, mi) in enumerate(plan.chips)
        if chip_no
    ]
    (halves,) = call(
        lambda *refs: halves_kernel(plan, *refs),
        [(len(plan.chips) * plan.sections * shard, cols)],
        back,
        limit=8,
    )
    swapped = swap(halves, plan.mask(mi=1))
    outcome = call(
        lambda *refs: third_kernel(plan, *refs),
        [(plan.tok_rows, width)] * windows,
        [where, kept] + back + [swapped] + last,
        [
            pltpu.VMEM((plan.sections * shard, features), bf16),
            pltpu.VMEM((features, width), bf16),
        ],
        [smem] + [vmem] * (2 + len(back) + inner),
        flops=1_000_000_000,
        limit=16,
    )
    outcome = [outcome[0]] + [swap(outcome[mz], plan.mask(mz=mz)) for mz in range(1, windows)]
    return call(
        lambda *refs: place_kernel(plan, *refs),
        [(windows, plan.tok_rows, width)],
        [where] + outcome,
        (),
        [smem] + [vmem] * windows,
        limit=8,
    )[0]


def solution(mesh):
    placed = (
        P(None, "seq", None),
        P("section", None),
        P("section", "seq", None),
        P("section", "seq", None),
        P("section", "seq", None),
    )

    def plane_step(*arguments):
        return plane_body(*arguments)

    def step(latents, *weights):
        sizes = (
            mesh.shape["section"],
            mesh.shape["seq"],
            latents.shape[0],
            latents.shape[1] // mesh.shape["seq"],
            latents.shape[2],
        )
        fits = Plan.fits(*sizes)
        mapped = jax.shard_map(
            plane_step if fits else body,
            mesh=mesh,
            in_specs=placed,
            out_specs=P(None, "seq", "section"),
            check_vma=False,
        )
        return mapped(latents, *weights)

    return step
```

```python
import jax
import jax.numpy as jnp
from jax import lax
from jax.experimental import pallas as pl
from jax.experimental.pallas import tpu as pltpu
from jax.sharding import PartitionSpec as P

HEADS = 16
HEAD_DIM = 64


EPSILON = 1e-05


def partner(value, axis, bit):
    mask = 2**bit
    pairs = [(source, source ^ mask) for source in range(lax.axis_size(axis))]
    return lax.ppermute(value, axis, pairs)


def shifted(value, axis, steps):
    count = lax.axis_size(axis)
    initial, last = (max(0, -steps), min(count, count - steps))
    return lax.ppermute(value, axis, [(source, source + steps) for source in range(initial, last)])


def layer_norm(hidden, gain_row):
    values = hidden.astype(jnp.float32)
    center = values - jnp.mean(values, axis=-1, keepdims=True)
    spread = jnp.mean(center * center, axis=-1, keepdims=True)
    return (center * lax.rsqrt(spread + EPSILON) * gain_row).astype(jnp.bfloat16)


def body(latents, norm_gain, qkv_weight, proj_weight, merge_weight):
    seq_count = lax.axis_size("seq")
    section_count = lax.axis_size("section")
    my_section = lax.axis_index("section")
    midpoint = section_count // 2
    windows = latents.shape[0]
    tok_rows = latents.shape[1]
    features = latents.shape[2]
    repeat = max(seq_count // HEADS, 1)
    groups = seq_count // repeat
    head_cols = features * repeat // seq_count
    per_device = head_cols // HEAD_DIM
    part_rows = tok_rows // repeat
    scale_factor = HEAD_DIM ** (-0.5)
    w_qkv, w_proj, w_merge = (
        lax.all_gather(qkv_weight, "seq", axis=1, tiled=True),
        lax.all_gather(proj_weight, "seq", axis=1, tiled=True),
        lax.all_gather(merge_weight, "seq", axis=1, tiled=True),
    )
    w_qkv = w_qkv[0]
    w_proj = w_proj[0]
    w_merge = w_merge[0]
    gain_row = norm_gain[0]
    decoder = my_section >= midpoint
    encoder = my_section < midpoint
    query_shape = (seq_count, part_rows * head_cols)
    key_shape = (seq_count, tok_rows * head_cols)

    def to_heads(array_in, spread_copies):
        if spread_copies:
            grouped = array_in.reshape(tok_rows, groups, head_cols).transpose(1, 0, 2)
            grouped = grouped.reshape(groups, 1, tok_rows * head_cols)
            grouped = jnp.broadcast_to(grouped, (groups, repeat, tok_rows * head_cols))
            return grouped.reshape(seq_count, tok_rows * head_cols)
        grouped = array_in.reshape(part_rows, repeat, groups, head_cols).transpose(2, 1, 0, 3)
        return grouped.reshape(seq_count, part_rows * head_cols)

    def from_heads(array_in):
        grouped = array_in.reshape(groups, repeat, part_rows, head_cols).transpose(2, 1, 0, 3)
        return grouped.reshape(tok_rows, features)

    def project(carried):
        normed = layer_norm(carried, gain_row)
        packed = jnp.dot(normed, w_qkv, preferred_element_type=jnp.float32).astype(jnp.bfloat16)
        return (
            to_heads(packed[:, :features], False),
            to_heads(packed[:, features : 2 * features], True),
            to_heads(packed[:, 2 * features :], True),
        )

    def spare_heads():
        return (
            jnp.zeros(query_shape, jnp.bfloat16),
            jnp.zeros(key_shape, jnp.bfloat16),
            jnp.zeros(key_shape, jnp.bfloat16),
        )

    def attend(queries, keys_in, values_in):
        query_rows = queries.reshape(-1, per_device, HEAD_DIM)
        key_rows = keys_in.reshape(-1, per_device, HEAD_DIM)
        value_rows = values_in.reshape(-1, per_device, HEAD_DIM)
        block_rows = min(512, query_rows.shape[0])
        blocked = query_rows.reshape(-1, block_rows, per_device, HEAD_DIM)

        def one_block(query_block):
            scores = (
                jnp.einsum(
                    "qhd,khd->hqk", query_block, key_rows, preferred_element_type=jnp.float32
                )
                * scale_factor
            )
            row_max = jnp.max(scores, axis=-1, keepdims=True)
            weights = jnp.exp(scores - row_max)
            totals = jnp.sum(weights, axis=-1)
            probs = weights.astype(jnp.bfloat16)
            mixed = jnp.einsum(
                "hqk,khd->qhd", probs, value_rows, preferred_element_type=jnp.float32
            )
            return (mixed / totals.T[:, :, None]).astype(jnp.bfloat16)

        return lax.map(one_block, blocked).reshape(query_shape)

    def mirror_each(skip_term):
        for bit_no in range(section_count.bit_length() - 1):
            skip_term = partner(skip_term, "section", bit_no)
        return skip_term

    def tick(tick_no, loop_state):
        incoming, skip_store, result = loop_state
        window_no = tick_no - my_section
        active = (window_no >= 0) & (window_no < windows)
        chosen = jnp.clip(window_no, 0, windows - 1)
        fresh = lax.dynamic_index_in_dim(latents, chosen, 0, keepdims=False)
        entering = jnp.where(my_section == 0, fresh, incoming)
        skip_slot = lax.dynamic_index_in_dim(skip_store, chosen, 0, keepdims=False)
        carried = lax.cond(
            active & decoder,
            lambda: (
                jnp.dot(entering, w_merge, preferred_element_type=jnp.float32)
                + skip_slot.astype(jnp.float32)
            ).astype(jnp.bfloat16),
            lambda: entering,
        )
        queries, keys_in, values_in = lax.cond(active, lambda: project(carried), spare_heads)
        queries, keys_in, values_in = (
            lax.all_to_all(queries, "seq", split_axis=0, concat_axis=0, tiled=True),
            lax.all_to_all(keys_in, "seq", split_axis=0, concat_axis=0, tiled=True),
            lax.all_to_all(values_in, "seq", split_axis=0, concat_axis=0, tiled=True),
        )
        attended = lax.cond(
            active,
            lambda: attend(queries, keys_in, values_in),
            lambda: jnp.zeros(query_shape, jnp.bfloat16),
        )
        attended = lax.all_to_all(attended, "seq", split_axis=0, concat_axis=0, tiled=True)
        leaving = lax.cond(
            active,
            lambda: (
                carried.astype(jnp.float32)
                + jnp.dot(from_heads(attended), w_proj, preferred_element_type=jnp.float32)
            ).astype(jnp.bfloat16),
            lambda: carried,
        )
        skip_term = lax.cond(
            active & encoder,
            lambda: jnp.dot(leaving, w_merge, preferred_element_type=jnp.float32).astype(
                jnp.bfloat16
            ),
            lambda: jnp.zeros_like(leaving),
        )
        arrived = mirror_each(skip_term)
        source_no = tick_no - (section_count - 1 - my_section)
        landing = decoder & (source_no >= 0) & (source_no < windows)
        target = jnp.clip(source_no, 0, windows - 1)
        updated = lax.dynamic_update_index_in_dim(skip_store, arrived, target, 0)
        skip_store = jnp.where(landing, updated, skip_store)
        incoming = shifted(leaving, "section", 1)
        finished = lax.dynamic_update_index_in_dim(result, leaving.astype(jnp.float32), chosen, 0)
        result = jnp.where(active & (my_section == section_count - 1), finished, result)
        return (incoming, skip_store, result)

    loop_state = (
        jnp.zeros(latents.shape[1:], jnp.bfloat16),
        jnp.zeros_like(latents),
        jnp.zeros(latents.shape, jnp.float32),
    )
    loop_state = lax.fori_loop(0, windows + section_count - 1, tick, loop_state)
    result = loop_state[2]
    return lax.psum_scatter(result.astype(jnp.bfloat16), "section", scatter_dimension=2, tiled=True)


class Plan:
    def __init__(self, sections, seq_count, windows, tok_rows, features):
        self.sections = sections
        self.seq_count = seq_count
        self.windows = windows
        self.tok_rows = tok_rows
        self.features = features
        self.inner = seq_count // windows
        self.slots = sections * self.inner
        self.half = tok_rows // sections
        self.shard = windows * self.half
        self.tokens = self.slots * self.shard
        self.cols = features // self.slots
        self.half_cols = features // sections
        self.w_rows = features // seq_count
        self.group = self.inner * self.w_rows
        self.chips = [(mx, mi) for mx in range(sections) for mi in range(0, self.inner, 2)]

    @staticmethod
    def fits(sections, seq_count, windows, tok_rows, features):
        if sections != 2 or windows & (windows - 1) or seq_count % (2 * windows):
            return False
        inner = seq_count // windows
        if inner & (inner - 1) or features % (sections * inner * 2 * HEAD_DIM):
            return False
        return features == HEADS * HEAD_DIM and tok_rows % 32 == 0

    def mask(self, mx=0, mz=0, mi=0):
        return mx * self.seq_count + mz * self.inner + mi


def attention(qkv, out, cols):
    lane_head = lax.broadcasted_iota(jnp.int32, (1, cols), 1) // HEAD_DIM
    queries = qkv[:, 0:cols]
    keys_in = qkv[:, cols : 2 * cols]
    values_in = qkv[:, 2 * cols : 3 * cols]
    mixed = jnp.zeros(queries.shape, jnp.float32)
    for head in range(cols // HEAD_DIM):
        mine = lane_head == head
        picked = jnp.where(mine, queries, jnp.zeros_like(queries))
        scores = lax.dot_general(
            keys_in, picked, (((1,), (1,)), ((), ())), preferred_element_type=jnp.float32
        )
        weights = jnp.exp(scores - jnp.max(scores, axis=0, keepdims=True))
        totals = jnp.sum(weights, axis=0, keepdims=True)
        part = lax.dot_general(
            values_in,
            weights.astype(jnp.bfloat16),
            (((0,), (0,)), ((), ())),
            preferred_element_type=jnp.float32,
        )
        mixed = jnp.where(mine, (part / totals).T, mixed)
    out[...] = mixed.astype(jnp.bfloat16)


def project_rows(normed, w_qkv, cols):
    packed = jnp.dot(normed, w_qkv, preferred_element_type=jnp.float32)
    lane = lax.broadcasted_iota(jnp.int32, (1, packed.shape[1]), 1)
    packed = packed.astype(jnp.bfloat16)
    return jnp.where(lane < cols, packed * jnp.bfloat16(HEAD_DIM ** (-0.5)), packed)


def slot_of(plan, where, mx, mi):
    return (where[0] ^ mx) * plan.inner + (where[2] ^ mi)


def aligned(index, size):
    return pl.ds(pl.multiple_of(index * size, size), size)


def prepare_kernel(plan, where, latents, gain, qkv_weight, proj_weight, merge_weight, *rest):
    shares = rest[: plan.windows]
    keep, give, cross, held, factor, sems = rest[plan.windows :]
    copies = []

    def add(source, target):
        copies.append(pltpu.make_async_copy(source, target, sems.at[len(copies)]))

    for part in range(3):
        add(
            qkv_weight.at[0, :, part * plan.features : (part + 1) * plan.features],
            held.at[part],
        )
    add(gain, factor)
    width, rows = (plan.half_cols, plan.w_rows)
    for part, matrix in enumerate((proj_weight, merge_weight)):
        add(
            matrix.at[0, :, aligned(where[0] ^ 1, width)],
            cross.at[part * rows : (part + 1) * rows, :],
        )
    for mz in range(plan.windows):
        add(latents.at[where[1] ^ mz, aligned(where[0], plan.half), :], shares[mz])
    for copy in copies:
        copy.start()
    for copy in copies[:4]:
        copy.wait()
    first_row = (where[1] * plan.inner + where[2]) * rows
    row = first_row + lax.broadcasted_iota(jnp.int32, (rows, plan.features), 0)
    lane = lax.broadcasted_iota(jnp.int32, (rows, plan.features), 1)
    factors = jnp.where(row == lane, factor[...], jnp.zeros((1, plan.features), jnp.float32))
    factors = jnp.sum(factors, axis=1, keepdims=True)
    for core, target in ((1, give), (0, keep)):
        for chip_no, (mx, mi) in enumerate(plan.chips):
            lanes = aligned(slot_of(plan, where, mx, mi ^ core), plan.cols)
            for part in range(3):
                scaled = held[part, :, lanes].astype(jnp.float32) * factors
                target[chip_no, :, part * plan.cols : (part + 1) * plan.cols] = scaled.astype(
                    jnp.bfloat16
                )
    for copy in copies[4:]:
        copy.wait()


def pair_kernel(plan, keep, given, *outs):
    rows = plan.w_rows
    for chip_no, out in enumerate(outs):
        out[0:rows, :] = keep[chip_no]
        out[rows:, :] = given[chip_no]


def merge_kernel(plan, where, proj_weight, merge_weight, crossed, mats, last):
    rows, width = (plan.w_rows, plan.half_cols)
    for section in range(plan.sections):

        @pl.when(where[0] == section)
        def _():
            lanes = slice(section * width, (section + 1) * width)
            mine = proj_weight[0, :, lanes]
            others = crossed[0:rows, :]
            mats[:, 0:width] = mine if section == 0 else others
            last[...] = others if section == 0 else mine
            total = merge_weight[0, :, lanes].astype(jnp.float32)
            total = total + crossed[rows:, :].astype(jnp.float32)
            mats[:, width:] = total.astype(jnp.bfloat16)


def sort_kernel(plan, where, last, *refs):
    count = len(plan.chips)
    pieces, (rows_a, rows_b) = (refs[:count], refs[count:])
    rows, cols = (plan.w_rows, 3 * plan.cols)
    lone = plan.half_cols // plan.inner
    for section in range(plan.sections):

        @pl.when(where[0] == section)
        def _():
            outs = (rows_a, rows_b)
            for piece, (mx, mi) in zip(pieces, plan.chips):
                part = slice(mi * rows, (mi + 2) * rows)
                outs[section ^ mx][part, 0:cols] = piece[...]

    for mi in range(plan.inner):
        rows_b[mi * rows : (mi + 1) * rows, cols:] = last[:, mi * lone : (mi + 1) * lone]


def last_kernel(plan, *refs):
    rows, lone = (plan.w_rows, plan.half_cols // plan.inner)
    for mz, piece in enumerate(refs[:-1]):
        for mi in range(plan.inner):
            refs[-1][mz * rows : (mz + 1) * rows, mi * lone : (mi + 1) * lone] = piece[
                mi * rows : (mi + 1) * rows, 3 * plan.cols :
            ]


def stack_kernel(*refs):
    start = 0
    for piece in refs[:-1]:
        rows = piece.shape[0]
        refs[-1][start : start + rows, :] = piece[...]
        start += rows


def gather_weights(plan, where, pieces, target):
    rows = plan.w_rows
    for mz, piece in enumerate(pieces):
        for mi in range(plan.inner):
            shard = (where[1] ^ mz) * plan.inner + (where[2] ^ mi)
            target[aligned(shard, rows), :] = piece[
                mi * rows : (mi + 1) * rows, 0 : 3 * plan.cols
            ]


def plane_order(plan):
    return [(mx, mi ^ core) for core in range(2) for mx, mi in plan.chips]


def normalize(values):
    center = values - jnp.mean(values, axis=-1, keepdims=True)
    spread = jnp.mean(center * center, axis=-1, keepdims=True)
    return (center * lax.rsqrt(spread + EPSILON)).astype(jnp.bfloat16)


def row_blocks(plan, one_block):
    size = min(512, plan.tokens)

    def step(block_no, carry):
        one_block(aligned(block_no, size))
        return carry

    lax.fori_loop(0, plan.tokens // size, step, 0)


def norm_kernel(plan, where, *refs):
    hid, normed = refs[plan.slots :]
    for piece, (mx, mi) in zip(refs, plane_order(plan)):
        rows = aligned(slot_of(plan, where, mx, mi), plan.shard)
        hid[rows, :] = piece[...]
        normed[rows, :] = normalize(piece[...].astype(jnp.float32))


def first_kernel(plan, where, normed, *rest):
    pieces = rest[: plan.windows]
    out, w_qkv, qkv = rest[plan.windows :]
    gather_weights(plan, where, pieces, w_qkv)

    def one_block(rows):
        qkv[rows, :] = project_rows(normed[rows, :], w_qkv[...], plan.cols)

    row_blocks(plan, one_block)
    attention(qkv, out, plan.cols)


def fold_kernel(plan, where, hid, *rest):
    mats_in, (merged, folded, mats) = (rest[: plan.slots], rest[plan.slots :])
    rows, width = (plan.w_rows, plan.half_cols)
    for piece, (mx, mi) in zip(mats_in, plane_order(plan)):
        for mz in range(plan.windows):
            shard = (where[1] ^ mz) * plan.inner + (where[2] ^ mi)
            part = piece[mz * rows : (mz + 1) * rows, :]
            for kind in range(2):
                lanes = aligned(where[0] ^ mx, width)
                mats[kind, aligned(shard, rows), lanes] = part[:, kind * width : (kind + 1) * width]

    def one_block(part):
        merged[part, :] = jnp.dot(hid[part, :], mats[1], preferred_element_type=jnp.float32)

    row_blocks(plan, one_block)
    size = min(512, plan.features)

    def one_part(block_no, carry):
        part = aligned(block_no, size)
        folded[part, :] = jnp.dot(
            mats[0, part, :], mats[1], preferred_element_type=jnp.float32
        ).astype(jnp.bfloat16)
        return carry

    lax.fori_loop(0, plan.features // size, one_part, 0)


def second_kernel(plan, where, merged, folded, *rest):
    slots, windows = (plan.slots, plan.windows)
    attended_in, rest = (rest[:slots], rest[slots:])
    pieces, rest = (rest[:windows], rest[windows:])
    outs, rest = (rest[: plan.inner // 2], rest[plan.inner // 2 :])
    kept, att, w_qkv, joined, qkv, mixed = rest
    for piece, (mx, mi) in zip(attended_in, plane_order(plan)):
        att[:, aligned(slot_of(plan, where, mx, mi), plan.cols)] = piece[...]
    gather_weights(plan, where, pieces, w_qkv)
    width = plan.half_cols

    def one_block(part):
        total = jnp.dot(att[part, :], folded[...], preferred_element_type=jnp.float32)
        total = (merged[part, :] + total).astype(jnp.bfloat16)
        joined[part, :] = total
        qkv[part, :] = project_rows(
            normalize(total.astype(jnp.float32)), w_qkv[...], plan.cols
        )

    row_blocks(plan, one_block)
    attention(qkv, mixed, plan.cols)
    lanes = aligned(where[0], width)
    for side in range(plan.sections):
        for mi in range(plan.inner):
            part = aligned(side * plan.inner + (where[2] ^ mi), plan.shard)
            start = ((mi % 2) * plan.sections + side) * plan.shard
            outs[mi // 2][start : start + plan.shard, :] = mixed[part, :]
            if mi == 0:
                kept[side * plan.shard : (side + 1) * plan.shard, :] = joined[part, lanes]


def third_kernel(plan, where, kept, *rest):
    chips, rest = (rest[: len(plan.chips)], rest[len(plan.chips) :])
    swapped, mats_in = (rest[0], rest[1 : 1 + plan.inner])
    outs, (att, mat) = (rest[1 + plan.inner : -2], rest[-2:])
    rows = plan.sections * plan.shard
    for chip_no, (mx, mi) in enumerate(plan.chips):
        for core in range(2):
            lanes = aligned(slot_of(plan, where, mx, mi ^ core), plan.cols)
            if core == 0:
                att[:, lanes] = chips[chip_no][0:rows, :]
            else:
                att[:, lanes] = swapped[chip_no * rows : (chip_no + 1) * rows, :]
    rows = plan.w_rows
    order = [mi ^ core for core in range(2) for mi in range(0, plan.inner, 2)]
    for piece, mi in zip(mats_in, order):
        for mz in range(plan.windows):
            shard = (where[1] ^ mz) * plan.inner + (where[2] ^ mi)
            mat[aligned(shard, rows), :] = piece[mz * rows : (mz + 1) * rows, :]
    result = jnp.dot(att[...], mat[...], preferred_element_type=jnp.float32)
    result = (kept[...].astype(jnp.float32) + result).astype(jnp.bfloat16)
    for side in range(plan.sections):
        for mz in range(plan.windows):
            start = side * plan.shard + mz * plan.half
            outs[mz][side * plan.half : (side + 1) * plan.half, :] = result[
                start : start + plan.half, :
            ]


def place_kernel(plan, where, *refs):
    for mz in range(plan.windows):
        refs[-1][where[1] ^ mz] = refs[mz][...]


def halves_kernel(plan, *refs):
    rows = plan.sections * plan.shard
    for chip_no, piece in enumerate(refs[:-1]):
        refs[-1][chip_no * rows : (chip_no + 1) * rows, :] = piece[rows:, :]


def plane_body(latents, norm_gain, qkv_weight, proj_weight, merge_weight):
    plan = Plan(
        lax.axis_size("section"), lax.axis_size("seq"), latents.shape[0], *latents.shape[1:]
    )
    windows, inner, shard, cols = (plan.windows, plan.inner, plan.shard, plan.cols)
    section = lax.axis_index("section")
    position = lax.axis_index("seq")
    window, place = (position // inner, position % inner)
    lane = lax.iota(jnp.int32, 3)
    where = jnp.where(lane == 0, section, jnp.where(lane == 1, window, place)).astype(jnp.int32)
    devices = plan.sections * plan.seq_count
    bf16 = jnp.bfloat16
    smem = pl.BlockSpec(memory_space=pltpu.SMEM)
    hbm = pl.BlockSpec(memory_space=pltpu.HBM)
    vmem = pl.BlockSpec(memory_space=pltpu.VMEM)
    tokens, features, width = (plan.tokens, plan.features, plan.half_cols)

    def swap(value, mask):
        pairs = [(source, source ^ mask) for source in range(devices)]
        return lax.ppermute(value, ("section", "seq"), pairs)

    def call(kernel, outs, ins, scratch=(), specs=None, flops=0, limit=40):
        typed = [shape if isinstance(shape[0], tuple) else (shape, bf16) for shape in outs]
        shapes = tuple(jax.ShapeDtypeStruct(*entry) for entry in typed)
        moved = sum(2 * value.size for value in ins)
        return pl.pallas_call(
            kernel,
            out_shape=shapes,
            in_specs=specs or [vmem] * len(ins),
            out_specs=tuple(vmem for _ in shapes),
            scratch_shapes=list(scratch),
            cost_estimate=pl.CostEstimate(
                flops=flops, bytes_accessed=moved, transcendentals=0
            ),
            compiler_params=pltpu.CompilerParams(vmem_limit_bytes=limit << 20),
        )(*ins)

    def stack(pieces):
        rows = sum(piece.shape[0] for piece in pieces)
        return call(stack_kernel, [(rows, pieces[0].shape[1])], pieces, limit=8)[0]

    def z_gather(value):
        pieces = [value]
        for mz in range(1, windows):
            low = mz & -mz
            pieces.append(swap(pieces[mz - low], plan.mask(mz=low)))
        return pieces

    def chip_gather(value):
        return [value] + [
            swap(value, plan.mask(mx=mx, mi=mi))
            for chip_no, (mx, mi) in enumerate(plan.chips)
            if chip_no
        ]

    def core_gather(pieces):
        return pieces + [swap(piece, plan.mask(mi=1)) for piece in pieces]

    latents, norm_gain, qkv_weight, proj_weight, merge_weight = (
        pltpu.with_memory_space_constraint(value, pltpu.HBM)
        for value in (latents, norm_gain, qkv_weight, proj_weight, merge_weight)
    )
    prepared = call(
        lambda *refs: prepare_kernel(plan, *refs),
        [(plan.half, features)] * windows
        + [(len(plan.chips), plan.w_rows, 3 * cols)] * 2
        + [(2 * plan.w_rows, width)],
        [where, latents, norm_gain, qkv_weight, proj_weight, merge_weight],
        [
            pltpu.VMEM((3, plan.w_rows, features), bf16),
            pltpu.VMEM((1, features), jnp.float32),
            pltpu.SemaphoreType.DMA((6 + windows,)),
        ],
        [smem] + [hbm] * 5,
        limit=8,
    )
    shares, (keep, give, cross) = (prepared[:windows], prepared[windows:])
    given = swap(give, plan.mask(mi=1))
    crossed = swap(cross, plan.mask(mx=1))
    shares = [shares[0]] + [swap(shares[mz], plan.mask(mz=mz)) for mz in range(1, windows)]
    outgoing = call(
        lambda *refs: pair_kernel(plan, *refs),
        [(2 * plan.w_rows, 3 * cols)] * len(plan.chips),
        [keep, given],
        limit=8,
    )
    incoming = [outgoing[0]] + [
        swap(outgoing[chip_no], plan.mask(mx=mx, mi=mi))
        for chip_no, (mx, mi) in enumerate(plan.chips)
        if chip_no
    ]
    hidden = chip_gather(stack(shares))
    hidden = core_gather(hidden)
    mats, last = call(
        lambda *refs: merge_kernel(plan, *refs),
        [(plan.w_rows, 2 * width), (plan.w_rows, width)],
        [where, proj_weight, merge_weight, crossed],
        (),
        [smem] + [vmem] * 3,
        limit=8,
    )
    rows_a, rows_b = call(
        lambda *refs: sort_kernel(plan, *refs),
        [
            (plan.group, 3 * cols),
            (plan.group, 3 * cols + width // inner),
        ],
        [where, last] + incoming,
        (),
        [smem] + [vmem] * (1 + len(incoming)),
        limit=8,
    )
    mats = z_gather(mats)
    pieces_a = z_gather(rows_a)
    pieces_b = z_gather(rows_b)
    mats = chip_gather(stack(mats))

    hid, normed = call(
        lambda *refs: norm_kernel(plan, *refs),
        [(tokens, features)] * 2,
        [where] + hidden,
        (),
        [smem] + [vmem] * len(hidden),
        limit=16,
    )
    (attended,) = call(
        lambda *refs: first_kernel(plan, *refs),
        [(tokens, cols)],
        [where, normed] + pieces_a,
        [pltpu.VMEM((features, 3 * cols), bf16), pltpu.VMEM((tokens, 3 * cols), bf16)],
        [smem] + [vmem] * (1 + windows),
        flops=10_000_000_000,
        limit=20,
    )
    attended = core_gather(chip_gather(attended))
    mats = core_gather(mats)
    merged, folded = call(
        lambda *refs: fold_kernel(plan, *refs),
        [((tokens, features), jnp.float32), (features, features)],
        [where, hid] + mats,
        [pltpu.VMEM((2, features, features), bf16)],
        [smem] + [vmem] * (1 + plan.slots),
        flops=4_000_000_000,
        limit=30,
    )
    (last,) = call(lambda *refs: last_kernel(plan, *refs), [(plan.group, width)], pieces_b, limit=8)
    last = [last] + [swap(last, plan.mask(mi=mi)) for mi in range(2, inner, 2)]
    last = core_gather(last)
    *attended, kept = call(
        lambda *refs: second_kernel(plan, *refs),
        [(2 * plan.sections * shard, cols)] * (inner // 2) + [(plan.sections * shard, width)],
        [where, merged, folded] + attended + pieces_b,
        [
            pltpu.VMEM((tokens, features), bf16),
            pltpu.VMEM((features, 3 * cols), bf16),
            pltpu.VMEM((tokens, features), bf16),
            pltpu.VMEM((tokens, 3 * cols), bf16),
            pltpu.VMEM((tokens, cols), bf16),
        ],
        [smem] + [vmem] * (2 + plan.slots + windows),
        flops=18_000_000_000,
    )
    back = [attended[0]] + [
        swap(attended[mi // 2], plan.mask(mx=mx, mi=mi))
        for chip_no, (mx, mi) in enumerate(plan.chips)
        if chip_no
    ]
    (halves,) = call(
        lambda *refs: halves_kernel(plan, *refs),
        [(len(plan.chips) * plan.sections * shard, cols)],
        back,
        limit=8,
    )
    swapped = swap(halves, plan.mask(mi=1))
    outcome = call(
        lambda *refs: third_kernel(plan, *refs),
        [(plan.tok_rows, width)] * windows,
        [where, kept] + back + [swapped] + last,
        [
            pltpu.VMEM((plan.sections * shard, features), bf16),
            pltpu.VMEM((features, width), bf16),
        ],
        [smem] + [vmem] * (2 + len(back) + inner),
        flops=1_000_000_000,
        limit=16,
    )
    outcome = [outcome[0]] + [swap(outcome[mz], plan.mask(mz=mz)) for mz in range(1, windows)]
    return call(
        lambda *refs: place_kernel(plan, *refs),
        [(windows, plan.tok_rows, width)],
        [where] + outcome,
        (),
        [smem] + [vmem] * windows,
        limit=8,
    )[0]


def solution(mesh):
    placed = (
        P(None, "seq", None),
        P("section", None),
        P("section", "seq", None),
        P("section", "seq", None),
        P("section", "seq", None),
    )

    def plane_step(*arguments):
        return plane_body(*arguments)

    def step(latents, *weights):
        sizes = (
            mesh.shape["section"],
            mesh.shape["seq"],
            latents.shape[0],
            latents.shape[1] // mesh.shape["seq"],
            latents.shape[2],
        )
        fits = Plan.fits(*sizes)
        mapped = jax.shard_map(
            plane_step if fits else body,
            mesh=mesh,
            in_specs=placed,
            out_specs=P(None, "seq", "section"),
            check_vma=False,
        )
        return mapped(latents, *weights)

    return step
```

```python
import jax
import jax.numpy as jnp
from jax import lax
from jax.experimental import pallas as pl
from jax.experimental.pallas import tpu as pltpu
from jax.sharding import PartitionSpec as P

HEADS = 16
HEAD_DIM = 64


EPSILON = 1e-05


def partner(value, axis, bit):
    mask = 2**bit
    pairs = [(source, source ^ mask) for source in range(lax.axis_size(axis))]
    return lax.ppermute(value, axis, pairs)


def shifted(value, axis, steps):
    count = lax.axis_size(axis)
    initial, last = (max(0, -steps), min(count, count - steps))
    return lax.ppermute(value, axis, [(source, source + steps) for source in range(initial, last)])


def layer_norm(hidden, gain_row):
    values = hidden.astype(jnp.float32)
    center = values - jnp.mean(values, axis=-1, keepdims=True)
    spread = jnp.mean(center * center, axis=-1, keepdims=True)
    return (center * lax.rsqrt(spread + EPSILON) * gain_row).astype(jnp.bfloat16)


def body(latents, norm_gain, qkv_weight, proj_weight, merge_weight):
    seq_count = lax.axis_size("seq")
    section_count = lax.axis_size("section")
    my_section = lax.axis_index("section")
    midpoint = section_count // 2
    windows = latents.shape[0]
    tok_rows = latents.shape[1]
    features = latents.shape[2]
    repeat = max(seq_count // HEADS, 1)
    groups = seq_count // repeat
    head_cols = features * repeat // seq_count
    per_device = head_cols // HEAD_DIM
    part_rows = tok_rows // repeat
    scale_factor = HEAD_DIM ** (-0.5)
    w_qkv, w_proj, w_merge = (
        lax.all_gather(qkv_weight, "seq", axis=1, tiled=True),
        lax.all_gather(proj_weight, "seq", axis=1, tiled=True),
        lax.all_gather(merge_weight, "seq", axis=1, tiled=True),
    )
    w_qkv = w_qkv[0]
    w_proj = w_proj[0]
    w_merge = w_merge[0]
    gain_row = norm_gain[0]
    decoder = my_section >= midpoint
    encoder = my_section < midpoint
    query_shape = (seq_count, part_rows * head_cols)
    key_shape = (seq_count, tok_rows * head_cols)

    def to_heads(array_in, spread_copies):
        if spread_copies:
            grouped = array_in.reshape(tok_rows, groups, head_cols).transpose(1, 0, 2)
            grouped = grouped.reshape(groups, 1, tok_rows * head_cols)
            grouped = jnp.broadcast_to(grouped, (groups, repeat, tok_rows * head_cols))
            return grouped.reshape(seq_count, tok_rows * head_cols)
        grouped = array_in.reshape(part_rows, repeat, groups, head_cols).transpose(2, 1, 0, 3)
        return grouped.reshape(seq_count, part_rows * head_cols)

    def from_heads(array_in):
        grouped = array_in.reshape(groups, repeat, part_rows, head_cols).transpose(2, 1, 0, 3)
        return grouped.reshape(tok_rows, features)

    def project(carried):
        normed = layer_norm(carried, gain_row)
        packed = jnp.dot(normed, w_qkv, preferred_element_type=jnp.float32).astype(jnp.bfloat16)
        return (
            to_heads(packed[:, :features], False),
            to_heads(packed[:, features : 2 * features], True),
            to_heads(packed[:, 2 * features :], True),
        )

    def spare_heads():
        return (
            jnp.zeros(query_shape, jnp.bfloat16),
            jnp.zeros(key_shape, jnp.bfloat16),
            jnp.zeros(key_shape, jnp.bfloat16),
        )

    def attend(queries, keys_in, values_in):
        query_rows = queries.reshape(-1, per_device, HEAD_DIM)
        key_rows = keys_in.reshape(-1, per_device, HEAD_DIM)
        value_rows = values_in.reshape(-1, per_device, HEAD_DIM)
        block_rows = min(512, query_rows.shape[0])
        blocked = query_rows.reshape(-1, block_rows, per_device, HEAD_DIM)

        def one_block(query_block):
            scores = (
                jnp.einsum(
                    "qhd,khd->hqk", query_block, key_rows, preferred_element_type=jnp.float32
                )
                * scale_factor
            )
            row_max = jnp.max(scores, axis=-1, keepdims=True)
            weights = jnp.exp(scores - row_max)
            totals = jnp.sum(weights, axis=-1)
            probs = weights.astype(jnp.bfloat16)
            mixed = jnp.einsum(
                "hqk,khd->qhd", probs, value_rows, preferred_element_type=jnp.float32
            )
            return (mixed / totals.T[:, :, None]).astype(jnp.bfloat16)

        return lax.map(one_block, blocked).reshape(query_shape)

    def mirror_each(skip_term):
        for bit_no in range(section_count.bit_length() - 1):
            skip_term = partner(skip_term, "section", bit_no)
        return skip_term

    def tick(tick_no, loop_state):
        incoming, skip_store, result = loop_state
        window_no = tick_no - my_section
        active = (window_no >= 0) & (window_no < windows)
        chosen = jnp.clip(window_no, 0, windows - 1)
        fresh = lax.dynamic_index_in_dim(latents, chosen, 0, keepdims=False)
        entering = jnp.where(my_section == 0, fresh, incoming)
        skip_slot = lax.dynamic_index_in_dim(skip_store, chosen, 0, keepdims=False)
        carried = lax.cond(
            active & decoder,
            lambda: (
                jnp.dot(entering, w_merge, preferred_element_type=jnp.float32)
                + skip_slot.astype(jnp.float32)
            ).astype(jnp.bfloat16),
            lambda: entering,
        )
        queries, keys_in, values_in = lax.cond(active, lambda: project(carried), spare_heads)
        queries, keys_in, values_in = (
            lax.all_to_all(queries, "seq", split_axis=0, concat_axis=0, tiled=True),
            lax.all_to_all(keys_in, "seq", split_axis=0, concat_axis=0, tiled=True),
            lax.all_to_all(values_in, "seq", split_axis=0, concat_axis=0, tiled=True),
        )
        attended = lax.cond(
            active,
            lambda: attend(queries, keys_in, values_in),
            lambda: jnp.zeros(query_shape, jnp.bfloat16),
        )
        attended = lax.all_to_all(attended, "seq", split_axis=0, concat_axis=0, tiled=True)
        leaving = lax.cond(
            active,
            lambda: (
                carried.astype(jnp.float32)
                + jnp.dot(from_heads(attended), w_proj, preferred_element_type=jnp.float32)
            ).astype(jnp.bfloat16),
            lambda: carried,
        )
        skip_term = lax.cond(
            active & encoder,
            lambda: jnp.dot(leaving, w_merge, preferred_element_type=jnp.float32).astype(
                jnp.bfloat16
            ),
            lambda: jnp.zeros_like(leaving),
        )
        arrived = mirror_each(skip_term)
        source_no = tick_no - (section_count - 1 - my_section)
        landing = decoder & (source_no >= 0) & (source_no < windows)
        target = jnp.clip(source_no, 0, windows - 1)
        updated = lax.dynamic_update_index_in_dim(skip_store, arrived, target, 0)
        skip_store = jnp.where(landing, updated, skip_store)
        incoming = shifted(leaving, "section", 1)
        finished = lax.dynamic_update_index_in_dim(result, leaving.astype(jnp.float32), chosen, 0)
        result = jnp.where(active & (my_section == section_count - 1), finished, result)
        return (incoming, skip_store, result)

    loop_state = (
        jnp.zeros(latents.shape[1:], jnp.bfloat16),
        jnp.zeros_like(latents),
        jnp.zeros(latents.shape, jnp.float32),
    )
    loop_state = lax.fori_loop(0, windows + section_count - 1, tick, loop_state)
    result = loop_state[2]
    return lax.psum_scatter(result.astype(jnp.bfloat16), "section", scatter_dimension=2, tiled=True)


class Plan:
    def __init__(self, sections, seq_count, windows, tok_rows, features):
        self.sections = sections
        self.seq_count = seq_count
        self.windows = windows
        self.tok_rows = tok_rows
        self.features = features
        self.inner = seq_count // windows
        self.slots = sections * self.inner
        self.half = tok_rows // sections
        self.shard = windows * self.half
        self.tokens = self.slots * self.shard
        self.cols = features // self.slots
        self.half_cols = features // sections
        self.w_rows = features // seq_count
        self.group = self.inner * self.w_rows
        self.chips = [(mx, mi) for mx in range(sections) for mi in range(0, self.inner, 2)]

    @staticmethod
    def fits(sections, seq_count, windows, tok_rows, features):
        if sections != 2 or windows & (windows - 1) or seq_count % (2 * windows):
            return False
        inner = seq_count // windows
        if inner != 4 or features % (sections * inner * 2 * HEAD_DIM):
            return False
        return features == HEADS * HEAD_DIM and tok_rows % 32 == 0

    def mask(self, mx=0, mz=0, mi=0):
        return mx * self.seq_count + mz * self.inner + mi


def attention(queries, qkv, out, cols):
    lane_head = lax.broadcasted_iota(jnp.int32, (1, cols), 1) // HEAD_DIM
    keys_in = qkv[:, cols : 2 * cols]
    values_in = qkv[:, 2 * cols : 3 * cols]
    mixed = jnp.zeros(queries.shape, jnp.float32)
    for head in range(cols // HEAD_DIM):
        mine = lane_head == head
        picked = jnp.where(mine, queries, jnp.zeros_like(queries))
        scores = lax.dot_general(
            keys_in, picked, (((1,), (1,)), ((), ())), preferred_element_type=jnp.float32
        )
        weights = jnp.exp(scores - jnp.max(scores, axis=0, keepdims=True))
        totals = jnp.sum(weights, axis=0, keepdims=True)
        part = lax.dot_general(
            values_in,
            weights.astype(jnp.bfloat16),
            (((0,), (0,)), ((), ())),
            preferred_element_type=jnp.float32,
        )
        mixed = jnp.where(mine, (part / totals).T, mixed)
    out[...] = mixed.astype(jnp.bfloat16)


def project_rows(normed, w_qkv, cols):
    packed = jnp.dot(normed, w_qkv, preferred_element_type=jnp.float32)
    lane = lax.broadcasted_iota(jnp.int32, (1, packed.shape[1]), 1)
    packed = packed.astype(jnp.bfloat16)
    return jnp.where(lane < cols, packed * jnp.bfloat16(HEAD_DIM ** (-0.5)), packed)


def slot_of(plan, where, mx, mi):
    return (where[0] ^ mx) * plan.inner + (where[2] ^ mi)


def aligned(index, size):
    return pl.ds(pl.multiple_of(index * size, size), size)


def prepare_kernel(plan, where, latents, gain, qkv_weight, proj_weight, merge_weight, *rest):
    shares = rest[: plan.windows]
    keep, give, cross, held, factor, sems = rest[plan.windows :]
    copies = []

    def add(source, target):
        copies.append(pltpu.make_async_copy(source, target, sems.at[len(copies)]))

    for part in range(3):
        add(
            qkv_weight.at[0, :, part * plan.features : (part + 1) * plan.features],
            held.at[part],
        )
    add(gain, factor)
    width, rows = (plan.half_cols, plan.w_rows)
    for part, matrix in enumerate((proj_weight, merge_weight)):
        add(
            matrix.at[0, :, aligned(where[0] ^ 1, width)],
            cross.at[part * rows : (part + 1) * rows, :],
        )
    for mz in range(plan.windows):
        add(latents.at[where[1] ^ mz, aligned(where[0], plan.half), :], shares[mz])
    for copy in copies:
        copy.start()
    for copy in copies[:4]:
        copy.wait()
    first_row = (where[1] * plan.inner + where[2]) * rows
    row = first_row + lax.broadcasted_iota(jnp.int32, (rows, plan.features), 0)
    lane = lax.broadcasted_iota(jnp.int32, (rows, plan.features), 1)
    factors = jnp.where(row == lane, factor[...], jnp.zeros((1, plan.features), jnp.float32))
    factors = jnp.sum(factors, axis=1, keepdims=True)
    for core, target in ((1, give), (0, keep)):
        for chip_no, (mx, mi) in enumerate(plan.chips):
            lanes = aligned(slot_of(plan, where, mx, mi ^ core), plan.cols)
            for part in range(3):
                scaled = held[part, :, lanes].astype(jnp.float32) * factors
                target[chip_no, :, part * plan.cols : (part + 1) * plan.cols] = scaled.astype(
                    jnp.bfloat16
                )
    for copy in copies[4:]:
        copy.wait()


def pair_kernel(plan, keep, given, *outs):
    rows = plan.w_rows
    for chip_no, out in enumerate(outs):
        out[0:rows, :] = keep[chip_no]
        out[rows:, :] = given[chip_no]


def merge_kernel(plan, where, proj_weight, merge_weight, crossed, mats, last):
    rows, width = (plan.w_rows, plan.half_cols)
    for section in range(plan.sections):

        @pl.when(where[0] == section)
        def _():
            lanes = slice(section * width, (section + 1) * width)
            mine = proj_weight[0, :, lanes]
            others = crossed[0:rows, :]
            mats[:, 0:width] = mine if section == 0 else others
            last[...] = others if section == 0 else mine
            total = merge_weight[0, :, lanes].astype(jnp.float32)
            total = total + crossed[rows:, :].astype(jnp.float32)
            mats[:, width:] = total.astype(jnp.bfloat16)


def sort_kernel(plan, where, last, *refs):
    count = len(plan.chips)
    pieces, (rows_a, rows_b) = (refs[:count], refs[count:])
    rows, cols = (plan.w_rows, 3 * plan.cols)
    lone = plan.half_cols // plan.inner
    for section in range(plan.sections):

        @pl.when(where[0] == section)
        def _():
            outs = (rows_a, rows_b)
            for piece, (mx, mi) in zip(pieces, plan.chips):
                part = slice(mi * rows, (mi + 2) * rows)
                outs[section ^ mx][part, 0:cols] = piece[...]

    for mi in range(plan.inner):
        rows_b[mi * rows : (mi + 1) * rows, cols:] = last[:, mi * lone : (mi + 1) * lone]


def last_kernel(plan, *refs):
    rows, lone = (plan.w_rows, plan.half_cols // plan.inner)
    for mz, piece in enumerate(refs[:-1]):
        for mi in range(plan.inner):
            refs[-1][mz * rows : (mz + 1) * rows, mi * lone : (mi + 1) * lone] = piece[
                mi * rows : (mi + 1) * rows, 3 * plan.cols :
            ]


def stack_kernel(*refs):
    start = 0
    for piece in refs[:-1]:
        rows = piece.shape[0]
        refs[-1][start : start + rows, :] = piece[...]
        start += rows


def gather_weights(plan, where, pieces, target):
    rows = plan.w_rows
    for mz, piece in enumerate(pieces):
        for mi in range(plan.inner):
            shard = (where[1] ^ mz) * plan.inner + (where[2] ^ mi)
            target[aligned(shard, rows), :] = piece[
                mi * rows : (mi + 1) * rows, 0 : 3 * plan.cols
            ]


def plane_order(plan):
    return [(mx, mi ^ core) for core in range(2) for mx, mi in plan.chips]


def normalize(values):
    center = values - jnp.mean(values, axis=-1, keepdims=True)
    spread = jnp.mean(center * center, axis=-1, keepdims=True)
    return (center * lax.rsqrt(spread + EPSILON)).astype(jnp.bfloat16)


def row_blocks(plan, one_block):
    size = min(512, plan.tokens)

    def step(block_no, carry):
        one_block(aligned(block_no, size))
        return carry

    lax.fori_loop(0, plan.tokens // size, step, 0)


def norm_kernel(plan, where, *refs):
    hid, normed = refs[plan.slots :]
    for piece, (mx, mi) in zip(refs, plane_order(plan)):
        rows = aligned(slot_of(plan, where, mx, mi), plan.shard)
        hid[rows, :] = piece[...]
        normed[rows, :] = normalize(piece[...].astype(jnp.float32))


def first_kernel(plan, where, normed, *rest):
    pieces = rest[: plan.windows]
    out, w_qkv, qkv = rest[plan.windows :]
    gather_weights(plan, where, pieces, w_qkv)

    def one_block(rows):
        qkv[rows, :] = project_rows(normed[rows, :], w_qkv[...], plan.cols)

    row_blocks(plan, one_block)
    attention(qkv[:, 0 : plan.cols], qkv, out, plan.cols)


def fold_kernel(plan, where, hid, *rest):
    mats_in, (merged, folded, mats) = (rest[: plan.slots], rest[plan.slots :])
    rows, width = (plan.w_rows, plan.half_cols)
    for piece, (mx, mi) in zip(mats_in, plane_order(plan)):
        for mz in range(plan.windows):
            shard = (where[1] ^ mz) * plan.inner + (where[2] ^ mi)
            part = piece[mz * rows : (mz + 1) * rows, :]
            for kind in range(2):
                lanes = aligned(where[0] ^ mx, width)
                mats[kind, aligned(shard, rows), lanes] = part[:, kind * width : (kind + 1) * width]

    def one_block(part):
        merged[part, :] = jnp.dot(hid[part, :], mats[1], preferred_element_type=jnp.float32)

    row_blocks(plan, one_block)
    size = min(512, plan.features)

    def one_part(block_no, carry):
        part = aligned(block_no, size)
        folded[part, :] = jnp.dot(
            mats[0, part, :], mats[1], preferred_element_type=jnp.float32
        ).astype(jnp.bfloat16)
        return carry

    lax.fori_loop(0, plan.features // size, one_part, 0)


def second_kernel(plan, where, merged, folded, *rest):
    slots, windows = (plan.slots, plan.windows)
    attended_in, rest = (rest[:slots], rest[slots:])
    pieces, rest = (rest[:windows], rest[windows:])
    out, kept, qkv, att, w_qkv, joined = rest
    for piece, (mx, mi) in zip(attended_in, plane_order(plan)):
        att[:, aligned(slot_of(plan, where, mx, mi), plan.cols)] = piece[...]
    gather_weights(plan, where, pieces, w_qkv)
    width = plan.half_cols

    def one_block(part):
        total = jnp.dot(att[part, :], folded[...], preferred_element_type=jnp.float32)
        total = (merged[part, :] + total).astype(jnp.bfloat16)
        joined[part, :] = total
        qkv[part, :] = project_rows(
            normalize(total.astype(jnp.float32)), w_qkv[...], plan.cols
        )

    row_blocks(plan, one_block)
    lanes = aligned(where[0], width)
    for side in range(plan.sections):
        part = aligned(side * plan.inner + where[2], plan.shard)
        kept[side * plan.shard : (side + 1) * plan.shard, :] = joined[part, lanes]
    attention(chip_queries(plan, where, qkv, 2), qkv, out, plan.cols)


def chip_queries(plan, where, qkv, mi):
    return jnp.concatenate(
        [
            qkv[aligned(side * plan.inner + (where[2] ^ mi ^ core), plan.shard), 0 : plan.cols]
            for core in range(2)
            for side in range(plan.sections)
        ],
        axis=0,
    )


def rest_kernel(plan, where, qkv, out):
    attention(chip_queries(plan, where, qkv, 0), qkv, out, plan.cols)


def third_kernel(plan, where, kept, *rest):
    chips, rest = (rest[: len(plan.chips)], rest[len(plan.chips) :])
    swapped, mats_in = (rest[0], rest[1 : 1 + plan.inner])
    outs, (att, mat) = (rest[1 + plan.inner : -2], rest[-2:])
    rows = plan.sections * plan.shard
    for chip_no, (mx, mi) in enumerate(plan.chips):
        for core in range(2):
            lanes = aligned(slot_of(plan, where, mx, mi ^ core), plan.cols)
            if core == 0:
                att[:, lanes] = chips[chip_no][0:rows, :]
            else:
                att[:, lanes] = swapped[chip_no * rows : (chip_no + 1) * rows, :]
    rows = plan.w_rows
    order = [mi ^ core for core in range(2) for mi in range(0, plan.inner, 2)]
    for piece, mi in zip(mats_in, order):
        for mz in range(plan.windows):
            shard = (where[1] ^ mz) * plan.inner + (where[2] ^ mi)
            mat[aligned(shard, rows), :] = piece[mz * rows : (mz + 1) * rows, :]
    result = jnp.dot(att[...], mat[...], preferred_element_type=jnp.float32)
    result = (kept[...].astype(jnp.float32) + result).astype(jnp.bfloat16)
    for side in range(plan.sections):
        for mz in range(plan.windows):
            start = side * plan.shard + mz * plan.half
            outs[mz][side * plan.half : (side + 1) * plan.half, :] = result[
                start : start + plan.half, :
            ]


def place_kernel(plan, where, *refs):
    for mz in range(plan.windows):
        refs[-1][where[1] ^ mz] = refs[mz][...]


def halves_kernel(plan, *refs):
    rows = plan.sections * plan.shard
    for chip_no, piece in enumerate(refs[:-1]):
        refs[-1][chip_no * rows : (chip_no + 1) * rows, :] = piece[rows:, :]


def plane_body(latents, norm_gain, qkv_weight, proj_weight, merge_weight):
    plan = Plan(
        lax.axis_size("section"), lax.axis_size("seq"), latents.shape[0], *latents.shape[1:]
    )
    windows, inner, shard, cols = (plan.windows, plan.inner, plan.shard, plan.cols)
    section = lax.axis_index("section")
    position = lax.axis_index("seq")
    window, place = (position // inner, position % inner)
    lane = lax.iota(jnp.int32, 3)
    where = jnp.where(lane == 0, section, jnp.where(lane == 1, window, place)).astype(jnp.int32)
    devices = plan.sections * plan.seq_count
    bf16 = jnp.bfloat16
    smem = pl.BlockSpec(memory_space=pltpu.SMEM)
    hbm = pl.BlockSpec(memory_space=pltpu.HBM)
    vmem = pl.BlockSpec(memory_space=pltpu.VMEM)
    tokens, features, width = (plan.tokens, plan.features, plan.half_cols)

    def swap(value, mask):
        pairs = [(source, source ^ mask) for source in range(devices)]
        return lax.ppermute(value, ("section", "seq"), pairs)

    def call(kernel, outs, ins, scratch=(), specs=None, flops=0, limit=40):
        typed = [shape if isinstance(shape[0], tuple) else (shape, bf16) for shape in outs]
        shapes = tuple(jax.ShapeDtypeStruct(*entry) for entry in typed)
        moved = sum(2 * value.size for value in ins)
        return pl.pallas_call(
            kernel,
            out_shape=shapes,
            in_specs=specs or [vmem] * len(ins),
            out_specs=tuple(vmem for _ in shapes),
            scratch_shapes=list(scratch),
            cost_estimate=pl.CostEstimate(
                flops=flops, bytes_accessed=moved, transcendentals=0
            ),
            compiler_params=pltpu.CompilerParams(vmem_limit_bytes=limit << 20),
        )(*ins)

    def stack(pieces):
        rows = sum(piece.shape[0] for piece in pieces)
        return call(stack_kernel, [(rows, pieces[0].shape[1])], pieces, limit=8)[0]

    def z_gather(value):
        pieces = [value]
        for mz in range(1, windows):
            low = mz & -mz
            pieces.append(swap(pieces[mz - low], plan.mask(mz=low)))
        return pieces

    def chip_gather(value):
        return [value] + [
            swap(value, plan.mask(mx=mx, mi=mi))
            for chip_no, (mx, mi) in enumerate(plan.chips)
            if chip_no
        ]

    def core_gather(pieces):
        return pieces + [swap(piece, plan.mask(mi=1)) for piece in pieces]

    latents, norm_gain, qkv_weight, proj_weight, merge_weight = (
        pltpu.with_memory_space_constraint(value, pltpu.HBM)
        for value in (latents, norm_gain, qkv_weight, proj_weight, merge_weight)
    )
    prepared = call(
        lambda *refs: prepare_kernel(plan, *refs),
        [(plan.half, features)] * windows
        + [(len(plan.chips), plan.w_rows, 3 * cols)] * 2
        + [(2 * plan.w_rows, width)],
        [where, latents, norm_gain, qkv_weight, proj_weight, merge_weight],
        [
            pltpu.VMEM((3, plan.w_rows, features), bf16),
            pltpu.VMEM((1, features), jnp.float32),
            pltpu.SemaphoreType.DMA((6 + windows,)),
        ],
        [smem] + [hbm] * 5,
        limit=8,
    )
    shares, (keep, give, cross) = (prepared[:windows], prepared[windows:])
    given = swap(give, plan.mask(mi=1))
    crossed = swap(cross, plan.mask(mx=1))
    shares = [shares[0]] + [swap(shares[mz], plan.mask(mz=mz)) for mz in range(1, windows)]
    outgoing = call(
        lambda *refs: pair_kernel(plan, *refs),
        [(2 * plan.w_rows, 3 * cols)] * len(plan.chips),
        [keep, given],
        limit=8,
    )
    incoming = [outgoing[0]] + [
        swap(outgoing[chip_no], plan.mask(mx=mx, mi=mi))
        for chip_no, (mx, mi) in enumerate(plan.chips)
        if chip_no
    ]
    hidden = chip_gather(stack(shares))
    hidden = core_gather(hidden)
    mats, last = call(
        lambda *refs: merge_kernel(plan, *refs),
        [(plan.w_rows, 2 * width), (plan.w_rows, width)],
        [where, proj_weight, merge_weight, crossed],
        (),
        [smem] + [vmem] * 3,
        limit=8,
    )
    rows_a, rows_b = call(
        lambda *refs: sort_kernel(plan, *refs),
        [
            (plan.group, 3 * cols),
            (plan.group, 3 * cols + width // inner),
        ],
        [where, last] + incoming,
        (),
        [smem] + [vmem] * (1 + len(incoming)),
        limit=8,
    )
    mats = z_gather(mats)
    pieces_a = z_gather(rows_a)
    pieces_b = z_gather(rows_b)
    mats = chip_gather(stack(mats))

    hid, normed = call(
        lambda *refs: norm_kernel(plan, *refs),
        [(tokens, features)] * 2,
        [where] + hidden,
        (),
        [smem] + [vmem] * len(hidden),
        limit=16,
    )
    (attended,) = call(
        lambda *refs: first_kernel(plan, *refs),
        [(tokens, cols)],
        [where, normed] + pieces_a,
        [pltpu.VMEM((features, 3 * cols), bf16), pltpu.VMEM((tokens, 3 * cols), bf16)],
        [smem] + [vmem] * (1 + windows),
        flops=10_000_000_000,
        limit=20,
    )
    attended = core_gather(chip_gather(attended))
    mats = core_gather(mats)
    merged, folded = call(
        lambda *refs: fold_kernel(plan, *refs),
        [((tokens, features), jnp.float32), (features, features)],
        [where, hid] + mats,
        [pltpu.VMEM((2, features, features), bf16)],
        [smem] + [vmem] * (1 + plan.slots),
        flops=4_000_000_000,
        limit=30,
    )
    (last,) = call(lambda *refs: last_kernel(plan, *refs), [(plan.group, width)], pieces_b, limit=8)
    last = [last] + [swap(last, plan.mask(mi=mi)) for mi in range(2, inner, 2)]
    last = core_gather(last)
    far_rows, kept, qkv = call(
        lambda *refs: second_kernel(plan, *refs),
        [
            (2 * plan.sections * shard, cols),
            (plan.sections * shard, width),
            (tokens, 3 * cols),
        ],
        [where, merged, folded] + attended + pieces_b,
        [
            pltpu.VMEM((tokens, features), bf16),
            pltpu.VMEM((features, 3 * cols), bf16),
            pltpu.VMEM((tokens, features), bf16),
        ],
        [smem] + [vmem] * (2 + plan.slots + windows),
        flops=12_000_000_000,
    )
    (near_rows,) = call(
        lambda *refs: rest_kernel(plan, *refs),
        [far_rows.shape],
        [where, qkv],
        (),
        [smem, vmem],
        flops=6_000_000_000,
        limit=20,
    )
    attended = [near_rows, far_rows]
    back = [attended[0]] + [
        swap(attended[mi // 2], plan.mask(mx=mx, mi=mi))
        for chip_no, (mx, mi) in enumerate(plan.chips)
        if chip_no
    ]
    (halves,) = call(
        lambda *refs: halves_kernel(plan, *refs),
        [(len(plan.chips) * plan.sections * shard, cols)],
        back,
        limit=8,
    )
    swapped = swap(halves, plan.mask(mi=1))
    outcome = call(
        lambda *refs: third_kernel(plan, *refs),
        [(plan.tok_rows, width)] * windows,
        [where, kept] + back + [swapped] + last,
        [
            pltpu.VMEM((plan.sections * shard, features), bf16),
            pltpu.VMEM((features, width), bf16),
        ],
        [smem] + [vmem] * (2 + len(back) + inner),
        flops=1_000_000_000,
        limit=16,
    )
    outcome = [outcome[0]] + [swap(outcome[mz], plan.mask(mz=mz)) for mz in range(1, windows)]
    return call(
        lambda *refs: place_kernel(plan, *refs),
        [(windows, plan.tok_rows, width)],
        [where] + outcome,
        (),
        [smem] + [vmem] * windows,
        limit=8,
    )[0]


def solution(mesh):
    placed = (
        P(None, "seq", None),
        P("section", None),
        P("section", "seq", None),
        P("section", "seq", None),
        P("section", "seq", None),
    )

    def plane_step(*arguments):
        return plane_body(*arguments)

    def step(latents, *weights):
        sizes = (
            mesh.shape["section"],
            mesh.shape["seq"],
            latents.shape[0],
            latents.shape[1] // mesh.shape["seq"],
            latents.shape[2],
        )
        fits = Plan.fits(*sizes)
        mapped = jax.shard_map(
            plane_step if fits else body,
            mesh=mesh,
            in_specs=placed,
            out_specs=P(None, "seq", "section"),
            check_vma=False,
        )
        return mapped(latents, *weights)

    return step
```

```python
import jax
import jax.numpy as jnp
from jax import lax
from jax.experimental import pallas as pl
from jax.experimental.pallas import tpu as pltpu
from jax.sharding import PartitionSpec as P

HEADS = 16
HEAD_DIM = 64


EPSILON = 1e-05


def partner(value, axis, bit):
    mask = 2**bit
    pairs = [(source, source ^ mask) for source in range(lax.axis_size(axis))]
    return lax.ppermute(value, axis, pairs)


def shifted(value, axis, steps):
    count = lax.axis_size(axis)
    initial, last = (max(0, -steps), min(count, count - steps))
    return lax.ppermute(value, axis, [(source, source + steps) for source in range(initial, last)])


def layer_norm(hidden, gain_row):
    values = hidden.astype(jnp.float32)
    center = values - jnp.mean(values, axis=-1, keepdims=True)
    spread = jnp.mean(center * center, axis=-1, keepdims=True)
    return (center * lax.rsqrt(spread + EPSILON) * gain_row).astype(jnp.bfloat16)


def body(latents, norm_gain, qkv_weight, proj_weight, merge_weight):
    seq_count = lax.axis_size("seq")
    section_count = lax.axis_size("section")
    my_section = lax.axis_index("section")
    midpoint = section_count // 2
    windows = latents.shape[0]
    tok_rows = latents.shape[1]
    features = latents.shape[2]
    repeat = max(seq_count // HEADS, 1)
    groups = seq_count // repeat
    head_cols = features * repeat // seq_count
    per_device = head_cols // HEAD_DIM
    part_rows = tok_rows // repeat
    scale_factor = HEAD_DIM ** (-0.5)
    w_qkv, w_proj, w_merge = (
        lax.all_gather(qkv_weight, "seq", axis=1, tiled=True),
        lax.all_gather(proj_weight, "seq", axis=1, tiled=True),
        lax.all_gather(merge_weight, "seq", axis=1, tiled=True),
    )
    w_qkv = w_qkv[0]
    w_proj = w_proj[0]
    w_merge = w_merge[0]
    gain_row = norm_gain[0]
    decoder = my_section >= midpoint
    encoder = my_section < midpoint
    query_shape = (seq_count, part_rows * head_cols)
    key_shape = (seq_count, tok_rows * head_cols)

    def to_heads(array_in, spread_copies):
        if spread_copies:
            grouped = array_in.reshape(tok_rows, groups, head_cols).transpose(1, 0, 2)
            grouped = grouped.reshape(groups, 1, tok_rows * head_cols)
            grouped = jnp.broadcast_to(grouped, (groups, repeat, tok_rows * head_cols))
            return grouped.reshape(seq_count, tok_rows * head_cols)
        grouped = array_in.reshape(part_rows, repeat, groups, head_cols).transpose(2, 1, 0, 3)
        return grouped.reshape(seq_count, part_rows * head_cols)

    def from_heads(array_in):
        grouped = array_in.reshape(groups, repeat, part_rows, head_cols).transpose(2, 1, 0, 3)
        return grouped.reshape(tok_rows, features)

    def project(carried):
        normed = layer_norm(carried, gain_row)
        packed = jnp.dot(normed, w_qkv, preferred_element_type=jnp.float32).astype(jnp.bfloat16)
        return (
            to_heads(packed[:, :features], False),
            to_heads(packed[:, features : 2 * features], True),
            to_heads(packed[:, 2 * features :], True),
        )

    def spare_heads():
        return (
            jnp.zeros(query_shape, jnp.bfloat16),
            jnp.zeros(key_shape, jnp.bfloat16),
            jnp.zeros(key_shape, jnp.bfloat16),
        )

    def attend(queries, keys_in, values_in):
        query_rows = queries.reshape(-1, per_device, HEAD_DIM)
        key_rows = keys_in.reshape(-1, per_device, HEAD_DIM)
        value_rows = values_in.reshape(-1, per_device, HEAD_DIM)
        block_rows = min(512, query_rows.shape[0])
        blocked = query_rows.reshape(-1, block_rows, per_device, HEAD_DIM)

        def one_block(query_block):
            scores = (
                jnp.einsum(
                    "qhd,khd->hqk", query_block, key_rows, preferred_element_type=jnp.float32
                )
                * scale_factor
            )
            row_max = jnp.max(scores, axis=-1, keepdims=True)
            weights = jnp.exp(scores - row_max)
            totals = jnp.sum(weights, axis=-1)
            probs = weights.astype(jnp.bfloat16)
            mixed = jnp.einsum(
                "hqk,khd->qhd", probs, value_rows, preferred_element_type=jnp.float32
            )
            return (mixed / totals.T[:, :, None]).astype(jnp.bfloat16)

        return lax.map(one_block, blocked).reshape(query_shape)

    def mirror_each(skip_term):
        for bit_no in range(section_count.bit_length() - 1):
            skip_term = partner(skip_term, "section", bit_no)
        return skip_term

    def tick(tick_no, loop_state):
        incoming, skip_store, result = loop_state
        window_no = tick_no - my_section
        active = (window_no >= 0) & (window_no < windows)
        chosen = jnp.clip(window_no, 0, windows - 1)
        fresh = lax.dynamic_index_in_dim(latents, chosen, 0, keepdims=False)
        entering = jnp.where(my_section == 0, fresh, incoming)
        skip_slot = lax.dynamic_index_in_dim(skip_store, chosen, 0, keepdims=False)
        carried = lax.cond(
            active & decoder,
            lambda: (
                jnp.dot(entering, w_merge, preferred_element_type=jnp.float32)
                + skip_slot.astype(jnp.float32)
            ).astype(jnp.bfloat16),
            lambda: entering,
        )
        queries, keys_in, values_in = lax.cond(active, lambda: project(carried), spare_heads)
        queries, keys_in, values_in = (
            lax.all_to_all(queries, "seq", split_axis=0, concat_axis=0, tiled=True),
            lax.all_to_all(keys_in, "seq", split_axis=0, concat_axis=0, tiled=True),
            lax.all_to_all(values_in, "seq", split_axis=0, concat_axis=0, tiled=True),
        )
        attended = lax.cond(
            active,
            lambda: attend(queries, keys_in, values_in),
            lambda: jnp.zeros(query_shape, jnp.bfloat16),
        )
        attended = lax.all_to_all(attended, "seq", split_axis=0, concat_axis=0, tiled=True)
        leaving = lax.cond(
            active,
            lambda: (
                carried.astype(jnp.float32)
                + jnp.dot(from_heads(attended), w_proj, preferred_element_type=jnp.float32)
            ).astype(jnp.bfloat16),
            lambda: carried,
        )
        skip_term = lax.cond(
            active & encoder,
            lambda: jnp.dot(leaving, w_merge, preferred_element_type=jnp.float32).astype(
                jnp.bfloat16
            ),
            lambda: jnp.zeros_like(leaving),
        )
        arrived = mirror_each(skip_term)
        source_no = tick_no - (section_count - 1 - my_section)
        landing = decoder & (source_no >= 0) & (source_no < windows)
        target = jnp.clip(source_no, 0, windows - 1)
        updated = lax.dynamic_update_index_in_dim(skip_store, arrived, target, 0)
        skip_store = jnp.where(landing, updated, skip_store)
        incoming = shifted(leaving, "section", 1)
        finished = lax.dynamic_update_index_in_dim(result, leaving.astype(jnp.float32), chosen, 0)
        result = jnp.where(active & (my_section == section_count - 1), finished, result)
        return (incoming, skip_store, result)

    loop_state = (
        jnp.zeros(latents.shape[1:], jnp.bfloat16),
        jnp.zeros_like(latents),
        jnp.zeros(latents.shape, jnp.float32),
    )
    loop_state = lax.fori_loop(0, windows + section_count - 1, tick, loop_state)
    result = loop_state[2]
    return lax.psum_scatter(result.astype(jnp.bfloat16), "section", scatter_dimension=2, tiled=True)


class Plan:
    def __init__(self, sections, seq_count, windows, tok_rows, features):
        self.sections = sections
        self.seq_count = seq_count
        self.windows = windows
        self.tok_rows = tok_rows
        self.features = features
        self.inner = seq_count // windows
        self.slots = sections * self.inner
        self.half = tok_rows // sections
        self.shard = windows * self.half
        self.tokens = self.slots * self.shard
        self.cols = features // self.slots
        self.half_cols = features // sections
        self.w_rows = features // seq_count
        self.group = self.inner * self.w_rows
        self.chips = [(mx, mi) for mx in range(sections) for mi in range(0, self.inner, 2)]

    @staticmethod
    def fits(sections, seq_count, windows, tok_rows, features):
        if sections != 2 or windows & (windows - 1) or seq_count % (2 * windows):
            return False
        inner = seq_count // windows
        if inner != 4 or features % (sections * inner * 2 * HEAD_DIM):
            return False
        return features == HEADS * HEAD_DIM and tok_rows % 32 == 0

    def mask(self, mx=0, mz=0, mi=0):
        return mx * self.seq_count + mz * self.inner + mi


def attention(queries, qkv, out, cols):
    lane_head = lax.broadcasted_iota(jnp.int32, (1, cols), 1) // HEAD_DIM
    keys_in = qkv[:, cols : 2 * cols]
    values_in = qkv[:, 2 * cols : 3 * cols]
    mixed = jnp.zeros(queries.shape, jnp.float32)
    for head in range(cols // HEAD_DIM):
        mine = lane_head == head
        picked = jnp.where(mine, queries, jnp.zeros_like(queries))
        scores = lax.dot_general(
            keys_in, picked, (((1,), (1,)), ((), ())), preferred_element_type=jnp.float32
        )
        weights = jnp.exp(scores - jnp.max(scores, axis=0, keepdims=True))
        totals = jnp.sum(weights, axis=0, keepdims=True)
        part = lax.dot_general(
            values_in,
            weights.astype(jnp.bfloat16),
            (((0,), (0,)), ((), ())),
            preferred_element_type=jnp.float32,
        )
        mixed = jnp.where(mine, (part / totals).T, mixed)
    out[...] = mixed.astype(jnp.bfloat16)


def project_rows(normed, w_qkv, cols):
    packed = jnp.dot(normed, w_qkv, preferred_element_type=jnp.float32)
    lane = lax.broadcasted_iota(jnp.int32, (1, packed.shape[1]), 1)
    packed = packed.astype(jnp.bfloat16)
    return jnp.where(lane < cols, packed * jnp.bfloat16(HEAD_DIM ** (-0.5)), packed)


def slot_of(plan, where, mx, mi):
    return (where[0] ^ mx) * plan.inner + (where[2] ^ mi)


def aligned(index, size):
    return pl.ds(pl.multiple_of(index * size, size), size)


def prepare_kernel(plan, where, latents, gain, qkv_weight, proj_weight, merge_weight, *rest):
    shares = rest[: plan.windows]
    keep, give, cross, held, factor, sems = rest[plan.windows :]
    copies = []

    def add(source, target):
        copies.append(pltpu.make_async_copy(source, target, sems.at[len(copies)]))

    for part in range(3):
        add(
            qkv_weight.at[0, :, part * plan.features : (part + 1) * plan.features],
            held.at[part],
        )
    add(gain, factor)
    width, rows = (plan.half_cols, plan.w_rows)
    for part, matrix in enumerate((proj_weight, merge_weight)):
        add(
            matrix.at[0, :, aligned(where[0] ^ 1, width)],
            cross.at[part * rows : (part + 1) * rows, :],
        )
    for mz in range(plan.windows):
        add(latents.at[where[1] ^ mz, aligned(where[0], plan.half), :], shares[mz])
    for copy in copies:
        copy.start()
    for copy in copies[:4]:
        copy.wait()
    first_row = (where[1] * plan.inner + where[2]) * rows
    row = first_row + lax.broadcasted_iota(jnp.int32, (rows, plan.features), 0)
    lane = lax.broadcasted_iota(jnp.int32, (rows, plan.features), 1)
    factors = jnp.where(row == lane, factor[...], jnp.zeros((1, plan.features), jnp.float32))
    factors = jnp.sum(factors, axis=1, keepdims=True)
    for core, target in ((1, give), (0, keep)):
        for chip_no, (mx, mi) in enumerate(plan.chips):
            lanes = aligned(slot_of(plan, where, mx, mi ^ core), plan.cols)
            for part in range(3):
                scaled = held[part, :, lanes].astype(jnp.float32) * factors
                target[chip_no, :, part * plan.cols : (part + 1) * plan.cols] = scaled.astype(
                    jnp.bfloat16
                )
    for copy in copies[4:]:
        copy.wait()


def pair_kernel(plan, keep, given, *outs):
    rows = plan.w_rows
    for chip_no, out in enumerate(outs):
        out[0:rows, :] = keep[chip_no]
        out[rows:, :] = given[chip_no]


def merge_kernel(plan, where, proj_weight, merge_weight, crossed, mats, last):
    rows, width = (plan.w_rows, plan.half_cols)
    for section in range(plan.sections):

        @pl.when(where[0] == section)
        def _():
            lanes = slice(section * width, (section + 1) * width)
            mine = proj_weight[0, :, lanes]
            others = crossed[0:rows, :]
            mats[:, 0:width] = mine if section == 0 else others
            last[...] = others if section == 0 else mine
            total = merge_weight[0, :, lanes].astype(jnp.float32)
            total = total + crossed[rows:, :].astype(jnp.float32)
            mats[:, width:] = total.astype(jnp.bfloat16)


def sort_kernel(plan, where, last, *refs):
    count = len(plan.chips)
    pieces, (rows_a, rows_b) = (refs[:count], refs[count:])
    rows, cols = (plan.w_rows, 3 * plan.cols)
    lone = plan.half_cols // plan.inner
    for section in range(plan.sections):

        @pl.when(where[0] == section)
        def _():
            outs = (rows_a, rows_b)
            for piece, (mx, mi) in zip(pieces, plan.chips):
                part = slice(mi * rows, (mi + 2) * rows)
                outs[section ^ mx][part, 0:cols] = piece[...]

    for mi in range(plan.inner):
        rows_b[mi * rows : (mi + 1) * rows, cols:] = last[:, mi * lone : (mi + 1) * lone]


def last_kernel(plan, *refs):
    rows, lone = (plan.w_rows, plan.half_cols // plan.inner)
    for mz, piece in enumerate(refs[:-1]):
        for mi in range(plan.inner):
            refs[-1][mz * rows : (mz + 1) * rows, mi * lone : (mi + 1) * lone] = piece[
                mi * rows : (mi + 1) * rows, 3 * plan.cols :
            ]


def stack_kernel(*refs):
    start = 0
    for piece in refs[:-1]:
        rows = piece.shape[0]
        refs[-1][start : start + rows, :] = piece[...]
        start += rows


def gather_weights(plan, where, pieces, target):
    rows = plan.w_rows
    for mz, piece in enumerate(pieces):
        for mi in range(plan.inner):
            shard = (where[1] ^ mz) * plan.inner + (where[2] ^ mi)
            target[aligned(shard, rows), :] = piece[
                mi * rows : (mi + 1) * rows, 0 : 3 * plan.cols
            ]


def plane_order(plan):
    return [(mx, mi ^ core) for core in range(2) for mx, mi in plan.chips]


def normalize(values):
    center = values - jnp.mean(values, axis=-1, keepdims=True)
    spread = jnp.mean(center * center, axis=-1, keepdims=True)
    return (center * lax.rsqrt(spread + EPSILON)).astype(jnp.bfloat16)


def row_blocks(plan, one_block):
    size = min(1024, plan.tokens)

    def step(block_no, carry):
        one_block(aligned(block_no, size))
        return carry

    lax.fori_loop(0, plan.tokens // size, step, 0)


def norm_kernel(plan, where, *refs):
    hid, normed = refs[plan.slots :]
    for piece, (mx, mi) in zip(refs, plane_order(plan)):
        hid[aligned(slot_of(plan, where, mx, mi), plan.shard), :] = piece[...]

    def one_block(rows):
        normed[rows, :] = normalize(hid[rows, :].astype(jnp.float32))

    row_blocks(plan, one_block)


def first_kernel(plan, where, normed, *rest):
    pieces = rest[: plan.windows]
    out, w_qkv, qkv = rest[plan.windows :]
    gather_weights(plan, where, pieces, w_qkv)

    def one_block(rows):
        qkv[rows, :] = project_rows(normed[rows, :], w_qkv[...], plan.cols)

    row_blocks(plan, one_block)
    attention(qkv[:, 0 : plan.cols], qkv, out, plan.cols)


def fold_kernel(plan, where, hid, *rest):
    mats_in, (merged, folded, mats) = (rest[: plan.slots], rest[plan.slots :])
    rows, width = (plan.w_rows, plan.half_cols)
    for piece, (mx, mi) in zip(mats_in, plane_order(plan)):
        for mz in range(plan.windows):
            shard = (where[1] ^ mz) * plan.inner + (where[2] ^ mi)
            part = piece[mz * rows : (mz + 1) * rows, :]
            for kind in range(2):
                lanes = aligned(where[0] ^ mx, width)
                mats[kind, aligned(shard, rows), lanes] = part[:, kind * width : (kind + 1) * width]

    def one_block(part):
        merged[part, :] = jnp.dot(hid[part, :], mats[1], preferred_element_type=jnp.float32)

    row_blocks(plan, one_block)
    size = min(512, plan.features)

    def one_part(block_no, carry):
        part = aligned(block_no, size)
        folded[part, :] = jnp.dot(
            mats[0, part, :], mats[1], preferred_element_type=jnp.float32
        ).astype(jnp.bfloat16)
        return carry

    lax.fori_loop(0, plan.features // size, one_part, 0)


def second_kernel(plan, where, merged, folded, *rest):
    slots, windows = (plan.slots, plan.windows)
    attended_in, rest = (rest[:slots], rest[slots:])
    pieces, rest = (rest[:windows], rest[windows:])
    out, kept, qkv, att, w_qkv, joined = rest
    for piece, (mx, mi) in zip(attended_in, plane_order(plan)):
        att[:, aligned(slot_of(plan, where, mx, mi), plan.cols)] = piece[...]
    gather_weights(plan, where, pieces, w_qkv)
    width = plan.half_cols

    def one_block(part):
        total = jnp.dot(att[part, :], folded[...], preferred_element_type=jnp.float32)
        total = (merged[part, :] + total).astype(jnp.bfloat16)
        joined[part, :] = total
        qkv[part, :] = project_rows(
            normalize(total.astype(jnp.float32)), w_qkv[...], plan.cols
        )

    row_blocks(plan, one_block)
    lanes = aligned(where[0], width)
    for side in range(plan.sections):
        part = aligned(side * plan.inner + where[2], plan.shard)
        kept[side * plan.shard : (side + 1) * plan.shard, :] = joined[part, lanes]
    attention(chip_queries(plan, where, qkv, 2), qkv, out, plan.cols)


def chip_queries(plan, where, qkv, mi):
    return jnp.concatenate(
        [
            qkv[aligned(side * plan.inner + (where[2] ^ mi ^ core), plan.shard), 0 : plan.cols]
            for core in range(2)
            for side in range(plan.sections)
        ],
        axis=0,
    )


def rest_kernel(plan, where, qkv, out):
    attention(chip_queries(plan, where, qkv, 0), qkv, out, plan.cols)


def third_kernel(plan, where, kept, *rest):
    chips, rest = (rest[: len(plan.chips)], rest[len(plan.chips) :])
    swapped, mats_in = (rest[0], rest[1 : 1 + plan.inner])
    outs, (att, mat) = (rest[1 + plan.inner : -2], rest[-2:])
    rows = plan.sections * plan.shard
    for chip_no, (mx, mi) in enumerate(plan.chips):
        for core in range(2):
            lanes = aligned(slot_of(plan, where, mx, mi ^ core), plan.cols)
            if core == 0:
                att[:, lanes] = chips[chip_no][0:rows, :]
            else:
                att[:, lanes] = swapped[chip_no * rows : (chip_no + 1) * rows, :]
    rows = plan.w_rows
    order = [mi ^ core for core in range(2) for mi in range(0, plan.inner, 2)]
    for piece, mi in zip(mats_in, order):
        for mz in range(plan.windows):
            shard = (where[1] ^ mz) * plan.inner + (where[2] ^ mi)
            mat[aligned(shard, rows), :] = piece[mz * rows : (mz + 1) * rows, :]
    result = jnp.dot(att[...], mat[...], preferred_element_type=jnp.float32)
    result = (kept[...].astype(jnp.float32) + result).astype(jnp.bfloat16)
    for side in range(plan.sections):
        for mz in range(plan.windows):
            start = side * plan.shard + mz * plan.half
            outs[mz][side * plan.half : (side + 1) * plan.half, :] = result[
                start : start + plan.half, :
            ]


def place_kernel(plan, where, *refs):
    for mz in range(plan.windows):
        refs[-1][where[1] ^ mz] = refs[mz][...]


def halves_kernel(plan, *refs):
    rows = plan.sections * plan.shard
    for chip_no, piece in enumerate(refs[:-1]):
        refs[-1][chip_no * rows : (chip_no + 1) * rows, :] = piece[rows:, :]


def plane_body(latents, norm_gain, qkv_weight, proj_weight, merge_weight):
    plan = Plan(
        lax.axis_size("section"), lax.axis_size("seq"), latents.shape[0], *latents.shape[1:]
    )
    windows, inner, shard, cols = (plan.windows, plan.inner, plan.shard, plan.cols)
    section = lax.axis_index("section")
    position = lax.axis_index("seq")
    window, place = (position // inner, position % inner)
    lane = lax.iota(jnp.int32, 3)
    where = jnp.where(lane == 0, section, jnp.where(lane == 1, window, place)).astype(jnp.int32)
    devices = plan.sections * plan.seq_count
    bf16 = jnp.bfloat16
    smem = pl.BlockSpec(memory_space=pltpu.SMEM)
    hbm = pl.BlockSpec(memory_space=pltpu.HBM)
    vmem = pl.BlockSpec(memory_space=pltpu.VMEM)
    tokens, features, width = (plan.tokens, plan.features, plan.half_cols)

    def swap(value, mask):
        pairs = [(source, source ^ mask) for source in range(devices)]
        return lax.ppermute(value, ("section", "seq"), pairs)

    def call(kernel, outs, ins, scratch=(), specs=None, flops=0, limit=40):
        typed = [shape if isinstance(shape[0], tuple) else (shape, bf16) for shape in outs]
        shapes = tuple(jax.ShapeDtypeStruct(*entry) for entry in typed)
        moved = sum(2 * value.size for value in ins)
        return pl.pallas_call(
            kernel,
            out_shape=shapes,
            in_specs=specs or [vmem] * len(ins),
            out_specs=tuple(vmem for _ in shapes),
            scratch_shapes=list(scratch),
            cost_estimate=pl.CostEstimate(
                flops=flops, bytes_accessed=moved, transcendentals=0
            ),
            compiler_params=pltpu.CompilerParams(vmem_limit_bytes=limit << 20),
        )(*ins)

    def stack(pieces):
        rows = sum(piece.shape[0] for piece in pieces)
        return call(stack_kernel, [(rows, pieces[0].shape[1])], pieces, limit=8)[0]

    def z_gather(value):
        pieces = [value]
        for mz in range(1, windows):
            low = mz & -mz
            pieces.append(swap(pieces[mz - low], plan.mask(mz=low)))
        return pieces

    def chip_gather(value):
        return [value] + [
            swap(value, plan.mask(mx=mx, mi=mi))
            for chip_no, (mx, mi) in enumerate(plan.chips)
            if chip_no
        ]

    def core_gather(pieces):
        return pieces + [swap(piece, plan.mask(mi=1)) for piece in pieces]

    latents, norm_gain, qkv_weight, proj_weight, merge_weight = (
        pltpu.with_memory_space_constraint(value, pltpu.HBM)
        for value in (latents, norm_gain, qkv_weight, proj_weight, merge_weight)
    )
    prepared = call(
        lambda *refs: prepare_kernel(plan, *refs),
        [(plan.half, features)] * windows
        + [(len(plan.chips), plan.w_rows, 3 * cols)] * 2
        + [(2 * plan.w_rows, width)],
        [where, latents, norm_gain, qkv_weight, proj_weight, merge_weight],
        [
            pltpu.VMEM((3, plan.w_rows, features), bf16),
            pltpu.VMEM((1, features), jnp.float32),
            pltpu.SemaphoreType.DMA((6 + windows,)),
        ],
        [smem] + [hbm] * 5,
        limit=8,
    )
    shares, (keep, give, cross) = (prepared[:windows], prepared[windows:])
    given = swap(give, plan.mask(mi=1))
    crossed = swap(cross, plan.mask(mx=1))
    shares = [shares[0]] + [swap(shares[mz], plan.mask(mz=mz)) for mz in range(1, windows)]
    outgoing = call(
        lambda *refs: pair_kernel(plan, *refs),
        [(2 * plan.w_rows, 3 * cols)] * len(plan.chips),
        [keep, given],
        limit=8,
    )
    incoming = [outgoing[0]] + [
        swap(outgoing[chip_no], plan.mask(mx=mx, mi=mi))
        for chip_no, (mx, mi) in enumerate(plan.chips)
        if chip_no
    ]
    hidden = chip_gather(stack(shares))
    hidden = core_gather(hidden)
    mats, last = call(
        lambda *refs: merge_kernel(plan, *refs),
        [(plan.w_rows, 2 * width), (plan.w_rows, width)],
        [where, proj_weight, merge_weight, crossed],
        (),
        [smem] + [vmem] * 3,
        limit=8,
    )
    rows_a, rows_b = call(
        lambda *refs: sort_kernel(plan, *refs),
        [
            (plan.group, 3 * cols),
            (plan.group, 3 * cols + width // inner),
        ],
        [where, last] + incoming,
        (),
        [smem] + [vmem] * (1 + len(incoming)),
        limit=8,
    )
    mats = z_gather(mats)
    pieces_a = z_gather(rows_a)
    pieces_b = z_gather(rows_b)
    mats = chip_gather(stack(mats))

    hid, normed = call(
        lambda *refs: norm_kernel(plan, *refs),
        [(tokens, features)] * 2,
        [where] + hidden,
        (),
        [smem] + [vmem] * len(hidden),
        limit=16,
    )
    (attended,) = call(
        lambda *refs: first_kernel(plan, *refs),
        [(tokens, cols)],
        [where, normed] + pieces_a,
        [pltpu.VMEM((features, 3 * cols), bf16), pltpu.VMEM((tokens, 3 * cols), bf16)],
        [smem] + [vmem] * (1 + windows),
        flops=10_000_000_000,
        limit=20,
    )
    attended = core_gather(chip_gather(attended))
    mats = core_gather(mats)
    merged, folded = call(
        lambda *refs: fold_kernel(plan, *refs),
        [((tokens, features), jnp.float32), (features, features)],
        [where, hid] + mats,
        [pltpu.VMEM((2, features, features), bf16)],
        [smem] + [vmem] * (1 + plan.slots),
        flops=4_000_000_000,
        limit=30,
    )
    (last,) = call(lambda *refs: last_kernel(plan, *refs), [(plan.group, width)], pieces_b, limit=8)
    last = [last] + [swap(last, plan.mask(mi=mi)) for mi in range(2, inner, 2)]
    last = core_gather(last)
    far_rows, kept, qkv = call(
        lambda *refs: second_kernel(plan, *refs),
        [
            (2 * plan.sections * shard, cols),
            (plan.sections * shard, width),
            (tokens, 3 * cols),
        ],
        [where, merged, folded] + attended + pieces_b,
        [
            pltpu.VMEM((tokens, features), bf16),
            pltpu.VMEM((features, 3 * cols), bf16),
            pltpu.VMEM((tokens, features), bf16),
        ],
        [smem] + [vmem] * (2 + plan.slots + windows),
        flops=12_000_000_000,
    )
    (near_rows,) = call(
        lambda *refs: rest_kernel(plan, *refs),
        [far_rows.shape],
        [where, qkv],
        (),
        [smem, vmem],
        flops=6_000_000_000,
        limit=20,
    )
    attended = [near_rows, far_rows]
    back = [attended[0]] + [
        swap(attended[mi // 2], plan.mask(mx=mx, mi=mi))
        for chip_no, (mx, mi) in enumerate(plan.chips)
        if chip_no
    ]
    (halves,) = call(
        lambda *refs: halves_kernel(plan, *refs),
        [(len(plan.chips) * plan.sections * shard, cols)],
        back,
        limit=8,
    )
    swapped = swap(halves, plan.mask(mi=1))
    outcome = call(
        lambda *refs: third_kernel(plan, *refs),
        [(plan.tok_rows, width)] * windows,
        [where, kept] + back + [swapped] + last,
        [
            pltpu.VMEM((plan.sections * shard, features), bf16),
            pltpu.VMEM((features, width), bf16),
        ],
        [smem] + [vmem] * (2 + len(back) + inner),
        flops=1_000_000_000,
        limit=16,
    )
    outcome = [outcome[0]] + [swap(outcome[mz], plan.mask(mz=mz)) for mz in range(1, windows)]
    return call(
        lambda *refs: place_kernel(plan, *refs),
        [(windows, plan.tok_rows, width)],
        [where] + outcome,
        (),
        [smem] + [vmem] * windows,
        limit=8,
    )[0]


def solution(mesh):
    placed = (
        P(None, "seq", None),
        P("section", None),
        P("section", "seq", None),
        P("section", "seq", None),
        P("section", "seq", None),
    )

    def plane_step(*arguments):
        return plane_body(*arguments)

    def step(latents, *weights):
        sizes = (
            mesh.shape["section"],
            mesh.shape["seq"],
            latents.shape[0],
            latents.shape[1] // mesh.shape["seq"],
            latents.shape[2],
        )
        fits = Plan.fits(*sizes)
        mapped = jax.shard_map(
            plane_step if fits else body,
            mesh=mesh,
            in_specs=placed,
            out_specs=P(None, "seq", "section"),
            check_vma=False,
        )
        return mapped(latents, *weights)

    return step
```
